32 devices in a mesh: dp: 16 (over z, x, core), mp: 2 (over y).
Axes of the slice: x: 2, y: 2, z: 4, core: 2. Of those that a mesh axis runs over, the one named last changes fastest.
Arguments:
- tokens: bfloat16 [80, 1024, 1024], P('dp'), may hold values from -6 to 6
- cotangent: bfloat16 [80, 1024, 1024], P('dp'), may hold values from -6 to 6
- lengths: int32 [80], P('dp'), may hold values from 64 to 1024, as said below
- first_norm_gain: float32 [1024], replicated, may hold values from 0.5 to 1.5
- first_norm_bias: float32 [1024], replicated, may hold values from -2 to 2
- query_key_value_weight: bfloat16 [3, 1024, 1024], P(None, None, 'mp'), may hold values from -0.1875 to 0.1875
- attention_output_weight: bfloat16 [1024, 1024], P('mp'), may hold values from -3 to 3
- attention_output_bias: float32 [1024], replicated, may hold values from -2 to 2
- second_norm_gain: float32 [1024], replicated, may hold values from 0.5 to 1.5
- second_norm_bias: float32 [1024], replicated, may hold values from -2 to 2
- feedforward_up_weight: bfloat16 [1024, 4096], P(None, 'mp'), may hold values from -0.1875 to 0.1875
- feedforward_up_bias: float32 [4096], P('mp'), may hold values from -3 to 3
- feedforward_down_weight: bfloat16 [4096, 1024], P('mp'), may hold values from -0.09375 to 0.09375
- feedforward_down_bias: float32 [1024], replicated, may hold values from -2 to 2
- adapter_down_factor: float32 [2, 1024, 4], replicated, may hold values from -0.1875 to 0.1875
- adapter_up_factor: float32 [2, 4, 1024], replicated, may hold values from -0.3 to 0.3
- down_first_moment: float32 [2, 1024, 4], replicated, may hold values from -0.006 to 0.006
- up_first_moment: float32 [2, 4, 1024], replicated, may hold values from -0.006 to 0.006
- down_second_moment: float32 [2, 1024, 4], replicated, may hold values from 1e-07 to 1e-05
- up_second_moment: float32 [2, 4, 1024], replicated, may hold values from 1e-07 to 1e-05
Outputs:
- block_out: bfloat16 [80, 1024, 1024], P('dp')
- input_grad: bfloat16 [80, 1024, 1024], P('dp')
- new_lora_down: float32 [2, 1024, 4], replicated
- new_lora_up: float32 [2, 4, 1024], replicated
- new_first_down: float32 [2, 1024, 4], replicated
- new_first_up: float32 [2, 4, 1024], replicated
- new_second_down: float32 [2, 1024, 4], replicated
- new_second_up: float32 [2, 4, 1024], replicated
The draws below stay inside these ranges and needn't reach their ends.
Inputs may be any that keep to these rules, and one draw needn't show every extreme that they name: `lengths`: the first of every 5 sequences (each index of dp's first) has 1024 live tokens.
All inputs are finite; a program needn't handle non-finite values.
Results may differ from the reference program's by a relative error of at most 0.015.
The reference program's roundings to bfloat16 on the way count: a program that leaves them out, or rounds other values in their place, can miss the bound.
Values may be sent and summed in bfloat16 or wider, within the bound.
A program may use at most 320 MiB of HBM per device.

```python
import math
import jax
import jax.numpy as jnp
from jax import lax

MODEL_DIMENSION = 1024
HEADS = 16
HEAD = 64
FF = 4096
ADAPTER_RANK = 4
LEN = 1024
MINLEN = 64
LEVELS = 5
ROWS = 5
SEQS = 80


def draw_lengths(key, part):
    level_key, extra_key = jax.random.split(key)
    octave = jax.random.randint(level_key, (SEQS,), 0, LEVELS)
    baseline = jnp.left_shift(jnp.full((SEQS,), MINLEN, jnp.int32), octave.astype(jnp.int32))
    offset_drawn = jax.random.randint(extra_key, (SEQS,), 0, 1 << 30) % baseline
    drawn = jnp.minimum(baseline + offset_drawn, LEN)
    leading = jnp.arange(SEQS) % ROWS == 0
    return jnp.where(leading, LEN, drawn).astype(jnp.int32)


def block_levels(key, extent, cuts, smallest, top_value):
    def one(axis_at, blocks):
        draws = jax.random.uniform(jax.random.fold_in(jax.random.fold_in(key, 6), axis_at), (blocks,), jnp.float32, smallest / len(cuts), top_value / len(cuts))
        return jnp.repeat(jnp.exp(draws), extent[axis_at] // blocks).reshape((-1,) + (1,) * (len(extent) - axis_at - 1))

    level = one(*cuts[0])
    for cut in cuts[1:]:
        level = level * one(*cut)
    return level


def gaussian(stream_key, shape, scale, reach, cuts=(), held_as=jnp.bfloat16):
    entries = jax.random.normal(stream_key, shape, jnp.float32) * scale
    if len(cuts) > 0:
        entries = block_levels(stream_key, shape, cuts, -0.22, 0.18) * entries
    return jnp.clip(entries, min=-reach, max=reach).astype(held_as)


def setup_inputs(seed: int = 0) -> dict:
    arg_keys = jax.random.split(jax.random.key(seed), 21)
    return {
        "tokens": gaussian(arg_keys[0], (SEQS, LEN, MODEL_DIMENSION), 1.0, 6.0, ((0, 16),)),
        "cotangent": gaussian(arg_keys[1], (SEQS, LEN, MODEL_DIMENSION), 1.0, 6.0, ((0, 16),)),
        "lengths": draw_lengths(jax.random.fold_in(arg_keys[20], 71), 0),
        "first_norm_gain": jnp.clip(1.0 + 0.1 * jax.random.normal(arg_keys[3], (MODEL_DIMENSION,), jnp.float32), 0.5, 1.5),
        "first_norm_bias": gaussian(arg_keys[4], (MODEL_DIMENSION,), 0.3, 2.0, (), jnp.float32),
        "query_key_value_weight": gaussian(arg_keys[5], (3, MODEL_DIMENSION, MODEL_DIMENSION), MODEL_DIMENSION ** -0.5, 0.1875, ((2, 2),)),
        "attention_output_weight": gaussian(arg_keys[6], (MODEL_DIMENSION, MODEL_DIMENSION), (max(MODEL_DIMENSION // 256, 1)) ** -0.5, 3.0, ((0, 2),)),
        "attention_output_bias": gaussian(arg_keys[7], (MODEL_DIMENSION,), 0.3, 2.0, (), jnp.float32),
        "second_norm_gain": jnp.clip(1.0 + 0.1 * jax.random.normal(arg_keys[8], (MODEL_DIMENSION,), jnp.float32), 0.5, 1.5),
        "second_norm_bias": gaussian(arg_keys[9], (MODEL_DIMENSION,), 0.3, 2.0, (), jnp.float32),
        "feedforward_up_weight": gaussian(arg_keys[10], (MODEL_DIMENSION, FF), MODEL_DIMENSION ** -0.5, 0.1875, ((1, 2),)),
        "feedforward_up_bias": gaussian(arg_keys[11], (FF,), 0.5, 3.0, ((0, 2),), jnp.float32),
        "feedforward_down_weight": gaussian(arg_keys[12], (FF, MODEL_DIMENSION), FF ** -0.5, 0.09375, ((0, 2),)),
        "feedforward_down_bias": gaussian(arg_keys[13], (MODEL_DIMENSION,), 0.3, 2.0, (), jnp.float32),
        "adapter_down_factor": gaussian(arg_keys[14], (2, MODEL_DIMENSION, ADAPTER_RANK), MODEL_DIMENSION ** -0.5, 0.1875, (), jnp.float32),
        "adapter_up_factor": gaussian(arg_keys[15], (2, ADAPTER_RANK, MODEL_DIMENSION), 0.05, 0.3, (), jnp.float32),
        "down_first_moment": gaussian(arg_keys[16], (2, MODEL_DIMENSION, ADAPTER_RANK), 0.001, 0.006, (), jnp.float32),
        "up_first_moment": gaussian(arg_keys[17], (2, ADAPTER_RANK, MODEL_DIMENSION), 0.001, 0.006, (), jnp.float32),
        "down_second_moment": jnp.clip(jnp.exp(jax.random.uniform(arg_keys[18], (2, MODEL_DIMENSION, ADAPTER_RANK), jnp.float32, math.log(1.0000000116860974e-07), math.log(9.999999747378752e-06))), 1.0000000116860974e-07, 9.999999747378752e-06),
        "up_second_moment": jnp.clip(jnp.exp(jax.random.uniform(arg_keys[19], (2, ADAPTER_RANK, MODEL_DIMENSION), jnp.float32, math.log(1.0000000116860974e-07), math.log(9.999999747378752e-06))), 1.0000000116860974e-07, 9.999999747378752e-06),
    }


@jax.custom_vjp
def low(v):
    return lax.optimization_barrier(v.astype(jnp.bfloat16)).astype(jnp.float32)

@jax.custom_vjp
def low_back(v):
    return v

def low_keep(v):
    return (low(v), None)

def low_pass(kept, grad):
    return (grad,)

def back_keep(v):
    return (v, None)

def back_low(kept, grad):
    return (low(grad),)
low.defvjp(low_keep, low_pass)
low_back.defvjp(back_keep, back_low)

def contract_product(pattern, first_op, second_op):
    return jnp.einsum(pattern, first_op, second_op, precision=lax.Precision.HIGHEST)

def layer_norm(values, norm_gain, norm_shift):
    centre = values - lax.optimization_barrier(jnp.mean(values, axis=-1, keepdims=True))
    spread = lax.optimization_barrier(jnp.mean(centre * centre, axis=-1, keepdims=True))
    return centre * lax.rsqrt(spread + 1e-05) * norm_gain + norm_shift

def gelu_tanh(values):
    return 0.5 * values * (1.0 + jnp.tanh(0.7978845608028654 * (values + 0.044715 * values * values * values)))

def paired_rounded(values):
    return low(low_back(values))

def attend_head(query_rows, key_rows, value_token_rows, seq_lengths):
    scores = low_back(contract_product('gqd,gkd->gqk', query_rows, key_rows) * HEAD ** (-0.5))
    position = jnp.arange(LEN)
    allowed = (position[None, None, :] <= position[None, :, None]) & (position[None, None, :] < seq_lengths[:, None, None])
    scores = jnp.where(allowed, scores, -1e+30)
    row_max = lax.optimization_barrier(jnp.max(scores, axis=-1, keepdims=True))
    weights = jnp.exp(scores - row_max)
    probabilities = weights / lax.optimization_barrier(jnp.sum(weights, axis=-1, keepdims=True))
    return contract_product('gqk,gkd->gqd', low(probabilities), value_token_rows)

def forward(tokens_f, seq_lengths, adapters_down, adapters_up, frozen):
    gain_one, shift_one, query_key_value, out_weight, out_bias, gain_two, shift_two, up_w, up_b, down_w, down_b = frozen
    group = tokens_f.shape[0]
    normalized_rows = low(layer_norm(tokens_f, gain_one, shift_one))
    down_reduced = low(adapters_down)
    up_reduced = low(adapters_up)
    adapter_query_delta = low(contract_product('hiz,zv->hiv', normalized_rows, down_reduced[0]))
    adapter_value_delta = low(contract_product('hiz,zv->hiv', normalized_rows, down_reduced[1]))
    query_rows = paired_rounded(contract_product('hxf,fn->hxn', normalized_rows, query_key_value[0]) + 8.0 * contract_product('yum,mh->yuh', adapter_query_delta, up_reduced[0]))
    key_rows = paired_rounded(contract_product('hxf,fn->hxn', normalized_rows, query_key_value[1]))
    value_token_rows = paired_rounded(contract_product('hxf,fn->hxn', normalized_rows, query_key_value[2]) + 8.0 * contract_product('yum,mh->yuh', adapter_value_delta, up_reduced[1]))

    def by_heads(matrix):
        return matrix.reshape(group, LEN, HEADS, HEAD).transpose(2, 0, 1, 3)

    def one_head(pieces):
        return attend_head(pieces[0], pieces[1], pieces[2], seq_lengths)
    head_out = lax.map(jax.checkpoint(one_head), (by_heads(query_rows), by_heads(key_rows), by_heads(value_token_rows)))
    attended = paired_rounded(head_out.transpose(1, 2, 0, 3).reshape(group, LEN, MODEL_DIMENSION))
    attn_branch = low_back(contract_product('gte,ed->gtd', attended, out_weight) + out_bias)
    residual = tokens_f + attn_branch
    normed_two = low(layer_norm(residual, gain_two, shift_two))
    hidden_pre = low_back(contract_product('gtd,df->gtf', normed_two, up_w) + up_b)
    hidden = low(gelu_tanh(hidden_pre))
    branch = low_back(contract_product('gtf,fd->gtd', hidden, down_w) + down_b)
    return residual + branch

def adam_decay_update(adapter, gradient, first_mom, second_mom):
    first_new = 0.9 * first_mom + 0.1 * gradient
    second_new = 0.999 * second_mom + 0.001 * gradient * gradient
    update = first_new / (1.0 - 0.9 ** 10) / (jnp.sqrt(second_new / (1.0 - 0.999 ** 10)) + 1e-08)
    return (adapter - 0.25 * (update + 0.01 * adapter), first_new, second_new)

def reference(tokens, cotangent, lengths, first_norm_gain, first_norm_bias, query_key_value_weight, attention_output_weight, attention_output_bias, second_norm_gain, second_norm_bias, feedforward_up_weight, feedforward_up_bias, feedforward_down_weight, feedforward_down_bias, adapter_down_factor, adapter_up_factor, down_first_moment, up_first_moment, down_second_moment, up_second_moment):
    frozen = tuple((operand.astype(jnp.float32) for operand in (first_norm_gain, first_norm_bias, query_key_value_weight, attention_output_weight, attention_output_bias, second_norm_gain, second_norm_bias, feedforward_up_weight, feedforward_up_bias, feedforward_down_weight, feedforward_down_bias)))
    blocks = SEQS // ROWS
    tokens_f = tokens.astype(jnp.float32).reshape(blocks, ROWS, LEN, MODEL_DIMENSION)
    cot_f = cotangent.astype(jnp.float32).reshape(blocks, ROWS, LEN, MODEL_DIMENSION)
    block_lengths = lengths.reshape(blocks, ROWS)

    def block_step(totals, pieces):
        block_token_rows, block_cot, block_len = pieces

        def single_sequence(tok, adown, aup):
            return forward(tok, block_len, adown, aup, frozen)
        layer_result, backward_function = jax.vjp(single_sequence, block_token_rows, adapter_down_factor, adapter_up_factor)
        live_mask = (jnp.arange(LEN)[None, :] < block_len[:, None]).astype(jnp.float32)
        grad_tok, grad_down, grad_up = backward_function(block_cot * live_mask[:, :, None])
        return ((totals[0] + grad_down, totals[1] + grad_up), (layer_result.astype(jnp.bfloat16), grad_tok.astype(jnp.bfloat16)))
    start_sums = (jnp.zeros((2, MODEL_DIMENSION, ADAPTER_RANK), jnp.float32), jnp.zeros((2, ADAPTER_RANK, MODEL_DIMENSION), jnp.float32))
    (down_gradient_sum, up_gradient_sum), (outputs, grads) = lax.scan(block_step, start_sums, (tokens_f, cot_f, block_lengths))
    active_token_total = jnp.sum(lengths.astype(jnp.float32))
    down_factor_next, down_first_moment_next, down_second_moment_next = adam_decay_update(adapter_down_factor, down_gradient_sum / active_token_total, down_first_moment, down_second_moment)
    up_factor_next, up_first_moment_next, up_second_moment_next = adam_decay_update(adapter_up_factor, up_gradient_sum / active_token_total, up_first_moment, up_second_moment)
    return (outputs.reshape(SEQS, LEN, MODEL_DIMENSION), grads.reshape(SEQS, LEN, MODEL_DIMENSION), down_factor_next, up_factor_next, down_first_moment_next, up_first_moment_next, down_second_moment_next, up_second_moment_next)
```

```python
import jax
import jax.numpy as jnp
from jax import lax
from jax.experimental import pallas as pl
from jax.experimental.pallas import tpu as pltpu
from jax.sharding import PartitionSpec as P

HEAD = 64


def layer_norm(values, norm_gain, norm_shift):
    centre = values - jnp.mean(values, axis=-1, keepdims=True)
    spread = jnp.mean(centre * centre, axis=-1, keepdims=True)
    return centre * lax.rsqrt(spread + 1e-05) * norm_gain + norm_shift


def gelu_tanh(values):
    return (
        0.5
        * values
        * (1.0 + jnp.tanh(0.7978845608028654 * (values + 0.044715 * values * values * values)))
    )


def head_major(matrix, seq_rows, head_count):
    return (
        matrix.reshape(seq_rows, -1, head_count, HEAD)
        .transpose(0, 2, 1, 3)
        .reshape(seq_rows * head_count, -1, HEAD)
    )


def token_major(stacked, seq_rows, head_count):
    return (
        stacked.reshape(seq_rows, head_count, -1, HEAD)
        .transpose(0, 2, 1, 3)
        .reshape(-1, head_count * HEAD)
    )


def masked_scores(query_rows, key_rows, seq_len):
    scores = jnp.einsum(
        "qd,kd->qk", query_rows, key_rows, preferred_element_type=jnp.float32
    ) * HEAD ** (-0.5)
    position = jnp.arange(scores.shape[0])
    allowed = (position[None, :] <= position[:, None]) & (position[None, :] < seq_len)
    return jnp.where(allowed, scores, -1e30)


def attend_forward(pieces):
    query_rows, key_rows, value_token_rows, seq_len = pieces
    scores = masked_scores(query_rows, key_rows, seq_len)
    row_max = jnp.max(scores, axis=-1, keepdims=True)
    weights = jnp.exp(scores - row_max)
    row_sum = jnp.sum(weights, axis=-1, keepdims=True)
    probabilities = (weights / row_sum).astype(jnp.bfloat16)
    head_out = jnp.dot(probabilities, value_token_rows, preferred_element_type=jnp.float32)
    return (head_out, row_max[:, 0] + jnp.log(row_sum[:, 0]))


def attend_backward(pieces):
    query_rows, key_rows, value_token_rows, seq_len, grad_head, log_sums = pieces
    scores = masked_scores(query_rows, key_rows, seq_len)
    probabilities = jnp.exp(scores - log_sums[:, None])
    value_gradient_rows = jnp.einsum(
        "qk,qd->kd",
        probabilities.astype(jnp.bfloat16),
        grad_head,
        preferred_element_type=jnp.float32,
    )
    grad_probs = jnp.einsum(
        "qd,kd->qk", grad_head, value_token_rows, preferred_element_type=jnp.float32
    )
    grad_scores = probabilities * (
        grad_probs - jnp.sum(grad_probs * probabilities, axis=-1, keepdims=True)
    )
    grad_scores = grad_scores.astype(jnp.bfloat16)
    query_gradient_rows = jnp.dot(
        grad_scores, key_rows, preferred_element_type=jnp.float32
    ) * HEAD ** (-0.5)
    grad_keys = jnp.einsum(
        "qk,qd->kd", grad_scores, query_rows, preferred_element_type=jnp.float32
    ) * HEAD ** (-0.5)
    return (query_gradient_rows, grad_keys, value_gradient_rows)


def adam_decay_update(adapter, gradient, first_mom, second_mom):
    first_new = 0.9 * first_mom + 0.1 * gradient
    second_new = 0.999 * second_mom + 0.001 * gradient * gradient
    update = first_new / (1.0 - 0.9**10) / (jnp.sqrt(second_new / (1.0 - 0.999**10)) + 1e-08)
    return (adapter - 0.25 * (update + 0.01 * adapter), first_new, second_new)


def per_device(
    tokens,
    cotangent,
    lengths,
    first_norm_gain,
    first_norm_bias,
    query_key_value_weight,
    attention_output_weight,
    attention_output_bias,
    second_norm_gain,
    second_norm_bias,
    feedforward_up_weight,
    feedforward_up_bias,
    feedforward_down_weight,
    feedforward_down_bias,
    adapter_down_factor,
    adapter_up_factor,
    down_first_moment,
    up_first_moment,
    down_second_moment,
    up_second_moment,
):
    seq_rows, seq_len_all, model_width = tokens.shape
    tok_count = seq_rows * seq_len_all
    groups = lax.axis_size("mp")
    worker_shard = lax.axis_index("mp")
    shard_width = query_key_value_weight.shape[2]
    head_count = shard_width // HEAD
    adapter_rank_size = adapter_down_factor.shape[2]
    tokens_f32 = tokens.reshape(tok_count, model_width).astype(jnp.float32)
    normalized_rows = layer_norm(tokens_f32, first_norm_gain, first_norm_bias).astype(jnp.bfloat16)
    down_reduced = adapter_down_factor.astype(jnp.bfloat16)
    up_reduced = adapter_up_factor.astype(jnp.bfloat16)
    up_columns = lax.dynamic_slice_in_dim(up_reduced, worker_shard * shard_width, shard_width, 2)
    down_pair = jnp.concatenate((down_reduced[0], down_reduced[1]), axis=1)
    adapter_pair = jnp.dot(normalized_rows, down_pair, preferred_element_type=jnp.float32).astype(
        jnp.bfloat16
    )
    adapter_query_delta = adapter_pair[:, :adapter_rank_size]
    adapter_value_delta = adapter_pair[:, adapter_rank_size:]
    query_rows = (
        jnp.dot(normalized_rows, query_key_value_weight[0], preferred_element_type=jnp.float32)
        + 8.0 * jnp.dot(adapter_query_delta, up_columns[0], preferred_element_type=jnp.float32)
    ).astype(jnp.bfloat16)
    key_rows = jnp.dot(
        normalized_rows, query_key_value_weight[1], preferred_element_type=jnp.float32
    ).astype(jnp.bfloat16)
    value_token_rows = (
        jnp.dot(normalized_rows, query_key_value_weight[2], preferred_element_type=jnp.float32)
        + 8.0 * jnp.dot(adapter_value_delta, up_columns[1], preferred_element_type=jnp.float32)
    ).astype(jnp.bfloat16)
    limits = jnp.repeat(lengths, head_count)
    query_heads = head_major(query_rows, seq_rows, head_count)
    key_heads = head_major(key_rows, seq_rows, head_count)
    value_heads = head_major(value_token_rows, seq_rows, head_count)
    head_out, log_sums = lax.map(attend_forward, (query_heads, key_heads, value_heads, limits))
    attended = token_major(head_out, seq_rows, head_count).astype(jnp.bfloat16)
    attn_share = (
        lax.psum_scatter(
            jnp.dot(attended, attention_output_weight, preferred_element_type=jnp.float32),
            "mp",
            scatter_dimension=0,
            tiled=True,
        )
        + attention_output_bias
    )

    def norm_two(values):
        return layer_norm(values, second_norm_gain, second_norm_bias)

    def norm_one(values):
        return layer_norm(values, first_norm_gain, first_norm_bias)

    attn_full = lax.all_gather(attn_share, "mp", axis=0, tiled=True)
    residual = tokens_f32 + attn_full
    normed_two = norm_two(residual).astype(jnp.bfloat16)
    hidden_pre = (
        jnp.dot(normed_two, feedforward_up_weight, preferred_element_type=jnp.float32)
        + feedforward_up_bias
    )
    hidden = gelu_tanh(hidden_pre).astype(jnp.bfloat16)
    mlp_share = (
        lax.psum_scatter(
            jnp.dot(hidden, feedforward_down_weight, preferred_element_type=jnp.float32).astype(
                jnp.bfloat16
            ),
            "mp",
            scatter_dimension=0,
            tiled=True,
        ).astype(jnp.float32)
        + feedforward_down_bias
    )
    mlp_full = lax.all_gather(mlp_share.astype(jnp.bfloat16), "mp", axis=0, tiled=True).astype(
        mlp_share.dtype
    )
    block_out = (residual + mlp_full).astype(jnp.bfloat16)
    live_mask = (jnp.arange(seq_len_all)[None, :] < lengths[:, None]).reshape(tok_count, 1)
    grad_out = jnp.where(
        live_mask, cotangent.reshape(tok_count, model_width), jnp.zeros((), jnp.bfloat16)
    )
    grad_hidden = jnp.einsum(
        "td,fd->tf", grad_out, feedforward_down_weight, preferred_element_type=jnp.float32
    )
    _, gelu_back = jax.vjp(gelu_tanh, hidden_pre)
    grad_pre = gelu_back(grad_hidden)[0].astype(jnp.bfloat16)
    grad_norm2_share = lax.psum_scatter(
        jnp.einsum(
            "tf,df->td", grad_pre, feedforward_up_weight, preferred_element_type=jnp.float32
        ),
        "mp",
        scatter_dimension=0,
        tiled=True,
    )
    grad_norm2 = lax.all_gather(grad_norm2_share, "mp", axis=0, tiled=True)
    _, norm2_back = jax.vjp(norm_two, residual)
    grad_resid = grad_out.astype(jnp.float32) + norm2_back(grad_norm2)[0]
    grad_resid_low = grad_resid.astype(jnp.bfloat16)
    grad_attended = jnp.einsum(
        "td,ed->te", grad_resid_low, attention_output_weight, preferred_element_type=jnp.float32
    ).astype(jnp.bfloat16)
    grad_head = head_major(grad_attended, seq_rows, head_count)
    head_dq, head_dk, head_dv = lax.map(
        attend_backward, (query_heads, key_heads, value_heads, limits, grad_head, log_sums)
    )
    query_gradient_rows = token_major(head_dq, seq_rows, head_count).astype(jnp.bfloat16)
    grad_keys = token_major(head_dk, seq_rows, head_count).astype(jnp.bfloat16)
    value_gradient_rows = token_major(head_dv, seq_rows, head_count).astype(jnp.bfloat16)
    adapter_query_gradient = 8.0 * jnp.einsum(
        "te,re->tr", query_gradient_rows, up_columns[0], preferred_element_type=jnp.float32
    )
    adapter_value_gradient = 8.0 * jnp.einsum(
        "te,re->tr", value_gradient_rows, up_columns[1], preferred_element_type=jnp.float32
    )
    adapter_gradient = jnp.concatenate((adapter_query_gradient, adapter_value_gradient), axis=1)
    down_pair_float32 = down_pair.astype(jnp.float32)
    partial_sum = jnp.einsum(
        "te,de->td",
        query_gradient_rows,
        query_key_value_weight[0],
        preferred_element_type=jnp.float32,
    )
    partial_sum = partial_sum + jnp.einsum(
        "te,de->td", grad_keys, query_key_value_weight[1], preferred_element_type=jnp.float32
    )
    partial_sum = partial_sum + jnp.einsum(
        "te,de->td",
        value_gradient_rows,
        query_key_value_weight[2],
        preferred_element_type=jnp.float32,
    )
    grad_norm1_share = lax.psum_scatter(
        partial_sum
        + jnp.einsum(
            "gy,wy->gw", adapter_gradient, down_pair_float32, precision=lax.Precision.HIGHEST
        ),
        "mp",
        scatter_dimension=0,
        tiled=True,
    )
    grad_down_both = jnp.einsum(
        "fi,fg->ig",
        normalized_rows.astype(jnp.float32),
        adapter_gradient,
        precision=lax.Precision.HIGHEST,
    )
    grad_down = jnp.stack(
        (grad_down_both[:, :adapter_rank_size], grad_down_both[:, adapter_rank_size:])
    )
    grad_up_query = 8.0 * jnp.einsum(
        "zm,zj->mj", adapter_query_delta, query_gradient_rows, preferred_element_type=jnp.float32
    )
    grad_up_value = 8.0 * jnp.einsum(
        "zm,zj->mj", adapter_value_delta, value_gradient_rows, preferred_element_type=jnp.float32
    )
    up_column_gradient = jnp.stack((grad_up_query, grad_up_value))
    grad_up = lax.dynamic_update_slice_in_dim(
        jnp.zeros(adapter_up_factor.shape, jnp.float32),
        up_column_gradient,
        worker_shard * shard_width,
        2,
    )
    live_local = jnp.sum(lengths).astype(jnp.float32)
    down_reduced_sum, up_reduced_sum, live_sum = lax.psum(
        (grad_down, grad_up, live_local), ("dp", "mp")
    )
    active_token_total = live_sum / groups
    grad_norm1 = lax.all_gather(grad_norm1_share, "mp", axis=0, tiled=True)
    _, norm1_back = jax.vjp(norm_one, tokens_f32)
    input_grad = (grad_resid + norm1_back(grad_norm1)[0]).astype(jnp.bfloat16)
    down_factor_next, down_first_moment_next, down_second_moment_next = adam_decay_update(
        adapter_down_factor,
        down_reduced_sum / active_token_total,
        down_first_moment,
        down_second_moment,
    )
    up_factor_next, up_first_moment_next, up_second_moment_next = adam_decay_update(
        adapter_up_factor, up_reduced_sum / active_token_total, up_first_moment, up_second_moment
    )
    return (
        block_out.reshape(seq_rows, seq_len_all, model_width),
        input_grad.reshape(seq_rows, seq_len_all, model_width),
        down_factor_next,
        up_factor_next,
        down_first_moment_next,
        up_first_moment_next,
        down_second_moment_next,
        up_second_moment_next,
    )


TILE = 256
NT = (((1,), (1,)), ((), ()))


def head_lanes(half):
    lane = lax.broadcasted_iota(jnp.int32, (1, 2 * HEAD), 1)
    return (lane >= half * HEAD) & (lane < (half + 1) * HEAD)


def one_head(block, half):
    return jnp.where(head_lanes(half), block, jnp.zeros((), block.dtype))


def edge_allowed(key_start, query_start, seq_len):
    key_at = key_start + lax.broadcasted_iota(jnp.int32, (TILE, TILE), 0)
    query_at = query_start + lax.broadcasted_iota(jnp.int32, (TILE, TILE), 1)
    return (key_at <= query_at) & (key_at < seq_len)


def attention_forward_kernel(lens_ref, q_ref, k_ref, v_ref, out_ref, lse_ref, vt_ref):
    seq_len = lens_ref[pl.program_id(0)]
    live_tiles = (seq_len + TILE - 1) // TILE
    vt_ref[...] = v_ref[0].T
    tiles = q_ref.shape[1] // TILE

    def row_tile(tile, extent):
        rows = pl.ds(tile * TILE, TILE)
        inner = (extent - 1) * TILE
        query = q_ref[0, rows, :] * HEAD ** (-0.5)
        allowed = edge_allowed(inner, tile * TILE, seq_len)
        outs = []
        for half in range(2):
            mine = one_head(query, half)
            edge = lax.dot_general(
                k_ref[0, pl.ds(inner, TILE), :], mine, NT, preferred_element_type=jnp.float32
            )
            edge = jnp.where(allowed, edge, -1e30)
            top = jnp.max(edge, axis=0, keepdims=True)
            if inner:
                past = lax.dot_general(
                    k_ref[0, pl.ds(0, inner), :], mine, NT, preferred_element_type=jnp.float32
                )
                top = jnp.maximum(top, jnp.max(past, axis=0, keepdims=True))
            head_rows = pl.ds(half * HEAD, HEAD)
            edge = jnp.exp(edge - top)
            total = jnp.sum(edge, axis=0, keepdims=True)
            out = jnp.dot(
                vt_ref[head_rows, pl.ds(inner, TILE)],
                edge.astype(jnp.bfloat16),
                preferred_element_type=jnp.float32,
            )
            if inner:
                past = jnp.exp(past - top)
                total = total + jnp.sum(past, axis=0, keepdims=True)
                out = out + jnp.dot(
                    vt_ref[head_rows, pl.ds(0, inner)],
                    past.astype(jnp.bfloat16),
                    preferred_element_type=jnp.float32,
                )
            outs.append(out / total)
            lse_ref[0, 0, pl.ds(half, 1), rows] = top + jnp.log(total)
        out_ref[0, rows, :] = jnp.concatenate(outs, axis=0).T.astype(out_ref.dtype)

    for tile in range(tiles):
        for extent in range(1, tile + 2):
            pl.when(jnp.minimum(live_tiles, tile + 1) == extent)(
                lambda tile=tile, extent=extent: row_tile(tile, extent)
            )


def attention_forward(lens, query, key, value):
    seqs, length, width = query.shape
    pairs = width // (2 * HEAD)
    spec = pl.BlockSpec((1, length, 2 * HEAD), lambda s, h, lens: (s, 0, h))
    return pl.pallas_call(
        attention_forward_kernel,
        grid_spec=pltpu.PrefetchScalarGridSpec(
            num_scalar_prefetch=1,
            grid=(seqs, pairs),
            in_specs=[spec] * 3,
            out_specs=[spec, pl.BlockSpec((1, 1, 2, length), lambda s, h, lens: (s, h, 0, 0))],
            scratch_shapes=[pltpu.VMEM((2 * HEAD, length), jnp.bfloat16)],
        ),
        out_shape=[
            jax.ShapeDtypeStruct(query.shape, jnp.bfloat16),
            jax.ShapeDtypeStruct((seqs, pairs, 2, length), jnp.float32),
        ],
        cost_estimate=pl.CostEstimate(
            flops=seqs * width * length * length * 3,
            bytes_accessed=seqs * width * length * 8,
            transcendentals=seqs * pairs * length * length,
        ),
        name="attention_forward",
    )(lens, query, key, value)


def attention_backward_kernel(
    lens_ref, q_ref, k_ref, v_ref, g_ref, lse_ref, dq_ref, dk_ref, dv_ref, kt_ref, dk_acc, dv_acc
):
    seq_len = lens_ref[pl.program_id(0)]
    kt_ref[...] = k_ref[0].T
    dk_acc[...] = jnp.zeros_like(dk_acc)
    dv_acc[...] = jnp.zeros_like(dv_acc)
    tiles = q_ref.shape[1] // TILE

    def row_tile(tile):
        rows = pl.ds(tile * TILE, TILE)
        inner = tile * TILE
        query = q_ref[0, rows, :] * HEAD ** (-0.5)
        grad = g_ref[0, rows, :]
        allowed = edge_allowed(inner, inner, seq_len)
        spans = [(inner, TILE)] + ([(0, inner)] if inner else [])
        outs = []
        for half in range(2):
            mine = one_head(query, half)
            mine_grad = one_head(grad, half)
            lse = lse_ref[0, 0, pl.ds(half, 1), rows]
            probs, grad_probs, row_dot = [], [], 0.0
            for at, (start, size) in enumerate(spans):
                keys = pl.ds(start, size)
                scores = lax.dot_general(
                    k_ref[0, keys, :], mine, NT, preferred_element_type=jnp.float32
                )
                if at == 0:
                    scores = jnp.where(allowed, scores, -1e30)
                prob = jnp.exp(scores - lse)
                dv_acc[keys, :] += jnp.dot(
                    prob.astype(jnp.bfloat16), mine_grad, preferred_element_type=jnp.float32
                )
                grad_prob = lax.dot_general(
                    v_ref[0, keys, :], mine_grad, NT, preferred_element_type=jnp.float32
                )
                row_dot = row_dot + jnp.sum(prob * grad_prob, axis=0, keepdims=True)
                probs.append(prob)
                grad_probs.append(grad_prob)
            out = 0.0
            for (start, size), prob, grad_prob in zip(spans, probs, grad_probs):
                keys = pl.ds(start, size)
                grad_scores = (prob * (grad_prob - row_dot)).astype(jnp.bfloat16)
                dk_acc[keys, :] += jnp.dot(grad_scores, mine, preferred_element_type=jnp.float32)
                out = out + jnp.dot(
                    kt_ref[pl.ds(half * HEAD, HEAD), keys],
                    grad_scores,
                    preferred_element_type=jnp.float32,
                )
            outs.append(out)
        dq = jnp.concatenate(outs, axis=0).T * HEAD ** (-0.5)
        dq_ref[0, rows, :] = dq.astype(dq_ref.dtype)

    for tile in range(tiles):
        pl.when(tile * TILE < seq_len)(lambda tile=tile: row_tile(tile))

        @pl.when(tile * TILE >= seq_len)
        def _(tile=tile):
            dq_ref[0, pl.ds(tile * TILE, TILE), :] = jnp.zeros((TILE, 2 * HEAD), dq_ref.dtype)

    dk_ref[0] = dk_acc[...].astype(dk_ref.dtype)
    dv_ref[0] = dv_acc[...].astype(dv_ref.dtype)


def attention_backward(lens, query, key, value, grad, lse):
    seqs, length, width = query.shape
    pairs = width // (2 * HEAD)
    spec = pl.BlockSpec((1, length, 2 * HEAD), lambda s, h, lens: (s, 0, h))
    return pl.pallas_call(
        attention_backward_kernel,
        grid_spec=pltpu.PrefetchScalarGridSpec(
            num_scalar_prefetch=1,
            grid=(seqs, pairs),
            in_specs=[spec] * 4
            + [pl.BlockSpec((1, 1, 2, length), lambda s, h, lens: (s, h, 0, 0))],
            out_specs=[spec] * 3,
            scratch_shapes=[
                pltpu.VMEM((2 * HEAD, length), jnp.bfloat16),
                pltpu.VMEM((length, 2 * HEAD), jnp.float32),
                pltpu.VMEM((length, 2 * HEAD), jnp.float32),
            ],
        ),
        out_shape=[jax.ShapeDtypeStruct(query.shape, jnp.bfloat16)] * 3,
        cost_estimate=pl.CostEstimate(
            flops=seqs * width * length * length * 7,
            bytes_accessed=seqs * width * length * 14,
            transcendentals=seqs * pairs * length * length,
        ),
        name="attention_backward",
    )(lens, query, key, value, grad, lse)


def swap(value):
    return lax.ppermute(value, "mp", [(0, 1), (1, 0)])


def partner_shard(shard, axis):
    size = shard.shape[axis] // 2
    core = lax.rem(lax.axis_index("dp"), 2)
    count = lax.axis_size("dp")
    half = lax.dynamic_slice_in_dim(shard, core * size, size, axis)
    mine = swap(half)
    other = lax.ppermute(mine, "dp", [(i, i ^ 1) for i in range(count)])
    low = jnp.where(core == 0, mine, other)
    high = jnp.where(core == 0, other, mine)
    return jnp.concatenate((shard, low, high), axis=axis)


def per_device_pair(
    tokens,
    cotangent,
    lengths,
    first_norm_gain,
    first_norm_bias,
    query_key_value_weight,
    attention_output_weight,
    attention_output_bias,
    second_norm_gain,
    second_norm_bias,
    feedforward_up_weight,
    feedforward_up_bias,
    feedforward_down_weight,
    feedforward_down_bias,
    adapter_down_factor,
    adapter_up_factor,
    down_first_moment,
    up_first_moment,
    down_second_moment,
    up_second_moment,
):
    f32, bf16 = jnp.float32, jnp.bfloat16
    length, width = tokens.shape[1:]
    rank = adapter_down_factor.shape[2]
    me = lax.axis_index("mp")
    half_width = query_key_value_weight.shape[2]
    whole, half = 2, length // 2
    split = 2 * whole

    def own(array, half_at):
        entire = lax.dynamic_slice_in_dim(array, whole * me, whole, 0)
        part = lax.dynamic_slice_in_dim(array[split], half_at * half, half, 0)
        return jnp.concatenate((entire.reshape(whole * length, width), part), axis=0)

    qkv_full = partner_shard(query_key_value_weight, 2)
    out_full = partner_shard(attention_output_weight, 0)
    up_full = partner_shard(feedforward_up_weight, 1)
    up_bias = jnp.concatenate((feedforward_up_bias, swap(feedforward_up_bias)))
    down_full = partner_shard(feedforward_down_weight, 0)

    def own_first(array):
        mine = lax.dynamic_slice_in_dim(array, me * half_width, half_width, 2)
        theirs = lax.dynamic_slice_in_dim(array, (1 - me) * half_width, half_width, 2)
        return mine, jnp.concatenate((mine, theirs), axis=2)

    down_low = adapter_down_factor.astype(bf16)
    down_pair = jnp.concatenate((down_low[0], down_low[1]), axis=1)
    up_mine, up_ordered = own_first(adapter_up_factor.astype(bf16))

    def dot(a, b):
        return jnp.dot(a, b, preferred_element_type=f32)

    def dot_t(a, b):
        return lax.dot_general(a, b, NT, preferred_element_type=f32)

    def project(rows, weight, up):
        normed = layer_norm(rows.astype(f32), first_norm_gain, first_norm_bias).astype(bf16)
        low = dot(normed, down_pair).astype(bf16)
        query = (dot(normed, weight[0]) + 8.0 * dot(low[:, :rank], up[0])).astype(bf16)
        key = dot(normed, weight[1]).astype(bf16)
        value = (dot(normed, weight[2]) + 8.0 * dot(low[:, rank:], up[1])).astype(bf16)
        return normed, low, query, key, value

    own_lens = lax.dynamic_slice_in_dim(lengths, whole * me, whole, 0)
    split_lens = lengths[split:]
    own_tokens = own(tokens, me)
    normed_s, low_s, query_s, key_s, value_s = project(
        tokens[split], query_key_value_weight, up_mine
    )
    heads_s = [piece[None] for piece in (query_s, key_s, value_s)]
    attended_s, lse_s = attention_forward(split_lens, *heads_s)
    attended_s = attended_s[0]

    def mine_rows(array):
        return lax.dynamic_slice_in_dim(array, me * half, half, 0)

    def theirs_rows(array):
        return lax.dynamic_slice_in_dim(array, (1 - me) * half, half, 0)

    attended_got = swap(theirs_rows(attended_s))
    normed_w, low_w, query_w, key_w, value_w = project(
        own_tokens[: whole * length], qkv_full, up_ordered
    )
    heads_w = [piece.reshape(whole, length, width) for piece in (query_w, key_w, value_w)]
    attended_w, lse_w = attention_forward(own_lens, *heads_w)
    attended = jnp.concatenate(
        (
            attended_w.reshape(whole * length, width),
            jnp.concatenate((mine_rows(attended_s), attended_got), axis=1),
        ),
        axis=0,
    )
    tokens_f32 = own_tokens.astype(f32)

    def norm_two(values):
        return layer_norm(values, second_norm_gain, second_norm_bias)

    def norm_one(values):
        return layer_norm(values, first_norm_gain, first_norm_bias)

    residual = tokens_f32 + (dot(attended, out_full) + attention_output_bias)
    normed_two = norm_two(residual).astype(bf16)
    hidden_pre = dot(normed_two, up_full) + up_bias
    hidden = gelu_tanh(hidden_pre).astype(bf16)
    block_own = (residual + dot(hidden, down_full) + feedforward_down_bias).astype(bf16)
    block_got = swap(block_own)

    def both(mine, got):
        first = jnp.where(me == 0, mine, got)
        second = jnp.where(me == 0, got, mine)
        parts = (
            first[: whole * length],
            second[: whole * length],
            first[whole * length :],
            second[whole * length :],
        )
        return jnp.concatenate(parts, axis=0).reshape(tokens.shape)

    block_out = both(block_own, block_got)
    at = jnp.arange(length)
    live = jnp.concatenate(
        (
            (at[None, :] < own_lens[:, None]).reshape(-1, 1),
            (mine_rows(at) < split_lens[0]).reshape(-1, 1),
        ),
        axis=0,
    )
    grad_out = jnp.where(live, own(cotangent, me), jnp.zeros((), bf16))
    grad_hidden = dot_t(grad_out, down_full)
    _, gelu_back = jax.vjp(gelu_tanh, hidden_pre)
    grad_pre = gelu_back(grad_hidden)[0].astype(bf16)
    grad_norm2 = dot_t(grad_pre, up_full)
    _, norm2_back = jax.vjp(norm_two, residual)
    grad_resid = grad_out.astype(f32) + norm2_back(grad_norm2)[0]
    grad_attended = dot_t(grad_resid.astype(bf16), out_full).astype(bf16)
    grad_got = swap(grad_attended[whole * length :, half_width:])
    grad_kept = grad_attended[whole * length :, :half_width]
    grad_s = jnp.concatenate(
        (
            jnp.where(me == 0, grad_kept, grad_got),
            jnp.where(me == 0, grad_got, grad_kept),
        ),
        axis=0,
    )
    grads_s = attention_backward(split_lens, *heads_s, grad_s[None], lse_s)
    grads_w = attention_backward(
        own_lens,
        *heads_w,
        grad_attended[: whole * length].reshape(whole, length, width),
        lse_w,
    )
    pack_s = jnp.stack([piece[0] for piece in grads_s])
    sent = swap(lax.dynamic_slice_in_dim(pack_s, (1 - me) * half, half, 1))
    kept = lax.dynamic_slice_in_dim(pack_s, me * half, half, 1)
    tail = jnp.concatenate((kept, sent), axis=2)
    grad_query, grad_key, grad_value = (
        jnp.concatenate((grads_w[i].reshape(whole * length, width), tail[i]), axis=0)
        for i in range(3)
    )
    adapter_gradient = 8.0 * jnp.concatenate(
        (dot_t(grad_query, up_ordered[0]), dot_t(grad_value, up_ordered[1])), axis=1
    )
    grad_norm1 = (
        dot_t(grad_query, qkv_full[0])
        + dot_t(grad_key, qkv_full[1])
        + dot_t(grad_value, qkv_full[2])
        + jnp.einsum(
            "gy,wy->gw", adapter_gradient, down_pair.astype(f32), precision=lax.Precision.HIGHEST
        )
    )
    _, norm1_back = jax.vjp(norm_one, tokens_f32)
    input_own = (grad_resid + norm1_back(grad_norm1)[0]).astype(bf16)
    input_grad = both(input_own, swap(input_own))

    normed = jnp.concatenate((normed_w, mine_rows(normed_s)), axis=0)
    low = jnp.concatenate((low_w, mine_rows(low_s)), axis=0)
    grad_down_both = jnp.einsum(
        "fi,fg->ig", normed.astype(f32), adapter_gradient, precision=lax.Precision.HIGHEST
    )
    grad_down = jnp.stack((grad_down_both[:, :rank], grad_down_both[:, rank:]))
    grad_up = 8.0 * jnp.stack(
        (
            jnp.einsum("zm,zj->mj", low[:, :rank], grad_query, preferred_element_type=f32),
            jnp.einsum("zm,zj->mj", low[:, rank:], grad_value, preferred_element_type=f32),
        )
    )
    first = jnp.where(me == 0, grad_up[:, :, :half_width], grad_up[:, :, half_width:])
    second = jnp.where(me == 0, grad_up[:, :, half_width:], grad_up[:, :, :half_width])
    grad_up = jnp.concatenate((first, second), axis=2)
    live_local = jnp.sum(lengths).astype(f32)
    down_sum, up_sum, live_sum = lax.psum((grad_down, grad_up, live_local), ("dp", "mp"))
    active = live_sum / 2
    new_down = adam_decay_update(
        adapter_down_factor, down_sum / active, down_first_moment, down_second_moment
    )
    new_up = adam_decay_update(
        adapter_up_factor, up_sum / active, up_first_moment, up_second_moment
    )
    return (
        block_out,
        input_grad,
        new_down[0],
        new_up[0],
        new_down[1],
        new_up[1],
        new_down[2],
        new_up[2],
    )


def solution(mesh):
    in_specs = (
        P("dp", None, None),
        P("dp", None, None),
        P("dp"),
        P(),
        P(),
        P(None, None, "mp"),
        P("mp", None),
        P(),
        P(),
        P(),
        P(None, "mp"),
        P("mp"),
        P("mp", None),
        P(),
        P(),
        P(),
        P(),
        P(),
        P(),
        P(),
    )
    out_specs = (P("dp", None, None), P("dp", None, None), P(), P(), P(), P(), P(), P())
    return jax.shard_map(
        per_device_pair if mesh.shape["mp"] == 2 else per_device,
        mesh=mesh,
        in_specs=in_specs,
        out_specs=out_specs,
        check_vma=False,
    )
```

```python
import functools

import jax
import jax.numpy as jnp
from jax import lax
from jax.experimental import pallas as pl
from jax.experimental.pallas import tpu as pltpu
from jax.sharding import PartitionSpec as P

HEAD = 64


def layer_norm(values, norm_gain, norm_shift):
    centre = values - jnp.mean(values, axis=-1, keepdims=True)
    spread = jnp.mean(centre * centre, axis=-1, keepdims=True)
    return centre * lax.rsqrt(spread + 1e-05) * norm_gain + norm_shift


def gelu_tanh(values):
    return (
        0.5
        * values
        * (1.0 + jnp.tanh(0.7978845608028654 * (values + 0.044715 * values * values * values)))
    )


def head_major(matrix, seq_rows, head_count):
    return (
        matrix.reshape(seq_rows, -1, head_count, HEAD)
        .transpose(0, 2, 1, 3)
        .reshape(seq_rows * head_count, -1, HEAD)
    )


def token_major(stacked, seq_rows, head_count):
    return (
        stacked.reshape(seq_rows, head_count, -1, HEAD)
        .transpose(0, 2, 1, 3)
        .reshape(-1, head_count * HEAD)
    )


def masked_scores(query_rows, key_rows, seq_len):
    scores = jnp.einsum(
        "qd,kd->qk", query_rows, key_rows, preferred_element_type=jnp.float32
    ) * HEAD ** (-0.5)
    position = jnp.arange(scores.shape[0])
    allowed = (position[None, :] <= position[:, None]) & (position[None, :] < seq_len)
    return jnp.where(allowed, scores, -1e30)


def attend_forward(pieces):
    query_rows, key_rows, value_token_rows, seq_len = pieces
    scores = masked_scores(query_rows, key_rows, seq_len)
    row_max = jnp.max(scores, axis=-1, keepdims=True)
    weights = jnp.exp(scores - row_max)
    row_sum = jnp.sum(weights, axis=-1, keepdims=True)
    probabilities = (weights / row_sum).astype(jnp.bfloat16)
    head_out = jnp.dot(probabilities, value_token_rows, preferred_element_type=jnp.float32)
    return (head_out, row_max[:, 0] + jnp.log(row_sum[:, 0]))


def attend_backward(pieces):
    query_rows, key_rows, value_token_rows, seq_len, grad_head, log_sums = pieces
    scores = masked_scores(query_rows, key_rows, seq_len)
    probabilities = jnp.exp(scores - log_sums[:, None])
    value_gradient_rows = jnp.einsum(
        "qk,qd->kd",
        probabilities.astype(jnp.bfloat16),
        grad_head,
        preferred_element_type=jnp.float32,
    )
    grad_probs = jnp.einsum(
        "qd,kd->qk", grad_head, value_token_rows, preferred_element_type=jnp.float32
    )
    grad_scores = probabilities * (
        grad_probs - jnp.sum(grad_probs * probabilities, axis=-1, keepdims=True)
    )
    grad_scores = grad_scores.astype(jnp.bfloat16)
    query_gradient_rows = jnp.dot(
        grad_scores, key_rows, preferred_element_type=jnp.float32
    ) * HEAD ** (-0.5)
    grad_keys = jnp.einsum(
        "qk,qd->kd", grad_scores, query_rows, preferred_element_type=jnp.float32
    ) * HEAD ** (-0.5)
    return (query_gradient_rows, grad_keys, value_gradient_rows)


def adam_decay_update(adapter, gradient, first_mom, second_mom):
    first_new = 0.9 * first_mom + 0.1 * gradient
    second_new = 0.999 * second_mom + 0.001 * gradient * gradient
    update = first_new / (1.0 - 0.9**10) / (jnp.sqrt(second_new / (1.0 - 0.999**10)) + 1e-08)
    return (adapter - 0.25 * (update + 0.01 * adapter), first_new, second_new)


def per_device(
    tokens,
    cotangent,
    lengths,
    first_norm_gain,
    first_norm_bias,
    query_key_value_weight,
    attention_output_weight,
    attention_output_bias,
    second_norm_gain,
    second_norm_bias,
    feedforward_up_weight,
    feedforward_up_bias,
    feedforward_down_weight,
    feedforward_down_bias,
    adapter_down_factor,
    adapter_up_factor,
    down_first_moment,
    up_first_moment,
    down_second_moment,
    up_second_moment,
):
    seq_rows, seq_len_all, model_width = tokens.shape
    tok_count = seq_rows * seq_len_all
    groups = lax.axis_size("mp")
    worker_shard = lax.axis_index("mp")
    shard_width = query_key_value_weight.shape[2]
    head_count = shard_width // HEAD
    adapter_rank_size = adapter_down_factor.shape[2]
    tokens_f32 = tokens.reshape(tok_count, model_width).astype(jnp.float32)
    normalized_rows = layer_norm(tokens_f32, first_norm_gain, first_norm_bias).astype(jnp.bfloat16)
    down_reduced = adapter_down_factor.astype(jnp.bfloat16)
    up_reduced = adapter_up_factor.astype(jnp.bfloat16)
    up_columns = lax.dynamic_slice_in_dim(up_reduced, worker_shard * shard_width, shard_width, 2)
    down_pair = jnp.concatenate((down_reduced[0], down_reduced[1]), axis=1)
    adapter_pair = jnp.dot(normalized_rows, down_pair, preferred_element_type=jnp.float32).astype(
        jnp.bfloat16
    )
    adapter_query_delta = adapter_pair[:, :adapter_rank_size]
    adapter_value_delta = adapter_pair[:, adapter_rank_size:]
    query_rows = (
        jnp.dot(normalized_rows, query_key_value_weight[0], preferred_element_type=jnp.float32)
        + 8.0 * jnp.dot(adapter_query_delta, up_columns[0], preferred_element_type=jnp.float32)
    ).astype(jnp.bfloat16)
    key_rows = jnp.dot(
        normalized_rows, query_key_value_weight[1], preferred_element_type=jnp.float32
    ).astype(jnp.bfloat16)
    value_token_rows = (
        jnp.dot(normalized_rows, query_key_value_weight[2], preferred_element_type=jnp.float32)
        + 8.0 * jnp.dot(adapter_value_delta, up_columns[1], preferred_element_type=jnp.float32)
    ).astype(jnp.bfloat16)
    limits = jnp.repeat(lengths, head_count)
    query_heads = head_major(query_rows, seq_rows, head_count)
    key_heads = head_major(key_rows, seq_rows, head_count)
    value_heads = head_major(value_token_rows, seq_rows, head_count)
    head_out, log_sums = lax.map(attend_forward, (query_heads, key_heads, value_heads, limits))
    attended = token_major(head_out, seq_rows, head_count).astype(jnp.bfloat16)
    attn_share = (
        lax.psum_scatter(
            jnp.dot(attended, attention_output_weight, preferred_element_type=jnp.float32),
            "mp",
            scatter_dimension=0,
            tiled=True,
        )
        + attention_output_bias
    )

    def norm_two(values):
        return layer_norm(values, second_norm_gain, second_norm_bias)

    def norm_one(values):
        return layer_norm(values, first_norm_gain, first_norm_bias)

    attn_full = lax.all_gather(attn_share, "mp", axis=0, tiled=True)
    residual = tokens_f32 + attn_full
    normed_two = norm_two(residual).astype(jnp.bfloat16)
    hidden_pre = (
        jnp.dot(normed_two, feedforward_up_weight, preferred_element_type=jnp.float32)
        + feedforward_up_bias
    )
    hidden = gelu_tanh(hidden_pre).astype(jnp.bfloat16)
    mlp_share = (
        lax.psum_scatter(
            jnp.dot(hidden, feedforward_down_weight, preferred_element_type=jnp.float32).astype(
                jnp.bfloat16
            ),
            "mp",
            scatter_dimension=0,
            tiled=True,
        ).astype(jnp.float32)
        + feedforward_down_bias
    )
    mlp_full = lax.all_gather(mlp_share.astype(jnp.bfloat16), "mp", axis=0, tiled=True).astype(
        mlp_share.dtype
    )
    block_out = (residual + mlp_full).astype(jnp.bfloat16)
    live_mask = (jnp.arange(seq_len_all)[None, :] < lengths[:, None]).reshape(tok_count, 1)
    grad_out = jnp.where(
        live_mask, cotangent.reshape(tok_count, model_width), jnp.zeros((), jnp.bfloat16)
    )
    grad_hidden = jnp.einsum(
        "td,fd->tf", grad_out, feedforward_down_weight, preferred_element_type=jnp.float32
    )
    _, gelu_back = jax.vjp(gelu_tanh, hidden_pre)
    grad_pre = gelu_back(grad_hidden)[0].astype(jnp.bfloat16)
    grad_norm2_share = lax.psum_scatter(
        jnp.einsum(
            "tf,df->td", grad_pre, feedforward_up_weight, preferred_element_type=jnp.float32
        ),
        "mp",
        scatter_dimension=0,
        tiled=True,
    )
    grad_norm2 = lax.all_gather(grad_norm2_share, "mp", axis=0, tiled=True)
    _, norm2_back = jax.vjp(norm_two, residual)
    grad_resid = grad_out.astype(jnp.float32) + norm2_back(grad_norm2)[0]
    grad_resid_low = grad_resid.astype(jnp.bfloat16)
    grad_attended = jnp.einsum(
        "td,ed->te", grad_resid_low, attention_output_weight, preferred_element_type=jnp.float32
    ).astype(jnp.bfloat16)
    grad_head = head_major(grad_attended, seq_rows, head_count)
    head_dq, head_dk, head_dv = lax.map(
        attend_backward, (query_heads, key_heads, value_heads, limits, grad_head, log_sums)
    )
    query_gradient_rows = token_major(head_dq, seq_rows, head_count).astype(jnp.bfloat16)
    grad_keys = token_major(head_dk, seq_rows, head_count).astype(jnp.bfloat16)
    value_gradient_rows = token_major(head_dv, seq_rows, head_count).astype(jnp.bfloat16)
    adapter_query_gradient = 8.0 * jnp.einsum(
        "te,re->tr", query_gradient_rows, up_columns[0], preferred_element_type=jnp.float32
    )
    adapter_value_gradient = 8.0 * jnp.einsum(
        "te,re->tr", value_gradient_rows, up_columns[1], preferred_element_type=jnp.float32
    )
    adapter_gradient = jnp.concatenate((adapter_query_gradient, adapter_value_gradient), axis=1)
    down_pair_float32 = down_pair.astype(jnp.float32)
    partial_sum = jnp.einsum(
        "te,de->td",
        query_gradient_rows,
        query_key_value_weight[0],
        preferred_element_type=jnp.float32,
    )
    partial_sum = partial_sum + jnp.einsum(
        "te,de->td", grad_keys, query_key_value_weight[1], preferred_element_type=jnp.float32
    )
    partial_sum = partial_sum + jnp.einsum(
        "te,de->td",
        value_gradient_rows,
        query_key_value_weight[2],
        preferred_element_type=jnp.float32,
    )
    grad_norm1_share = lax.psum_scatter(
        partial_sum
        + jnp.einsum(
            "gy,wy->gw", adapter_gradient, down_pair_float32, precision=lax.Precision.HIGHEST
        ),
        "mp",
        scatter_dimension=0,
        tiled=True,
    )
    grad_down_both = jnp.einsum(
        "fi,fg->ig",
        normalized_rows.astype(jnp.float32),
        adapter_gradient,
        precision=lax.Precision.HIGHEST,
    )
    grad_down = jnp.stack(
        (grad_down_both[:, :adapter_rank_size], grad_down_both[:, adapter_rank_size:])
    )
    grad_up_query = 8.0 * jnp.einsum(
        "zm,zj->mj", adapter_query_delta, query_gradient_rows, preferred_element_type=jnp.float32
    )
    grad_up_value = 8.0 * jnp.einsum(
        "zm,zj->mj", adapter_value_delta, value_gradient_rows, preferred_element_type=jnp.float32
    )
    up_column_gradient = jnp.stack((grad_up_query, grad_up_value))
    grad_up = lax.dynamic_update_slice_in_dim(
        jnp.zeros(adapter_up_factor.shape, jnp.float32),
        up_column_gradient,
        worker_shard * shard_width,
        2,
    )
    live_local = jnp.sum(lengths).astype(jnp.float32)
    down_reduced_sum, up_reduced_sum, live_sum = lax.psum(
        (grad_down, grad_up, live_local), ("dp", "mp")
    )
    active_token_total = live_sum / groups
    grad_norm1 = lax.all_gather(grad_norm1_share, "mp", axis=0, tiled=True)
    _, norm1_back = jax.vjp(norm_one, tokens_f32)
    input_grad = (grad_resid + norm1_back(grad_norm1)[0]).astype(jnp.bfloat16)
    down_factor_next, down_first_moment_next, down_second_moment_next = adam_decay_update(
        adapter_down_factor,
        down_reduced_sum / active_token_total,
        down_first_moment,
        down_second_moment,
    )
    up_factor_next, up_first_moment_next, up_second_moment_next = adam_decay_update(
        adapter_up_factor, up_reduced_sum / active_token_total, up_first_moment, up_second_moment
    )
    return (
        block_out.reshape(seq_rows, seq_len_all, model_width),
        input_grad.reshape(seq_rows, seq_len_all, model_width),
        down_factor_next,
        up_factor_next,
        down_first_moment_next,
        up_first_moment_next,
        down_second_moment_next,
        up_second_moment_next,
    )


TILE = 256
NT = (((1,), (1,)), ((), ()))


def head_lanes(half):
    lane = lax.broadcasted_iota(jnp.int32, (1, 2 * HEAD), 1)
    return (lane >= half * HEAD) & (lane < (half + 1) * HEAD)


def one_head(block, half):
    return jnp.where(head_lanes(half), block, jnp.zeros((), block.dtype))


def edge_allowed(key_start, query_start, seq_len):
    key_at = key_start + lax.broadcasted_iota(jnp.int32, (TILE, TILE), 0)
    query_at = query_start + lax.broadcasted_iota(jnp.int32, (TILE, TILE), 1)
    return (key_at <= query_at) & (key_at < seq_len)


def attention_forward_kernel(lens_ref, q_ref, k_ref, v_ref, out_ref, lse_ref, vt_ref):
    seq_len = lens_ref[pl.program_id(0)]
    live_tiles = (seq_len + TILE - 1) // TILE
    vt_ref[...] = v_ref[0].T
    tiles = q_ref.shape[1] // TILE

    def row_tile(tile, extent):
        rows = pl.ds(tile * TILE, TILE)
        inner = (extent - 1) * TILE
        query = q_ref[0, rows, :] * HEAD ** (-0.5)
        allowed = edge_allowed(inner, tile * TILE, seq_len)
        outs = []
        for half in range(2):
            mine = one_head(query, half)
            edge = lax.dot_general(
                k_ref[0, pl.ds(inner, TILE), :], mine, NT, preferred_element_type=jnp.float32
            )
            edge = jnp.where(allowed, edge, -1e30)
            top = jnp.max(edge, axis=0, keepdims=True)
            if inner:
                past = lax.dot_general(
                    k_ref[0, pl.ds(0, inner), :], mine, NT, preferred_element_type=jnp.float32
                )
                top = jnp.maximum(top, jnp.max(past, axis=0, keepdims=True))
            head_rows = pl.ds(half * HEAD, HEAD)
            edge = jnp.exp(edge - top)
            total = jnp.sum(edge, axis=0, keepdims=True)
            out = jnp.dot(
                vt_ref[head_rows, pl.ds(inner, TILE)],
                edge.astype(jnp.bfloat16),
                preferred_element_type=jnp.float32,
            )
            if inner:
                past = jnp.exp(past - top)
                total = total + jnp.sum(past, axis=0, keepdims=True)
                out = out + jnp.dot(
                    vt_ref[head_rows, pl.ds(0, inner)],
                    past.astype(jnp.bfloat16),
                    preferred_element_type=jnp.float32,
                )
            outs.append(out / total)
            lse_ref[0, 0, pl.ds(half, 1), rows] = top + jnp.log(total)
        out_ref[0, rows, :] = jnp.concatenate(outs, axis=0).T.astype(out_ref.dtype)

    for tile in range(tiles):
        for extent in range(1, tile + 2):
            pl.when(jnp.minimum(live_tiles, tile + 1) == extent)(
                lambda tile=tile, extent=extent: row_tile(tile, extent)
            )


def attention_forward(lens, query, key, value):
    seqs, length, width = query.shape
    pairs = width // (2 * HEAD)
    spec = pl.BlockSpec((1, length, 2 * HEAD), lambda s, h, lens: (s, 0, h))
    return pl.pallas_call(
        attention_forward_kernel,
        grid_spec=pltpu.PrefetchScalarGridSpec(
            num_scalar_prefetch=1,
            grid=(seqs, pairs),
            in_specs=[spec] * 3,
            out_specs=[spec, pl.BlockSpec((1, 1, 2, length), lambda s, h, lens: (s, h, 0, 0))],
            scratch_shapes=[pltpu.VMEM((2 * HEAD, length), jnp.bfloat16)],
        ),
        out_shape=[
            jax.ShapeDtypeStruct(query.shape, jnp.bfloat16),
            jax.ShapeDtypeStruct((seqs, pairs, 2, length), jnp.float32),
        ],
        cost_estimate=pl.CostEstimate(
            flops=seqs * width * length * length * 3,
            bytes_accessed=seqs * width * length * 8,
            transcendentals=seqs * pairs * length * length,
        ),
        name="attention_forward",
    )(lens, query, key, value)


def attention_backward_kernel(
    lens_ref, q_ref, k_ref, v_ref, g_ref, lse_ref, dq_ref, dk_ref, dv_ref, kt_ref, dk_acc, dv_acc
):
    seq_len = lens_ref[pl.program_id(0)]
    kt_ref[...] = k_ref[0].T
    dk_acc[...] = jnp.zeros_like(dk_acc)
    dv_acc[...] = jnp.zeros_like(dv_acc)
    tiles = q_ref.shape[1] // TILE

    def row_tile(tile):
        rows = pl.ds(tile * TILE, TILE)
        inner = tile * TILE
        query = q_ref[0, rows, :] * HEAD ** (-0.5)
        grad = g_ref[0, rows, :]
        allowed = edge_allowed(inner, inner, seq_len)
        spans = [(inner, TILE)] + ([(0, inner)] if inner else [])
        outs = []
        for half in range(2):
            mine = one_head(query, half)
            mine_grad = one_head(grad, half)
            lse = lse_ref[0, 0, pl.ds(half, 1), rows]
            probs, grad_probs, row_dot = [], [], 0.0
            for at, (start, size) in enumerate(spans):
                keys = pl.ds(start, size)
                scores = lax.dot_general(
                    k_ref[0, keys, :], mine, NT, preferred_element_type=jnp.float32
                )
                if at == 0:
                    scores = jnp.where(allowed, scores, -1e30)
                prob = jnp.exp(scores - lse)
                dv_acc[keys, :] += jnp.dot(
                    prob.astype(jnp.bfloat16), mine_grad, preferred_element_type=jnp.float32
                )
                grad_prob = lax.dot_general(
                    v_ref[0, keys, :], mine_grad, NT, preferred_element_type=jnp.float32
                )
                row_dot = row_dot + jnp.sum(prob * grad_prob, axis=0, keepdims=True)
                probs.append(prob)
                grad_probs.append(grad_prob)
            out = 0.0
            for (start, size), prob, grad_prob in zip(spans, probs, grad_probs):
                keys = pl.ds(start, size)
                grad_scores = (prob * (grad_prob - row_dot)).astype(jnp.bfloat16)
                dk_acc[keys, :] += jnp.dot(grad_scores, mine, preferred_element_type=jnp.float32)
                out = out + jnp.dot(
                    kt_ref[pl.ds(half * HEAD, HEAD), keys],
                    grad_scores,
                    preferred_element_type=jnp.float32,
                )
            outs.append(out)
        dq = jnp.concatenate(outs, axis=0).T * HEAD ** (-0.5)
        dq_ref[0, rows, :] = dq.astype(dq_ref.dtype)

    for tile in range(tiles):
        pl.when(tile * TILE < seq_len)(lambda tile=tile: row_tile(tile))

        @pl.when(tile * TILE >= seq_len)
        def _(tile=tile):
            dq_ref[0, pl.ds(tile * TILE, TILE), :] = jnp.zeros((TILE, 2 * HEAD), dq_ref.dtype)

    dk_ref[0] = dk_acc[...].astype(dk_ref.dtype)
    dv_ref[0] = dv_acc[...].astype(dv_ref.dtype)


def attention_backward(lens, query, key, value, grad, lse, start, grad_start):
    length, width = query.shape[1:]
    seqs = lens.shape[0]
    pairs = width // (2 * HEAD)

    def block(first):
        return pl.BlockSpec((1, length, 2 * HEAD), lambda s, h, lens: (s + first, 0, h))

    return pl.pallas_call(
        attention_backward_kernel,
        grid_spec=pltpu.PrefetchScalarGridSpec(
            num_scalar_prefetch=1,
            grid=(seqs, pairs),
            in_specs=[block(start)] * 3
            + [
                block(grad_start),
                pl.BlockSpec((1, 1, 2, length), lambda s, h, lens: (s + start, h, 0, 0)),
            ],
            out_specs=[block(0)] * 3,
            scratch_shapes=[
                pltpu.VMEM((2 * HEAD, length), jnp.bfloat16),
                pltpu.VMEM((length, 2 * HEAD), jnp.float32),
                pltpu.VMEM((length, 2 * HEAD), jnp.float32),
            ],
        ),
        out_shape=[jax.ShapeDtypeStruct((seqs, length, width), jnp.bfloat16)] * 3,
        cost_estimate=pl.CostEstimate(
            flops=seqs * width * length * length * 7,
            bytes_accessed=seqs * width * length * 14,
            transcendentals=seqs * pairs * length * length,
        ),
        name="attention_backward",
    )(lens, query, key, value, grad, lse)


MID_ROWS = 256
CHUNK = 1024


def centred(values):
    centre = values - jnp.mean(values, axis=-1, keepdims=True)
    inverse = lax.rsqrt(jnp.mean(centre * centre, axis=-1, keepdims=True) + 1e-05)
    return centre * inverse, inverse


def norm_backward(grad, gain, normal, inverse):
    grad = grad * gain
    mean = jnp.mean(grad, axis=-1, keepdims=True)
    along = jnp.mean(grad * normal, axis=-1, keepdims=True)
    return (grad - mean - normal * along) * inverse


def dot(a, b):
    return jnp.dot(a, b, preferred_element_type=jnp.float32)


def dot_t(a, b):
    return lax.dot_general(a, b, NT, preferred_element_type=jnp.float32)


def copies_of(pairs, sems):
    return [pltpu.make_async_copy(a, b, sems.at[i]) for i, (a, b) in enumerate(pairs)]


def middle_kernel(
    table_ref,
    tokens_ref,
    cotangent_ref,
    attended_own,
    attended_far,
    out_bias_ref,
    gain_ref,
    shift_ref,
    up_bias_ref,
    down_bias_ref,
    out_own,
    out_near,
    out_far,
    up_own,
    up_near,
    up_far,
    down_own,
    down_near,
    down_far,
    block_ref,
    resid_grad_ref,
    own_grad_ref,
    far_grad_ref,
    out_w,
    up_w,
    down_w,
    residual_ref,
    normed_ref,
    normal_ref,
    acc_ref,
    grad_acc_ref,
    sems,
):
    step = pl.program_id(0)

    pairs = []
    start = 0
    for piece in (out_own, out_near, out_far):
        rows = piece.shape[0]
        pairs.append((piece, out_w.at[pl.ds(start, rows), :]))
        start += rows
    chunk = 0
    for up, down in ((up_own, down_own), (up_near, down_near), (up_far, down_far)):
        for at in range(up.shape[1] // CHUNK):
            units = pl.ds(at * CHUNK, CHUNK)
            pairs.append((up.at[:, units], up_w.at[chunk]))
            pairs.append((down.at[units, :], down_w.at[chunk]))
            chunk += 1
    loads = copies_of(pairs, sems)

    @pl.when(step == 0)
    def _():
        for load in loads:
            load.start()
        for load in loads[:3]:
            load.wait()

    live = table_ref[2, step]
    residual = tokens_ref[...].astype(jnp.float32) + (
        dot(jnp.concatenate((attended_own[...], attended_far[...]), axis=1), out_w[...])
        + out_bias_ref[...]
    )
    residual_ref[...] = residual
    normal, inverse = centred(residual)
    normal_ref[...] = normal
    normed_ref[...] = (normal * gain_ref[...] + shift_ref[...]).astype(jnp.bfloat16)
    acc_ref[...] = jnp.zeros_like(acc_ref)

    @pl.when(step == 0)
    def _():
        for load in loads[3:]:
            load.wait()

    scale = 0.7978845608028654
    cube = 0.044715 * scale

    def forward_only(chunk, carry):
        pre = dot(normed_ref[...], up_w[chunk]) + up_bias_ref[chunk]
        tanh = jnp.tanh(pre * (scale + cube * (pre * pre)))
        hidden = (pre * (0.5 + 0.5 * tanh)).astype(jnp.bfloat16)
        acc_ref[...] += dot(hidden, down_w[chunk])
        return carry

    def finish():
        block_ref[...] = (residual_ref[...] + acc_ref[...] + down_bias_ref[...]).astype(
            block_ref.dtype
        )

    @pl.when(live > 0)
    def _():
        row = lax.broadcasted_iota(jnp.int32, (MID_ROWS, 1), 0)
        grad_out = jnp.where(row < live, cotangent_ref[...], jnp.zeros((), jnp.bfloat16))
        grad_acc_ref[...] = jnp.zeros_like(grad_acc_ref)

        def both_ways(chunk, carry):
            pre = dot(normed_ref[...], up_w[chunk]) + up_bias_ref[chunk]
            grad_hidden = dot_t(grad_out, down_w[chunk])
            square = pre * pre
            tanh = jnp.tanh(pre * (scale + cube * square))
            gate = 0.5 + 0.5 * tanh
            hidden = (pre * gate).astype(jnp.bfloat16)
            slope = gate + (pre * (0.5 - 0.5 * (tanh * tanh))) * (scale + 3.0 * cube * square)
            grad_pre = (grad_hidden * slope).astype(jnp.bfloat16)
            acc_ref[...] += dot(hidden, down_w[chunk])
            grad_acc_ref[...] += dot_t(grad_pre, up_w[chunk])
            return carry

        lax.fori_loop(0, up_w.shape[0], both_ways, 0, unroll=UNROLL)
        finish()
        grad_resid = grad_out.astype(jnp.float32) + norm_backward(
            grad_acc_ref[...], gain_ref[...], normal_ref[...], inverse
        )
        low = grad_resid.astype(jnp.bfloat16)
        resid_grad_ref[...] = low
        columns = own_grad_ref.shape[1]
        own_grad_ref[...] = dot_t(low, out_w[:columns]).astype(jnp.bfloat16)
        far_grad_ref[...] = dot_t(low, out_w[columns:]).astype(jnp.bfloat16)

    @pl.when(live <= 0)
    def _():
        lax.fori_loop(0, up_w.shape[0], forward_only, 0, unroll=UNROLL)
        finish()
        resid_grad_ref[...] = jnp.zeros_like(resid_grad_ref)
        own_grad_ref[...] = jnp.zeros_like(own_grad_ref)
        far_grad_ref[...] = jnp.zeros_like(far_grad_ref)


UNROLL = 2


def middle(
    table, tokens, cotangent, own, far, out_bias, gain, shift, up_bias, down_bias, weights
):
    rows, width = far.shape[0], tokens.shape[1]
    columns = far.shape[1]
    units = up_bias.shape[0] * up_bias.shape[2]
    tile = pl.BlockSpec((MID_ROWS, width), lambda i, t: (i, 0))
    picked = pl.BlockSpec((MID_ROWS, width), lambda i, t: (t[0, i], 0))
    part = pl.BlockSpec((MID_ROWS, columns), lambda i, t: (i, 0))
    vector = pl.BlockSpec((1, width), lambda i, t: (0, 0))
    chunks = units // CHUNK
    low = jax.ShapeDtypeStruct((rows, width), jnp.bfloat16)
    thin = jax.ShapeDtypeStruct((rows, columns), jnp.bfloat16)
    wide = pltpu.VMEM((MID_ROWS, width), jnp.float32)
    return pl.pallas_call(
        middle_kernel,
        grid_spec=pltpu.PrefetchScalarGridSpec(
            num_scalar_prefetch=1,
            grid=(rows // MID_ROWS,),
            in_specs=[picked] * 2
            + [pl.BlockSpec((MID_ROWS, columns), lambda i, t: (t[1, i], 0)), part]
            + [vector] * 3
            + [pl.BlockSpec(up_bias.shape, lambda i, t: (0, 0, 0)), vector]
            + [pl.BlockSpec(memory_space=pl.ANY)] * 9,
            out_specs=[tile, tile, part, part],
            scratch_shapes=[
                pltpu.VMEM((width, width), jnp.bfloat16),
                pltpu.VMEM((chunks, width, CHUNK), jnp.bfloat16),
                pltpu.VMEM((chunks, CHUNK, width), jnp.bfloat16),
                wide,
                pltpu.VMEM((MID_ROWS, width), jnp.bfloat16),
                wide,
                wide,
                wide,
                pltpu.SemaphoreType.DMA((3 + 2 * chunks,)),
            ],
        ),
        out_shape=[low, low, thin, thin],
        compiler_params=pltpu.CompilerParams(vmem_limit_bytes=56 << 20),
        cost_estimate=pl.CostEstimate(
            flops=rows * width * (units * 8 + width * 4),
            bytes_accessed=rows * width * 12 + units * width * 4,
            transcendentals=rows * units,
        ),
        name="middle",
    )(
        table,
        tokens,
        cotangent,
        own,
        far,
        out_bias,
        gain,
        shift,
        up_bias,
        down_bias,
        *weights,
    )


PROJECT_ROWS = 256


def qkv_loads(own, near, far, weight_ref, sems):
    pairs = []
    start = 0
    for piece in (own, near, far):
        if piece is not None:
            columns = pl.ds(start, piece.shape[2])
            pairs.append((piece, weight_ref.at[:, :, columns]))
            start += piece.shape[2]
    return copies_of(pairs, sems)


def project_kernel(pieces, table_ref, *refs):
    tokens_ref, gain_ref, shift_ref, down_ref, up_ref = refs[:5]
    weights = list(refs[5 : 5 + pieces]) + [None] * (3 - pieces)
    query_ref, key_ref, value_ref, low_ref, weight_ref, sems = refs[5 + pieces :]
    loads = qkv_loads(*weights, weight_ref, sems)
    first = pl.program_id(0) == 0

    @pl.when(first)
    def _():
        for load in loads:
            load.start()

    normal, _ = centred(tokens_ref[...].astype(jnp.float32))
    normed = (normal * gain_ref[...] + shift_ref[...]).astype(jnp.bfloat16)
    low = dot_t(normed, down_ref[...]).astype(jnp.bfloat16)
    low_ref[...] = low.astype(jnp.float32).T

    @pl.when(first)
    def _():
        for load in loads:
            load.wait()

    query_ref[...] = (dot(normed, weight_ref[0]) + 8.0 * dot(low, up_ref[0])).astype(jnp.bfloat16)
    key_ref[...] = dot(normed, weight_ref[1]).astype(jnp.bfloat16)
    value_ref[...] = (dot(normed, weight_ref[2]) + 8.0 * dot(low, up_ref[1])).astype(jnp.bfloat16)


def project(table, tokens, gain, shift, down, up, *weights):
    rows, width = table.shape[0] * PROJECT_ROWS, tokens.shape[1]
    columns = up.shape[2]
    pairs = down.shape[0]
    out = pl.BlockSpec((PROJECT_ROWS, columns), lambda i, t: (i, 0))
    vector = pl.BlockSpec((1, width), lambda i, t: (0, 0))
    return pl.pallas_call(
        functools.partial(project_kernel, len(weights)),
        grid_spec=pltpu.PrefetchScalarGridSpec(
            num_scalar_prefetch=1,
            grid=(rows // PROJECT_ROWS,),
            in_specs=[
                pl.BlockSpec((PROJECT_ROWS, width), lambda i, t: (t[i], 0)),
                vector,
                vector,
                pl.BlockSpec(down.shape, lambda i, t: (0, 0)),
                pl.BlockSpec(up.shape, lambda i, t: (0, 0, 0)),
            ]
            + [pl.BlockSpec(memory_space=pl.ANY)] * len(weights),
            out_specs=[out] * 3 + [pl.BlockSpec((pairs, PROJECT_ROWS), lambda i, t: (0, i))],
            scratch_shapes=[
                pltpu.VMEM((3, width, columns), jnp.bfloat16),
                pltpu.SemaphoreType.DMA((len(weights),)),
            ],
        ),
        out_shape=[jax.ShapeDtypeStruct((rows, columns), jnp.bfloat16)] * 3
        + [jax.ShapeDtypeStruct((pairs, rows), jnp.float32)],
        cost_estimate=pl.CostEstimate(
            flops=rows * width * columns * 6,
            bytes_accessed=rows * (width + 3 * columns) * 2 + 6 * width * columns,
            transcendentals=rows,
        ),
        name="project",
    )(table, tokens, gain, shift, down, up, *weights)


def first_backward_kernel(
    table_ref,
    tokens_ref,
    resid_grad_ref,
    low_ref,
    query_own,
    key_own,
    value_own,
    query_far,
    key_far,
    value_far,
    gain_ref,
    shift_ref,
    down_ref,
    up_ref,
    own_ref,
    near_ref,
    far_ref,
    input_ref,
    down_grad_ref,
    query_up_ref,
    value_up_ref,
    weight_ref,
    sems,
):
    first = pl.program_id(0) == 0
    loads = qkv_loads(own_ref, near_ref, far_ref, weight_ref, sems)

    @pl.when(first)
    def _():
        for load in loads:
            load.start()
        down_grad_ref[...] = jnp.zeros_like(down_grad_ref)
        query_up_ref[...] = jnp.zeros_like(query_up_ref)
        value_up_ref[...] = jnp.zeros_like(value_up_ref)

    normal, inverse = centred(tokens_ref[...].astype(jnp.float32))
    normed = (normal * gain_ref[...] + shift_ref[...]).astype(jnp.bfloat16)
    query = jnp.concatenate((query_own[...], query_far[...]), axis=1)
    key = jnp.concatenate((key_own[...], key_far[...]), axis=1)
    value = jnp.concatenate((value_own[...], value_far[...]), axis=1)
    adapter = 8.0 * (dot_t(query, up_ref[0]) + dot_t(value, up_ref[1]))
    high = adapter.astype(jnp.bfloat16)
    rest = (adapter - high.astype(jnp.float32)).astype(jnp.bfloat16)
    down_grad_ref[...] += dot(high.astype(jnp.float32).T.astype(jnp.bfloat16), normed) + dot(
        rest.astype(jnp.float32).T.astype(jnp.bfloat16), normed
    )
    low = low_ref[...].astype(jnp.bfloat16)
    query_up_ref[...] += dot(low, query)
    value_up_ref[...] += dot(low, value)

    @pl.when(first)
    def _():
        for load in loads:
            load.wait()

    grad = (
        dot_t(query, weight_ref[0])
        + dot_t(key, weight_ref[1])
        + dot_t(value, weight_ref[2])
        + dot(high, down_ref[...])
        + dot(rest, down_ref[...])
    )
    input_ref[...] = (
        resid_grad_ref[...].astype(jnp.float32)
        + norm_backward(grad, gain_ref[...], normal, inverse)
    ).astype(input_ref.dtype)


def first_backward(
    table, tokens, resid_grad, low, own, far, gain, shift, down, up, weights
):
    tiles = table.shape[1]
    rows, width = tiles * PROJECT_ROWS, tokens.shape[1]
    pairs = down.shape[0]
    columns = own[0].shape[1]
    tile = pl.BlockSpec((PROJECT_ROWS, width), lambda i, t: (t[0, i], 0))
    vector = pl.BlockSpec((1, width), lambda i, t: (0, 0))
    small = pl.BlockSpec((pairs, width), lambda i, t: (0, 0))
    sums = jax.ShapeDtypeStruct((pairs, width), jnp.float32)
    return pl.pallas_call(
        first_backward_kernel,
        grid_spec=pltpu.PrefetchScalarGridSpec(
            num_scalar_prefetch=1,
            grid=(tiles,),
            in_specs=[
                tile,
                pl.BlockSpec((PROJECT_ROWS, width), lambda i, t: (t[1, i], 0)),
                pl.BlockSpec((pairs, PROJECT_ROWS), lambda i, t: (0, t[2, i])),
            ]
            + [pl.BlockSpec((PROJECT_ROWS, columns), lambda i, t: (t[3, i], 0))] * 3
            + [pl.BlockSpec((PROJECT_ROWS, columns), lambda i, t: (i, 0))] * 3
            + [vector, vector, small, pl.BlockSpec(up.shape, lambda i, t: (0, 0, 0))]
            + [pl.BlockSpec(memory_space=pl.ANY)] * 3,
            out_specs=[pl.BlockSpec((PROJECT_ROWS, width), lambda i, t: (i, 0))] + [small] * 3,
            scratch_shapes=[
                pltpu.VMEM((3, width, width), jnp.bfloat16),
                pltpu.SemaphoreType.DMA((3,)),
            ],
        ),
        out_shape=[jax.ShapeDtypeStruct((rows, width), jnp.bfloat16)] + [sums] * 3,
        cost_estimate=pl.CostEstimate(
            flops=rows * width * width * 7,
            bytes_accessed=rows * width * 12 + 6 * width * width,
            transcendentals=rows,
        ),
        name="first_backward",
    )(table, tokens, resid_grad, low, *own, *far, gain, shift, down, up, *weights)


def swap(value):
    return lax.ppermute(value, "mp", [(0, 1), (1, 0)])


def after(value, *earlier):
    return lax.optimization_barrier((value, *earlier))[0]


def core_swap(value):
    return lax.ppermute(value, "dp", [(i, i ^ 1) for i in range(lax.axis_size("dp"))])


def core_half(shard, axis):
    size = shard.shape[axis] // 2
    core = lax.rem(lax.axis_index("dp"), 2)
    return lax.dynamic_slice_in_dim(shard, core * size, size, axis)


def core_order(value, axis):
    size = value.shape[axis] // 2
    core = lax.rem(lax.axis_index("dp"), 2)
    low = lax.slice_in_dim(value, 0, size, axis=axis)
    high = lax.slice_in_dim(value, size, 2 * size, axis=axis)
    return jnp.where(
        core == 0, value, jnp.concatenate((high, low), axis=axis)
    )


def sum_all(value):
    count = lax.axis_size("dp")
    if count & (count - 1):
        return lax.psum(value, ("dp", "mp"))
    bit = 1
    while bit < count:
        value = value + lax.ppermute(value, "dp", [(i, i ^ bit) for i in range(count)])
        bit *= 2
    return value + swap(value)


def per_device_pair(
    tokens,
    cotangent,
    lengths,
    first_norm_gain,
    first_norm_bias,
    query_key_value_weight,
    attention_output_weight,
    attention_output_bias,
    second_norm_gain,
    second_norm_bias,
    feedforward_up_weight,
    feedforward_up_bias,
    feedforward_down_weight,
    feedforward_down_bias,
    adapter_down_factor,
    adapter_up_factor,
    down_first_moment,
    up_first_moment,
    down_second_moment,
    up_second_moment,
):
    f32, bf16 = jnp.float32, jnp.bfloat16
    seqs, length, width = tokens.shape
    rank = adapter_down_factor.shape[2]
    me = lax.axis_index("mp")
    columns = query_key_value_weight.shape[2]
    whole, half = 2, length // 2
    split = 2 * whole
    tiles, half_tiles = length // MID_ROWS, half // MID_ROWS

    def row(vector):
        return vector.reshape(1, -1)

    qkv_near = swap(core_half(query_key_value_weight, 2))
    qkv_far = core_swap(qkv_near)
    out_near = swap(after(core_half(attention_output_weight, 0), qkv_near))
    out_far = core_swap(out_near)
    up_near = swap(after(core_half(feedforward_up_weight, 1), out_near))
    up_far = core_swap(up_near)
    down_near = swap(after(core_half(feedforward_down_weight, 0), up_near))
    down_far = core_swap(down_near)
    qkv = (query_key_value_weight, qkv_near, qkv_far)
    up_bias = jnp.concatenate(
        (feedforward_up_bias, core_order(swap(feedforward_up_bias), 0))
    ).reshape(-1, 1, CHUNK)

    down_low = adapter_down_factor.astype(bf16).transpose(0, 2, 1).reshape(2 * rank, width)
    up_low = adapter_up_factor.astype(bf16)
    blank = jnp.zeros_like(up_low[0])
    up_low = jnp.stack(
        (jnp.concatenate((up_low[0], blank)), jnp.concatenate((blank, up_low[1])))
    )
    up_own = lax.dynamic_slice_in_dim(up_low, me * columns, columns, 2)
    up_other = core_order(
        lax.dynamic_slice_in_dim(up_low, (1 - me) * columns, columns, 2), 2
    )
    up_both = jnp.concatenate((up_own, up_other), axis=2)

    own_lens = lax.dynamic_slice_in_dim(lengths, whole * me, whole, 0)
    split_lens = lengths[split:]
    three_lens = jnp.concatenate((own_lens, split_lens))
    flat_tokens = tokens.reshape(-1, width)
    flat_cotangent = cotangent.reshape(-1, width)
    step = jnp.arange(whole * tiles, dtype=jnp.int32)
    extra = jnp.arange(half_tiles, dtype=jnp.int32) + me * half_tiles
    whole_table = step + whole * me * tiles
    token_table = jnp.concatenate((whole_table, split * tiles + extra))
    own_table = jnp.concatenate((step, whole * tiles + extra))
    live_table = jnp.concatenate(
        (
            own_lens[step // tiles] - (step % tiles) * MID_ROWS,
            split_lens[0] - extra * MID_ROWS,
        )
    )
    three_table = jnp.concatenate(
        (whole_table, split * tiles + jnp.arange(tiles, dtype=jnp.int32))
    )
    gain_one, shift_one = row(first_norm_gain), row(first_norm_bias)

    def sequences(pieces):
        return [piece.reshape(-1, length, columns) for piece in pieces]

    *own_heads, low = project(
        three_table,
        flat_tokens,
        gain_one,
        shift_one,
        down_low,
        up_own,
        query_key_value_weight,
    )
    own_heads = sequences(own_heads)
    attended_own, lse_own = attention_forward(three_lens, *own_heads)
    sent = lax.dynamic_slice_in_dim(attended_own[whole], (1 - me) * half, half, 0)
    attended_got = swap(core_order(sent, 1))
    *far_heads, _ = project(
        whole_table,
        flat_tokens,
        gain_one,
        shift_one,
        down_low,
        up_other,
        qkv_near,
        after(qkv_far, attended_own),
    )
    far_heads = sequences(far_heads)
    attended_far, lse_far = attention_forward(own_lens, *far_heads)
    block_own, resid_grad, grad_own, grad_far = middle(
        jnp.stack((token_table, own_table, live_table)),
        flat_tokens,
        flat_cotangent,
        attended_own.reshape(-1, columns),
        jnp.concatenate((attended_far.reshape(-1, columns), attended_got), axis=0),
        row(attention_output_bias),
        row(second_norm_gain),
        row(second_norm_bias),
        up_bias,
        row(feedforward_down_bias),
        (
            attention_output_weight,
            out_near,
            out_far,
            feedforward_up_weight,
            up_near,
            up_far,
            feedforward_down_weight,
            down_near,
            down_far,
        ),
    )
    grad_got = swap(core_order(grad_far[whole * length :], 1))
    block_got = swap(after(block_own, grad_got))
    grad_kept = grad_own[whole * length :]
    grad_split = jnp.concatenate(
        (jnp.where(me == 0, grad_kept, grad_got), jnp.where(me == 0, grad_got, grad_kept))
    )
    grad_own = grad_own[: whole * length].reshape(whole, length, columns)
    grad_far = grad_far[: whole * length].reshape(whole, length, columns)

    def flat(pieces):
        return [piece.reshape(-1, columns) for piece in pieces]

    def back_whole(index):
        lens = own_lens[index : index + 1]
        own = attention_backward(lens, *own_heads, grad_own, lse_own, index, index)
        far = attention_backward(lens, *far_heads, grad_far, lse_far, index, index)
        return flat(own), flat(far)

    span = jnp.arange(tiles, dtype=jnp.int32)

    def back_first(own, far, table):
        return first_backward(
            table,
            flat_tokens,
            resid_grad,
            low,
            own,
            far,
            gain_one,
            shift_one,
            down_low,
            up_both,
            qkv,
        )

    def whole_rows(index):
        at = index * tiles + span
        return jnp.stack((whole * me * tiles + at, at, at, span))

    back_zero = back_whole(0)
    split_own = attention_backward(
        split_lens, *own_heads, grad_split[None], lse_own, whole, 0
    )
    split_sent = jnp.stack(
        [lax.dynamic_slice_in_dim(p[0], (1 - me) * half, half, 0) for p in split_own]
    )
    split_got = swap(
        core_order(split_sent, 2)
    )
    first_zero = back_first(*back_zero, whole_rows(0))
    send_zero = swap(first_zero[0])
    back_one = back_whole(1)
    first_split = back_first(
        flat(split_own),
        [split_got[i] for i in range(3)],
        jnp.stack(
            (
                split * tiles + extra,
                whole * tiles + extra - me * half_tiles,
                whole * tiles + extra,
                extra,
            )
        ),
    )
    send_split = swap(first_split[0])
    first_one = back_first(*back_one, whole_rows(1))
    send_one = swap(first_one[0])

    down_sum, query_sum, value_sum = (
        first_zero[i] + first_split[i] + first_one[i] for i in range(1, 4)
    )
    up_sum = 8.0 * jnp.concatenate((query_sum[:rank], value_sum[rank:]))
    up_mine = up_sum[:, :columns]
    up_theirs = core_order(up_sum[:, columns:], 1)
    up_sum = jnp.concatenate(
        (jnp.where(me == 0, up_mine, up_theirs), jnp.where(me == 0, up_theirs, up_mine)), axis=1
    )
    live_row = jnp.full((8, width), jnp.sum(lengths).astype(f32))
    total = sum_all(jnp.concatenate((down_sum, up_sum, live_row)))
    active = total[-1, 0] / 2
    grad_down = total[: 2 * rank].reshape(2, rank, width).transpose(0, 2, 1) / active
    grad_up = total[2 * rank : 4 * rank].reshape(2, rank, width) / active

    def place(pieces):
        out = jnp.zeros((seqs * length, width), bf16)
        for piece, start in pieces:
            out = lax.dynamic_update_slice_in_dim(out, piece, start, 0)
        return out.reshape(tokens.shape)

    mine, theirs = whole * length * me, whole * length * (1 - me)
    block_out = place(
        (
            (block_own[: whole * length], mine),
            (block_own[whole * length :], split * length + half * me),
            (block_got[: whole * length], theirs),
            (block_got[whole * length :], split * length + half * (1 - me)),
        )
    )
    input_grad = place(
        (
            (first_zero[0], mine),
            (first_split[0], split * length + half * me),
            (first_one[0], mine + length),
            (send_zero, theirs),
            (send_split, split * length + half * (1 - me)),
            (send_one, theirs + length),
        )
    )
    new_down = adam_decay_update(
        adapter_down_factor, grad_down, down_first_moment, down_second_moment
    )
    new_up = adam_decay_update(adapter_up_factor, grad_up, up_first_moment, up_second_moment)
    return (
        block_out,
        input_grad,
        new_down[0],
        new_up[0],
        new_down[1],
        new_up[1],
        new_down[2],
        new_up[2],
    )


def solution(mesh):
    in_specs = (
        P("dp", None, None),
        P("dp", None, None),
        P("dp"),
        P(),
        P(),
        P(None, None, "mp"),
        P("mp", None),
        P(),
        P(),
        P(),
        P(None, "mp"),
        P("mp"),
        P("mp", None),
        P(),
        P(),
        P(),
        P(),
        P(),
        P(),
        P(),
    )
    out_specs = (P("dp", None, None), P("dp", None, None), P(), P(), P(), P(), P(), P())
    return jax.shard_map(
        per_device_pair if mesh.shape["mp"] == 2 else per_device,
        mesh=mesh,
        in_specs=in_specs,
        out_specs=out_specs,
        check_vma=False,
    )
```

```python
import functools

import jax
import jax.numpy as jnp
from jax import lax
from jax.experimental import pallas as pl
from jax.experimental.pallas import tpu as pltpu
from jax.sharding import PartitionSpec as P

HEAD = 64


def layer_norm(values, norm_gain, norm_shift):
    centre = values - jnp.mean(values, axis=-1, keepdims=True)
    spread = jnp.mean(centre * centre, axis=-1, keepdims=True)
    return centre * lax.rsqrt(spread + 1e-05) * norm_gain + norm_shift


def gelu_tanh(values):
    return (
        0.5
        * values
        * (1.0 + jnp.tanh(0.7978845608028654 * (values + 0.044715 * values * values * values)))
    )


def head_major(matrix, seq_rows, head_count):
    return (
        matrix.reshape(seq_rows, -1, head_count, HEAD)
        .transpose(0, 2, 1, 3)
        .reshape(seq_rows * head_count, -1, HEAD)
    )


def token_major(stacked, seq_rows, head_count):
    return (
        stacked.reshape(seq_rows, head_count, -1, HEAD)
        .transpose(0, 2, 1, 3)
        .reshape(-1, head_count * HEAD)
    )


def masked_scores(query_rows, key_rows, seq_len):
    scores = jnp.einsum(
        "qd,kd->qk", query_rows, key_rows, preferred_element_type=jnp.float32
    ) * HEAD ** (-0.5)
    position = jnp.arange(scores.shape[0])
    allowed = (position[None, :] <= position[:, None]) & (position[None, :] < seq_len)
    return jnp.where(allowed, scores, -1e30)


def attend_forward(pieces):
    query_rows, key_rows, value_token_rows, seq_len = pieces
    scores = masked_scores(query_rows, key_rows, seq_len)
    row_max = jnp.max(scores, axis=-1, keepdims=True)
    weights = jnp.exp(scores - row_max)
    row_sum = jnp.sum(weights, axis=-1, keepdims=True)
    probabilities = (weights / row_sum).astype(jnp.bfloat16)
    head_out = jnp.dot(probabilities, value_token_rows, preferred_element_type=jnp.float32)
    return (head_out, row_max[:, 0] + jnp.log(row_sum[:, 0]))


def attend_backward(pieces):
    query_rows, key_rows, value_token_rows, seq_len, grad_head, log_sums = pieces
    scores = masked_scores(query_rows, key_rows, seq_len)
    probabilities = jnp.exp(scores - log_sums[:, None])
    value_gradient_rows = jnp.einsum(
        "qk,qd->kd",
        probabilities.astype(jnp.bfloat16),
        grad_head,
        preferred_element_type=jnp.float32,
    )
    grad_probs = jnp.einsum(
        "qd,kd->qk", grad_head, value_token_rows, preferred_element_type=jnp.float32
    )
    grad_scores = probabilities * (
        grad_probs - jnp.sum(grad_probs * probabilities, axis=-1, keepdims=True)
    )
    grad_scores = grad_scores.astype(jnp.bfloat16)
    query_gradient_rows = jnp.dot(
        grad_scores, key_rows, preferred_element_type=jnp.float32
    ) * HEAD ** (-0.5)
    grad_keys = jnp.einsum(
        "qk,qd->kd", grad_scores, query_rows, preferred_element_type=jnp.float32
    ) * HEAD ** (-0.5)
    return (query_gradient_rows, grad_keys, value_gradient_rows)


def adam_decay_update(adapter, gradient, first_mom, second_mom):
    first_new = 0.9 * first_mom + 0.1 * gradient
    second_new = 0.999 * second_mom + 0.001 * gradient * gradient
    update = first_new / (1.0 - 0.9**10) / (jnp.sqrt(second_new / (1.0 - 0.999**10)) + 1e-08)
    return (adapter - 0.25 * (update + 0.01 * adapter), first_new, second_new)


def per_device(
    tokens,
    cotangent,
    lengths,
    first_norm_gain,
    first_norm_bias,
    query_key_value_weight,
    attention_output_weight,
    attention_output_bias,
    second_norm_gain,
    second_norm_bias,
    feedforward_up_weight,
    feedforward_up_bias,
    feedforward_down_weight,
    feedforward_down_bias,
    adapter_down_factor,
    adapter_up_factor,
    down_first_moment,
    up_first_moment,
    down_second_moment,
    up_second_moment,
):
    seq_rows, seq_len_all, model_width = tokens.shape
    tok_count = seq_rows * seq_len_all
    groups = lax.axis_size("mp")
    worker_shard = lax.axis_index("mp")
    shard_width = query_key_value_weight.shape[2]
    head_count = shard_width // HEAD
    adapter_rank_size = adapter_down_factor.shape[2]
    tokens_f32 = tokens.reshape(tok_count, model_width).astype(jnp.float32)
    normalized_rows = layer_norm(tokens_f32, first_norm_gain, first_norm_bias).astype(jnp.bfloat16)
    down_reduced = adapter_down_factor.astype(jnp.bfloat16)
    up_reduced = adapter_up_factor.astype(jnp.bfloat16)
    up_columns = lax.dynamic_slice_in_dim(up_reduced, worker_shard * shard_width, shard_width, 2)
    down_pair = jnp.concatenate((down_reduced[0], down_reduced[1]), axis=1)
    adapter_pair = jnp.dot(normalized_rows, down_pair, preferred_element_type=jnp.float32).astype(
        jnp.bfloat16
    )
    adapter_query_delta = adapter_pair[:, :adapter_rank_size]
    adapter_value_delta = adapter_pair[:, adapter_rank_size:]
    query_rows = (
        jnp.dot(normalized_rows, query_key_value_weight[0], preferred_element_type=jnp.float32)
        + 8.0 * jnp.dot(adapter_query_delta, up_columns[0], preferred_element_type=jnp.float32)
    ).astype(jnp.bfloat16)
    key_rows = jnp.dot(
        normalized_rows, query_key_value_weight[1], preferred_element_type=jnp.float32
    ).astype(jnp.bfloat16)
    value_token_rows = (
        jnp.dot(normalized_rows, query_key_value_weight[2], preferred_element_type=jnp.float32)
        + 8.0 * jnp.dot(adapter_value_delta, up_columns[1], preferred_element_type=jnp.float32)
    ).astype(jnp.bfloat16)
    limits = jnp.repeat(lengths, head_count)
    query_heads = head_major(query_rows, seq_rows, head_count)
    key_heads = head_major(key_rows, seq_rows, head_count)
    value_heads = head_major(value_token_rows, seq_rows, head_count)
    head_out, log_sums = lax.map(attend_forward, (query_heads, key_heads, value_heads, limits))
    attended = token_major(head_out, seq_rows, head_count).astype(jnp.bfloat16)
    attn_share = (
        lax.psum_scatter(
            jnp.dot(attended, attention_output_weight, preferred_element_type=jnp.float32),
            "mp",
            scatter_dimension=0,
            tiled=True,
        )
        + attention_output_bias
    )

    def norm_two(values):
        return layer_norm(values, second_norm_gain, second_norm_bias)

    def norm_one(values):
        return layer_norm(values, first_norm_gain, first_norm_bias)

    attn_full = lax.all_gather(attn_share, "mp", axis=0, tiled=True)
    residual = tokens_f32 + attn_full
    normed_two = norm_two(residual).astype(jnp.bfloat16)
    hidden_pre = (
        jnp.dot(normed_two, feedforward_up_weight, preferred_element_type=jnp.float32)
        + feedforward_up_bias
    )
    hidden = gelu_tanh(hidden_pre).astype(jnp.bfloat16)
    mlp_share = (
        lax.psum_scatter(
            jnp.dot(hidden, feedforward_down_weight, preferred_element_type=jnp.float32).astype(
                jnp.bfloat16
            ),
            "mp",
            scatter_dimension=0,
            tiled=True,
        ).astype(jnp.float32)
        + feedforward_down_bias
    )
    mlp_full = lax.all_gather(mlp_share.astype(jnp.bfloat16), "mp", axis=0, tiled=True).astype(
        mlp_share.dtype
    )
    block_out = (residual + mlp_full).astype(jnp.bfloat16)
    live_mask = (jnp.arange(seq_len_all)[None, :] < lengths[:, None]).reshape(tok_count, 1)
    grad_out = jnp.where(
        live_mask, cotangent.reshape(tok_count, model_width), jnp.zeros((), jnp.bfloat16)
    )
    grad_hidden = jnp.einsum(
        "td,fd->tf", grad_out, feedforward_down_weight, preferred_element_type=jnp.float32
    )
    _, gelu_back = jax.vjp(gelu_tanh, hidden_pre)
    grad_pre = gelu_back(grad_hidden)[0].astype(jnp.bfloat16)
    grad_norm2_share = lax.psum_scatter(
        jnp.einsum(
            "tf,df->td", grad_pre, feedforward_up_weight, preferred_element_type=jnp.float32
        ),
        "mp",
        scatter_dimension=0,
        tiled=True,
    )
    grad_norm2 = lax.all_gather(grad_norm2_share, "mp", axis=0, tiled=True)
    _, norm2_back = jax.vjp(norm_two, residual)
    grad_resid = grad_out.astype(jnp.float32) + norm2_back(grad_norm2)[0]
    grad_resid_low = grad_resid.astype(jnp.bfloat16)
    grad_attended = jnp.einsum(
        "td,ed->te", grad_resid_low, attention_output_weight, preferred_element_type=jnp.float32
    ).astype(jnp.bfloat16)
    grad_head = head_major(grad_attended, seq_rows, head_count)
    head_dq, head_dk, head_dv = lax.map(
        attend_backward, (query_heads, key_heads, value_heads, limits, grad_head, log_sums)
    )
    query_gradient_rows = token_major(head_dq, seq_rows, head_count).astype(jnp.bfloat16)
    grad_keys = token_major(head_dk, seq_rows, head_count).astype(jnp.bfloat16)
    value_gradient_rows = token_major(head_dv, seq_rows, head_count).astype(jnp.bfloat16)
    adapter_query_gradient = 8.0 * jnp.einsum(
        "te,re->tr", query_gradient_rows, up_columns[0], preferred_element_type=jnp.float32
    )
    adapter_value_gradient = 8.0 * jnp.einsum(
        "te,re->tr", value_gradient_rows, up_columns[1], preferred_element_type=jnp.float32
    )
    adapter_gradient = jnp.concatenate((adapter_query_gradient, adapter_value_gradient), axis=1)
    down_pair_float32 = down_pair.astype(jnp.float32)
    partial_sum = jnp.einsum(
        "te,de->td",
        query_gradient_rows,
        query_key_value_weight[0],
        preferred_element_type=jnp.float32,
    )
    partial_sum = partial_sum + jnp.einsum(
        "te,de->td", grad_keys, query_key_value_weight[1], preferred_element_type=jnp.float32
    )
    partial_sum = partial_sum + jnp.einsum(
        "te,de->td",
        value_gradient_rows,
        query_key_value_weight[2],
        preferred_element_type=jnp.float32,
    )
    grad_norm1_share = lax.psum_scatter(
        partial_sum
        + jnp.einsum(
            "gy,wy->gw", adapter_gradient, down_pair_float32, precision=lax.Precision.HIGHEST
        ),
        "mp",
        scatter_dimension=0,
        tiled=True,
    )
    grad_down_both = jnp.einsum(
        "fi,fg->ig",
        normalized_rows.astype(jnp.float32),
        adapter_gradient,
        precision=lax.Precision.HIGHEST,
    )
    grad_down = jnp.stack(
        (grad_down_both[:, :adapter_rank_size], grad_down_both[:, adapter_rank_size:])
    )
    grad_up_query = 8.0 * jnp.einsum(
        "zm,zj->mj", adapter_query_delta, query_gradient_rows, preferred_element_type=jnp.float32
    )
    grad_up_value = 8.0 * jnp.einsum(
        "zm,zj->mj", adapter_value_delta, value_gradient_rows, preferred_element_type=jnp.float32
    )
    up_column_gradient = jnp.stack((grad_up_query, grad_up_value))
    grad_up = lax.dynamic_update_slice_in_dim(
        jnp.zeros(adapter_up_factor.shape, jnp.float32),
        up_column_gradient,
        worker_shard * shard_width,
        2,
    )
    live_local = jnp.sum(lengths).astype(jnp.float32)
    down_reduced_sum, up_reduced_sum, live_sum = lax.psum(
        (grad_down, grad_up, live_local), ("dp", "mp")
    )
    active_token_total = live_sum / groups
    grad_norm1 = lax.all_gather(grad_norm1_share, "mp", axis=0, tiled=True)
    _, norm1_back = jax.vjp(norm_one, tokens_f32)
    input_grad = (grad_resid + norm1_back(grad_norm1)[0]).astype(jnp.bfloat16)
    down_factor_next, down_first_moment_next, down_second_moment_next = adam_decay_update(
        adapter_down_factor,
        down_reduced_sum / active_token_total,
        down_first_moment,
        down_second_moment,
    )
    up_factor_next, up_first_moment_next, up_second_moment_next = adam_decay_update(
        adapter_up_factor, up_reduced_sum / active_token_total, up_first_moment, up_second_moment
    )
    return (
        block_out.reshape(seq_rows, seq_len_all, model_width),
        input_grad.reshape(seq_rows, seq_len_all, model_width),
        down_factor_next,
        up_factor_next,
        down_first_moment_next,
        up_first_moment_next,
        down_second_moment_next,
        up_second_moment_next,
    )


TILE = 256
NT = (((1,), (1,)), ((), ()))


def head_lanes(half):
    lane = lax.broadcasted_iota(jnp.int32, (1, 2 * HEAD), 1)
    return (lane >= half * HEAD) & (lane < (half + 1) * HEAD)


def one_head(block, half):
    return jnp.where(head_lanes(half), block, jnp.zeros((), block.dtype))


def edge_allowed(key_start, query_start, seq_len):
    key_at = key_start + lax.broadcasted_iota(jnp.int32, (TILE, TILE), 0)
    query_at = query_start + lax.broadcasted_iota(jnp.int32, (TILE, TILE), 1)
    return (key_at <= query_at) & (key_at < seq_len)


def attention_forward_kernel(lens_ref, q_ref, k_ref, v_ref, out_ref, lse_ref, vt_ref):
    seq_len = lens_ref[pl.program_id(0)]
    live_tiles = (seq_len + TILE - 1) // TILE
    vt_ref[...] = v_ref[0].T
    tiles = q_ref.shape[1] // TILE

    def row_tile(tile, extent):
        rows = pl.ds(tile * TILE, TILE)
        inner = (extent - 1) * TILE
        query = q_ref[0, rows, :] * HEAD ** (-0.5)
        allowed = edge_allowed(inner, tile * TILE, seq_len)
        outs = []
        for half in range(2):
            mine = one_head(query, half)
            edge = lax.dot_general(
                k_ref[0, pl.ds(inner, TILE), :], mine, NT, preferred_element_type=jnp.float32
            )
            edge = jnp.where(allowed, edge, -1e30)
            top = jnp.max(edge, axis=0, keepdims=True)
            if inner:
                past = lax.dot_general(
                    k_ref[0, pl.ds(0, inner), :], mine, NT, preferred_element_type=jnp.float32
                )
                top = jnp.maximum(top, jnp.max(past, axis=0, keepdims=True))
            head_rows = pl.ds(half * HEAD, HEAD)
            edge = jnp.exp(edge - top)
            total = jnp.sum(edge, axis=0, keepdims=True)
            out = jnp.dot(
                vt_ref[head_rows, pl.ds(inner, TILE)],
                edge.astype(jnp.bfloat16),
                preferred_element_type=jnp.float32,
            )
            if inner:
                past = jnp.exp(past - top)
                total = total + jnp.sum(past, axis=0, keepdims=True)
                out = out + jnp.dot(
                    vt_ref[head_rows, pl.ds(0, inner)],
                    past.astype(jnp.bfloat16),
                    preferred_element_type=jnp.float32,
                )
            outs.append(out / total)
            lse_ref[0, 0, pl.ds(half, 1), rows] = top + jnp.log(total)
        out_ref[0, rows, :] = jnp.concatenate(outs, axis=0).T.astype(out_ref.dtype)

    for tile in range(tiles):
        for extent in range(1, tile + 2):
            pl.when(jnp.minimum(live_tiles, tile + 1) == extent)(
                lambda tile=tile, extent=extent: row_tile(tile, extent)
            )


def attention_forward(lens, query, key, value):
    seqs, length, width = query.shape
    pairs = width // (2 * HEAD)
    spec = pl.BlockSpec((1, length, 2 * HEAD), lambda s, h, lens: (s, 0, h))
    return pl.pallas_call(
        attention_forward_kernel,
        grid_spec=pltpu.PrefetchScalarGridSpec(
            num_scalar_prefetch=1,
            grid=(seqs, pairs),
            in_specs=[spec] * 3,
            out_specs=[spec, pl.BlockSpec((1, 1, 2, length), lambda s, h, lens: (s, h, 0, 0))],
            scratch_shapes=[pltpu.VMEM((2 * HEAD, length), jnp.bfloat16)],
        ),
        out_shape=[
            jax.ShapeDtypeStruct(query.shape, jnp.bfloat16),
            jax.ShapeDtypeStruct((seqs, pairs, 2, length), jnp.float32),
        ],
        cost_estimate=pl.CostEstimate(
            flops=seqs * width * length * length * 3,
            bytes_accessed=seqs * width * length * 8,
            transcendentals=seqs * pairs * length * length,
        ),
        name="attention_forward",
    )(lens, query, key, value)


def attention_backward_kernel(
    lens_ref, q_ref, k_ref, v_ref, g_ref, lse_ref, dq_ref, dk_ref, dv_ref, kt_ref, dk_acc, dv_acc
):
    seq_len = lens_ref[pl.program_id(0)]
    kt_ref[...] = k_ref[0].T
    dk_acc[...] = jnp.zeros_like(dk_acc)
    dv_acc[...] = jnp.zeros_like(dv_acc)
    tiles = q_ref.shape[1] // TILE

    def row_tile(tile):
        rows = pl.ds(tile * TILE, TILE)
        inner = tile * TILE
        query = q_ref[0, rows, :] * HEAD ** (-0.5)
        grad = g_ref[rows, :]
        allowed = edge_allowed(inner, inner, seq_len)
        spans = [(inner, TILE)] + ([(0, inner)] if inner else [])
        outs = []
        for half in range(2):
            mine = one_head(query, half)
            mine_grad = one_head(grad, half)
            lse = lse_ref[0, 0, pl.ds(half, 1), rows]
            probs, grad_probs, row_dot = [], [], 0.0
            for at, (start, size) in enumerate(spans):
                keys = pl.ds(start, size)
                scores = lax.dot_general(
                    k_ref[0, keys, :], mine, NT, preferred_element_type=jnp.float32
                )
                if at == 0:
                    scores = jnp.where(allowed, scores, -1e30)
                prob = jnp.exp(scores - lse)
                dv_acc[keys, :] += jnp.dot(
                    prob.astype(jnp.bfloat16), mine_grad, preferred_element_type=jnp.float32
                )
                grad_prob = lax.dot_general(
                    v_ref[0, keys, :], mine_grad, NT, preferred_element_type=jnp.float32
                )
                row_dot = row_dot + jnp.sum(prob * grad_prob, axis=0, keepdims=True)
                probs.append(prob)
                grad_probs.append(grad_prob)
            out = 0.0
            for (start, size), prob, grad_prob in zip(spans, probs, grad_probs):
                keys = pl.ds(start, size)
                grad_scores = (prob * (grad_prob - row_dot)).astype(jnp.bfloat16)
                dk_acc[keys, :] += jnp.dot(grad_scores, mine, preferred_element_type=jnp.float32)
                out = out + jnp.dot(
                    kt_ref[pl.ds(half * HEAD, HEAD), keys],
                    grad_scores,
                    preferred_element_type=jnp.float32,
                )
            outs.append(out)
        dq = jnp.concatenate(outs, axis=0).T * HEAD ** (-0.5)
        dq_ref[0, rows, :] = dq.astype(dq_ref.dtype)

    for tile in range(tiles):
        pl.when(tile * TILE < seq_len)(lambda tile=tile: row_tile(tile))

        @pl.when(tile * TILE >= seq_len)
        def _(tile=tile):
            dq_ref[0, pl.ds(tile * TILE, TILE), :] = jnp.zeros((TILE, 2 * HEAD), dq_ref.dtype)

    dk_ref[0] = dk_acc[...].astype(dk_ref.dtype)
    dv_ref[0] = dv_acc[...].astype(dv_ref.dtype)


def attention_backward(lens, query, key, value, grad, lse, start):
    length, width = query.shape[1:]
    seqs = lens.shape[0]
    pairs = width // (2 * HEAD)

    def block(first):
        return pl.BlockSpec((1, length, 2 * HEAD), lambda s, h, lens: (s + first, 0, h))

    return pl.pallas_call(
        attention_backward_kernel,
        grid_spec=pltpu.PrefetchScalarGridSpec(
            num_scalar_prefetch=1,
            grid=(seqs, pairs),
            in_specs=[block(start)] * 3
            + [
                pl.BlockSpec((length, 2 * HEAD), lambda s, h, lens: (s, h)),
                pl.BlockSpec((1, 1, 2, length), lambda s, h, lens: (s + start, h, 0, 0)),
            ],
            out_specs=[block(0)] * 3,
            scratch_shapes=[
                pltpu.VMEM((2 * HEAD, length), jnp.bfloat16),
                pltpu.VMEM((length, 2 * HEAD), jnp.float32),
                pltpu.VMEM((length, 2 * HEAD), jnp.float32),
            ],
        ),
        out_shape=[jax.ShapeDtypeStruct((seqs, length, width), jnp.bfloat16)] * 3,
        cost_estimate=pl.CostEstimate(
            flops=seqs * width * length * length * 7,
            bytes_accessed=seqs * width * length * 14,
            transcendentals=seqs * pairs * length * length,
        ),
        name="attention_backward",
    )(lens, query, key, value, grad, lse)


MID_ROWS = 256
CHUNK = 1024


def centred(values):
    centre = values - jnp.mean(values, axis=-1, keepdims=True)
    inverse = lax.rsqrt(jnp.mean(centre * centre, axis=-1, keepdims=True) + 1e-05)
    return centre * inverse, inverse


def norm_backward(grad, gain, normal, inverse):
    grad = grad * gain
    mean = jnp.mean(grad, axis=-1, keepdims=True)
    along = jnp.mean(grad * normal, axis=-1, keepdims=True)
    return (grad - mean - normal * along) * inverse


def dot(a, b):
    return jnp.dot(a, b, preferred_element_type=jnp.float32)


def dot_t(a, b):
    return lax.dot_general(a, b, NT, preferred_element_type=jnp.float32)


def copies_of(pairs, sems):
    return [pltpu.make_async_copy(a, b, sems.at[i]) for i, (a, b) in enumerate(pairs)]


def middle_kernel(
    table_ref,
    tokens_ref,
    cotangent_ref,
    attended_own,
    attended_far,
    out_bias_ref,
    gain_ref,
    shift_ref,
    up_bias_ref,
    down_bias_ref,
    out_own,
    out_near,
    out_far,
    up_own,
    up_near,
    up_far,
    down_own,
    down_near,
    down_far,
    block_ref,
    resid_grad_ref,
    own_grad_ref,
    far_grad_ref,
    out_w,
    up_w,
    down_w,
    residual_ref,
    normed_ref,
    normal_ref,
    acc_ref,
    grad_acc_ref,
    sems,
):
    step = pl.program_id(0)

    pairs = []
    start = 0
    for piece in (out_own, out_near, out_far):
        rows = piece.shape[0]
        pairs.append((piece, out_w.at[pl.ds(start, rows), :]))
        start += rows
    chunk = 0
    for up, down in ((up_own, down_own), (up_near, down_near), (up_far, down_far)):
        for at in range(up.shape[1] // CHUNK):
            units = pl.ds(at * CHUNK, CHUNK)
            pairs.append((up.at[:, units], up_w.at[chunk]))
            pairs.append((down.at[units, :], down_w.at[chunk]))
            chunk += 1
    loads = copies_of(pairs, sems)

    @pl.when(step == 0)
    def _():
        for load in loads:
            load.start()
        for load in loads[:3]:
            load.wait()

    live = table_ref[2, step]
    residual = tokens_ref[...].astype(jnp.float32) + (
        dot(jnp.concatenate((attended_own[...], attended_far[...]), axis=1), out_w[...])
        + out_bias_ref[...]
    )
    residual_ref[...] = residual
    normal, inverse = centred(residual)
    normal_ref[...] = normal
    normed_ref[...] = (normal * gain_ref[...] + shift_ref[...]).astype(jnp.bfloat16)
    acc_ref[...] = jnp.zeros_like(acc_ref)

    @pl.when(step == 0)
    def _():
        for load in loads[3:]:
            load.wait()

    scale = 0.7978845608028654
    cube = 0.044715 * scale

    def forward_only(chunk, carry):
        pre = dot(normed_ref[...], up_w[chunk]) + up_bias_ref[chunk]
        tanh = jnp.tanh(pre * (scale + cube * (pre * pre)))
        hidden = (pre * (0.5 + 0.5 * tanh)).astype(jnp.bfloat16)
        acc_ref[...] += dot(hidden, down_w[chunk])
        return carry

    def finish():
        block_ref[...] = (residual_ref[...] + acc_ref[...] + down_bias_ref[...]).astype(
            block_ref.dtype
        )

    @pl.when(live > 0)
    def _():
        row = lax.broadcasted_iota(jnp.int32, (MID_ROWS, 1), 0)
        grad_out = jnp.where(row < live, cotangent_ref[...], jnp.zeros((), jnp.bfloat16))
        grad_acc_ref[...] = jnp.zeros_like(grad_acc_ref)

        def both_ways(chunk, carry):
            pre = dot(normed_ref[...], up_w[chunk]) + up_bias_ref[chunk]
            grad_hidden = dot_t(grad_out, down_w[chunk])
            square = pre * pre
            tanh = jnp.tanh(pre * (scale + cube * square))
            gate = 0.5 + 0.5 * tanh
            hidden = (pre * gate).astype(jnp.bfloat16)
            slope = gate + (pre * (0.5 - 0.5 * (tanh * tanh))) * (scale + 3.0 * cube * square)
            grad_pre = (grad_hidden * slope).astype(jnp.bfloat16)
            acc_ref[...] += dot(hidden, down_w[chunk])
            grad_acc_ref[...] += dot_t(grad_pre, up_w[chunk])
            return carry

        lax.fori_loop(0, up_w.shape[0], both_ways, 0, unroll=UNROLL)
        finish()
        grad_resid = grad_out.astype(jnp.float32) + norm_backward(
            grad_acc_ref[...], gain_ref[...], normal_ref[...], inverse
        )
        low = grad_resid.astype(jnp.bfloat16)
        resid_grad_ref[...] = low
        columns = own_grad_ref.shape[1]
        own_grad_ref[...] = dot_t(low, out_w[:columns]).astype(jnp.bfloat16)
        far_grad_ref[...] = dot_t(low, out_w[columns:]).astype(jnp.bfloat16)

    @pl.when(live <= 0)
    def _():
        lax.fori_loop(0, up_w.shape[0], forward_only, 0, unroll=UNROLL)
        finish()
        resid_grad_ref[...] = jnp.zeros_like(resid_grad_ref)
        own_grad_ref[...] = jnp.zeros_like(own_grad_ref)
        far_grad_ref[...] = jnp.zeros_like(far_grad_ref)


UNROLL = 2


def middle(
    table, tokens, cotangent, own, far, out_bias, gain, shift, up_bias, down_bias, weights
):
    rows, width = table.shape[1] * MID_ROWS, tokens.shape[1]
    columns = far.shape[1]
    units = up_bias.shape[0] * up_bias.shape[2]
    tile = pl.BlockSpec((MID_ROWS, width), lambda i, t: (i, 0))
    picked = pl.BlockSpec((MID_ROWS, width), lambda i, t: (t[0, i], 0))
    part = pl.BlockSpec((MID_ROWS, columns), lambda i, t: (i, 0))
    vector = pl.BlockSpec((1, width), lambda i, t: (0, 0))
    chunks = units // CHUNK
    low = jax.ShapeDtypeStruct((rows, width), jnp.bfloat16)
    thin = jax.ShapeDtypeStruct((rows, columns), jnp.bfloat16)
    wide = pltpu.VMEM((MID_ROWS, width), jnp.float32)
    return pl.pallas_call(
        middle_kernel,
        grid_spec=pltpu.PrefetchScalarGridSpec(
            num_scalar_prefetch=1,
            grid=(rows // MID_ROWS,),
            in_specs=[picked] * 2
            + [pl.BlockSpec((MID_ROWS, columns), lambda i, t, a=a: (t[a, i], 0)) for a in (1, 3)]
            + [vector] * 3
            + [pl.BlockSpec(up_bias.shape, lambda i, t: (0, 0, 0)), vector]
            + [pl.BlockSpec(memory_space=pl.ANY)] * 9,
            out_specs=[tile, tile, part, part],
            scratch_shapes=[
                pltpu.VMEM((width, width), jnp.bfloat16),
                pltpu.VMEM((chunks, width, CHUNK), jnp.bfloat16),
                pltpu.VMEM((chunks, CHUNK, width), jnp.bfloat16),
                wide,
                pltpu.VMEM((MID_ROWS, width), jnp.bfloat16),
                wide,
                wide,
                wide,
                pltpu.SemaphoreType.DMA((3 + 2 * chunks,)),
            ],
        ),
        out_shape=[low, low, thin, thin],
        compiler_params=pltpu.CompilerParams(vmem_limit_bytes=56 << 20),
        cost_estimate=pl.CostEstimate(
            flops=rows * width * (units * 8 + width * 4),
            bytes_accessed=rows * width * 12 + units * width * 4,
            transcendentals=rows * units,
        ),
        name="middle",
    )(
        table,
        tokens,
        cotangent,
        own,
        far,
        out_bias,
        gain,
        shift,
        up_bias,
        down_bias,
        *weights,
    )


PROJECT_ROWS = 256


def qkv_loads(own, near, far, weight_ref, sems):
    pairs = []
    start = 0
    for piece in (own, near, far):
        if piece is not None:
            columns = pl.ds(start, piece.shape[2])
            pairs.append((piece, weight_ref.at[:, :, columns]))
            start += piece.shape[2]
    return copies_of(pairs, sems)


def project_kernel(pieces, table_ref, *refs):
    tokens_ref, gain_ref, shift_ref, down_ref, up_ref = refs[:5]
    weights = list(refs[5 : 5 + pieces]) + [None] * (3 - pieces)
    query_ref, key_ref, value_ref, low_ref, weight_ref, sems = refs[5 + pieces :]
    loads = qkv_loads(*weights, weight_ref, sems)
    first = pl.program_id(0) == 0

    @pl.when(first)
    def _():
        for load in loads:
            load.start()

    normal, _ = centred(tokens_ref[...].astype(jnp.float32))
    normed = (normal * gain_ref[...] + shift_ref[...]).astype(jnp.bfloat16)
    low = dot_t(normed, down_ref[...]).astype(jnp.bfloat16)
    low_ref[...] = low.astype(jnp.float32).T

    @pl.when(first)
    def _():
        for load in loads:
            load.wait()

    query_ref[...] = (dot(normed, weight_ref[0]) + 8.0 * dot(low, up_ref[0])).astype(jnp.bfloat16)
    key_ref[...] = dot(normed, weight_ref[1]).astype(jnp.bfloat16)
    value_ref[...] = (dot(normed, weight_ref[2]) + 8.0 * dot(low, up_ref[1])).astype(jnp.bfloat16)


def project(table, tokens, gain, shift, down, up, *weights):
    rows, width = table.shape[0] * PROJECT_ROWS, tokens.shape[1]
    columns = up.shape[2]
    pairs = down.shape[0]
    out = pl.BlockSpec((PROJECT_ROWS, columns), lambda i, t: (i, 0))
    vector = pl.BlockSpec((1, width), lambda i, t: (0, 0))
    return pl.pallas_call(
        functools.partial(project_kernel, len(weights)),
        grid_spec=pltpu.PrefetchScalarGridSpec(
            num_scalar_prefetch=1,
            grid=(rows // PROJECT_ROWS,),
            in_specs=[
                pl.BlockSpec((PROJECT_ROWS, width), lambda i, t: (t[i], 0)),
                vector,
                vector,
                pl.BlockSpec(down.shape, lambda i, t: (0, 0)),
                pl.BlockSpec(up.shape, lambda i, t: (0, 0, 0)),
            ]
            + [pl.BlockSpec(memory_space=pl.ANY)] * len(weights),
            out_specs=[out] * 3 + [pl.BlockSpec((pairs, PROJECT_ROWS), lambda i, t: (0, i))],
            scratch_shapes=[
                pltpu.VMEM((3, width, columns), jnp.bfloat16),
                pltpu.SemaphoreType.DMA((len(weights),)),
            ],
        ),
        out_shape=[jax.ShapeDtypeStruct((rows, columns), jnp.bfloat16)] * 3
        + [jax.ShapeDtypeStruct((pairs, rows), jnp.float32)],
        cost_estimate=pl.CostEstimate(
            flops=rows * width * columns * 6,
            bytes_accessed=rows * (width + 3 * columns) * 2 + 6 * width * columns,
            transcendentals=rows,
        ),
        name="project",
    )(table, tokens, gain, shift, down, up, *weights)


def first_backward_kernel(
    table_ref,
    tokens_ref,
    resid_grad_ref,
    low_ref,
    query_own,
    key_own,
    value_own,
    query_far,
    key_far,
    value_far,
    gain_ref,
    shift_ref,
    down_ref,
    up_ref,
    own_ref,
    near_ref,
    far_ref,
    input_ref,
    down_grad_ref,
    query_up_ref,
    value_up_ref,
    weight_ref,
    sems,
):
    first = pl.program_id(0) == 0
    loads = qkv_loads(own_ref, near_ref, far_ref, weight_ref, sems)

    @pl.when(first)
    def _():
        for load in loads:
            load.start()
        down_grad_ref[...] = jnp.zeros_like(down_grad_ref)
        query_up_ref[...] = jnp.zeros_like(query_up_ref)
        value_up_ref[...] = jnp.zeros_like(value_up_ref)

    normal, inverse = centred(tokens_ref[...].astype(jnp.float32))
    normed = (normal * gain_ref[...] + shift_ref[...]).astype(jnp.bfloat16)
    query = jnp.concatenate((query_own[...], query_far[...]), axis=1)
    key = jnp.concatenate((key_own[...], key_far[...]), axis=1)
    value = jnp.concatenate((value_own[...], value_far[...]), axis=1)
    adapter = 8.0 * (dot_t(query, up_ref[0]) + dot_t(value, up_ref[1]))
    high = adapter.astype(jnp.bfloat16)
    rest = (adapter - high.astype(jnp.float32)).astype(jnp.bfloat16)
    down_grad_ref[...] += dot(high.astype(jnp.float32).T.astype(jnp.bfloat16), normed) + dot(
        rest.astype(jnp.float32).T.astype(jnp.bfloat16), normed
    )
    low = low_ref[...].astype(jnp.bfloat16)
    query_up_ref[...] += dot(low, query)
    value_up_ref[...] += dot(low, value)

    @pl.when(first)
    def _():
        for load in loads:
            load.wait()

    grad = (
        dot_t(query, weight_ref[0])
        + dot_t(key, weight_ref[1])
        + dot_t(value, weight_ref[2])
        + dot(high, down_ref[...])
        + dot(rest, down_ref[...])
    )
    input_ref[...] = (
        resid_grad_ref[...].astype(jnp.float32)
        + norm_backward(grad, gain_ref[...], normal, inverse)
    ).astype(input_ref.dtype)


def first_backward(
    table, tokens, resid_grad, low, own, far, gain, shift, down, up, weights
):
    tiles = table.shape[1]
    rows, width = tiles * PROJECT_ROWS, tokens.shape[1]
    pairs = down.shape[0]
    columns = own[0].shape[1]
    tile = pl.BlockSpec((PROJECT_ROWS, width), lambda i, t: (t[0, i], 0))
    vector = pl.BlockSpec((1, width), lambda i, t: (0, 0))
    small = pl.BlockSpec((pairs, width), lambda i, t: (0, 0))
    sums = jax.ShapeDtypeStruct((pairs, width), jnp.float32)
    return pl.pallas_call(
        first_backward_kernel,
        grid_spec=pltpu.PrefetchScalarGridSpec(
            num_scalar_prefetch=1,
            grid=(tiles,),
            in_specs=[
                tile,
                pl.BlockSpec((PROJECT_ROWS, width), lambda i, t: (t[1, i], 0)),
                pl.BlockSpec((pairs, PROJECT_ROWS), lambda i, t: (0, t[2, i])),
            ]
            + [pl.BlockSpec((PROJECT_ROWS, columns), lambda i, t: (t[3, i], 0))] * 3
            + [pl.BlockSpec((PROJECT_ROWS, columns), lambda i, t: (i, 0))] * 3
            + [vector, vector, small, pl.BlockSpec(up.shape, lambda i, t: (0, 0, 0))]
            + [pl.BlockSpec(memory_space=pl.ANY)] * 3,
            out_specs=[pl.BlockSpec((PROJECT_ROWS, width), lambda i, t: (i, 0))] + [small] * 3,
            scratch_shapes=[
                pltpu.VMEM((3, width, width), jnp.bfloat16),
                pltpu.SemaphoreType.DMA((3,)),
            ],
        ),
        out_shape=[jax.ShapeDtypeStruct((rows, width), jnp.bfloat16)] + [sums] * 3,
        cost_estimate=pl.CostEstimate(
            flops=rows * width * width * 7,
            bytes_accessed=rows * width * 12 + 6 * width * width,
            transcendentals=rows,
        ),
        name="first_backward",
    )(table, tokens, resid_grad, low, *own, *far, gain, shift, down, up, *weights)


def swap(value):
    return lax.ppermute(value, "mp", [(0, 1), (1, 0)])


def after(value, *earlier):
    return lax.optimization_barrier((value, *earlier))[0]


def core_swap(value):
    return lax.ppermute(value, "dp", [(i, i ^ 1) for i in range(lax.axis_size("dp"))])


def core_half(shard, axis):
    size = shard.shape[axis] // 2
    core = lax.rem(lax.axis_index("dp"), 2)
    return lax.dynamic_slice_in_dim(shard, core * size, size, axis)


def core_order(value, axis):
    size = value.shape[axis] // 2
    core = lax.rem(lax.axis_index("dp"), 2)
    low = lax.slice_in_dim(value, 0, size, axis=axis)
    high = lax.slice_in_dim(value, size, 2 * size, axis=axis)
    return jnp.where(
        core == 0, value, jnp.concatenate((high, low), axis=axis)
    )


def sum_all(value):
    count = lax.axis_size("dp")
    if count & (count - 1):
        return lax.psum(value, ("dp", "mp"))
    bit = 1
    while bit < count:
        value = value + lax.ppermute(value, "dp", [(i, i ^ bit) for i in range(count)])
        bit *= 2
    return value + swap(value)


def per_device_pair(
    tokens,
    cotangent,
    lengths,
    first_norm_gain,
    first_norm_bias,
    query_key_value_weight,
    attention_output_weight,
    attention_output_bias,
    second_norm_gain,
    second_norm_bias,
    feedforward_up_weight,
    feedforward_up_bias,
    feedforward_down_weight,
    feedforward_down_bias,
    adapter_down_factor,
    adapter_up_factor,
    down_first_moment,
    up_first_moment,
    down_second_moment,
    up_second_moment,
):
    f32, bf16 = jnp.float32, jnp.bfloat16
    seqs, length, width = tokens.shape
    rank = adapter_down_factor.shape[2]
    me = lax.axis_index("mp")
    columns = query_key_value_weight.shape[2]
    whole, half = 2, length // 2
    tiles, half_tiles = length // MID_ROWS, half // MID_ROWS

    def row(vector):
        return vector.reshape(1, -1)

    qkv_near = swap(core_half(query_key_value_weight, 2))
    up_bias = jnp.concatenate(
        (feedforward_up_bias, core_order(swap(feedforward_up_bias), 0))
    ).reshape(-1, 1, CHUNK)

    down_low = adapter_down_factor.astype(bf16).transpose(0, 2, 1).reshape(2 * rank, width)
    up_low = adapter_up_factor.astype(bf16)
    blank = jnp.zeros_like(up_low[0])
    up_low = jnp.stack(
        (jnp.concatenate((up_low[0], blank)), jnp.concatenate((blank, up_low[1])))
    )
    up_own = lax.dynamic_slice_in_dim(up_low, me * columns, columns, 2)
    up_other = core_order(
        lax.dynamic_slice_in_dim(up_low, (1 - me) * columns, columns, 2), 2
    )
    up_both = jnp.concatenate((up_own, up_other), axis=2)

    places = jnp.arange(seqs, dtype=jnp.int32)
    longer = (lengths[None, :] > lengths[:, None]) | (
        (lengths[None, :] == lengths[:, None]) & (places[None, :] < places[:, None])
    )
    standing = jnp.sum(longer.astype(jnp.int32), axis=1)
    order = jnp.sum(jnp.where(standing[None, :] == places[:, None], places[None, :], 0), axis=1)
    split = order[0]

    mine = jnp.stack((jnp.where(me == 0, order[1], order[2]), jnp.where(me == 0, order[4], order[3])))
    theirs = jnp.stack(
        (jnp.where(me == 0, order[2], order[1]), jnp.where(me == 0, order[3], order[4]))
    )

    def lens_of(index):
        return jnp.sum(jnp.where(places[None, :] == index[:, None], lengths[None, :], 0), axis=1)

    own_lens = lens_of(mine)
    split_lens = lens_of(split[None])
    three_lens = jnp.concatenate((own_lens, split_lens))
    flat_tokens = tokens.reshape(-1, width)
    flat_cotangent = cotangent.reshape(-1, width)
    step = jnp.arange(whole * tiles, dtype=jnp.int32)
    extra = jnp.arange(half_tiles, dtype=jnp.int32) + me * half_tiles
    whole_table = mine[step // tiles] * tiles + step % tiles
    token_table = jnp.concatenate((whole_table, split * tiles + extra))
    own_table = jnp.concatenate((step, whole * tiles + extra))
    live_table = jnp.concatenate(
        (
            own_lens[step // tiles] - (step % tiles) * MID_ROWS,
            split_lens[0] - extra * MID_ROWS,
        )
    )
    three_table = jnp.concatenate(
        (whole_table, split * tiles + jnp.arange(tiles, dtype=jnp.int32))
    )
    gain_one, shift_one = row(first_norm_gain), row(first_norm_bias)

    def sequences(pieces):
        return [piece.reshape(-1, length, columns) for piece in pieces]

    *own_heads, low = project(
        three_table,
        flat_tokens,
        gain_one,
        shift_one,
        down_low,
        up_own,
        query_key_value_weight,
    )
    own_heads = sequences(own_heads)
    qkv_near = after(qkv_near, own_heads[0])
    qkv_far = core_swap(qkv_near)
    out_near = swap(after(core_half(attention_output_weight, 0), qkv_near))
    up_near = swap(after(core_half(feedforward_up_weight, 1), qkv_near))
    attended_own, lse_own = attention_forward(three_lens, *own_heads)
    sent = lax.dynamic_slice_in_dim(attended_own[whole], (1 - me) * half, half, 0)
    attended_got = swap(core_order(sent, 1))
    down_near = swap(after(core_half(feedforward_down_weight, 0), attended_own))
    qkv_far = after(qkv_far, attended_own)
    qkv = (query_key_value_weight, qkv_near, qkv_far)
    *far_heads, _ = project(
        whole_table,
        flat_tokens,
        gain_one,
        shift_one,
        down_low,
        up_other,
        qkv_near,
        qkv_far,
    )
    far_heads = sequences(far_heads)
    out_far = core_swap(after(out_near, far_heads[0]))
    up_far = core_swap(after(up_near, far_heads[0]))
    attended_far, lse_far = attention_forward(own_lens, *far_heads)
    down_far = core_swap(after(down_near, attended_far))
    far_all = jnp.concatenate((attended_far.reshape(-1, columns), attended_got), axis=0)
    weights = (
        attention_output_weight,
        out_near,
        out_far,
        feedforward_up_weight,
        up_near,
        up_far,
        feedforward_down_weight,
        down_near,
        down_far,
    )
    middle_table = jnp.stack(
        (token_table, own_table, live_table, jnp.arange(token_table.shape[0], dtype=jnp.int32))
    )

    def run_middle(first, last):
        return middle(
            middle_table[:, first:last],
            flat_tokens,
            flat_cotangent,
            attended_own.reshape(-1, columns),
            far_all,
            row(attention_output_bias),
            row(second_norm_gain),
            row(second_norm_bias),
            up_bias,
            row(feedforward_down_bias),
            weights,
        )

    block_zero, resid_zero, *grads_zero = run_middle(0, tiles)
    block_zero_got = swap(block_zero)
    block_rest, resid_rest, *grads_rest = run_middle(tiles, token_table.shape[0])
    grad_got = swap(core_order(grads_rest[1][length:], 1))
    block_rest_got = swap(block_rest)
    grad_kept = grads_rest[0][length:]
    grad_split = jnp.concatenate(
        (jnp.where(me == 0, grad_kept, grad_got), jnp.where(me == 0, grad_got, grad_kept))
    )

    def flat(pieces):
        return [piece.reshape(-1, columns) for piece in pieces]

    def back_whole(index, grads):
        lens = own_lens[index : index + 1]
        own = attention_backward(lens, *own_heads, grads[0], lse_own, index)
        far = attention_backward(lens, *far_heads, grads[1], lse_far, index)
        return flat(own), flat(far)

    span = jnp.arange(tiles, dtype=jnp.int32)

    def back_first(own, far, table, resid_grad):
        return first_backward(
            table,
            flat_tokens,
            resid_grad,
            low,
            own,
            far,
            gain_one,
            shift_one,
            down_low,
            up_both,
            qkv,
        )

    def whole_rows(index):
        at = index * tiles + span
        return jnp.stack((token_table[at], span, at, span, live_table[at]))

    back_zero = back_whole(0, grads_zero)
    split_own = attention_backward(split_lens, *own_heads, grad_split, lse_own, whole)
    split_sent = jnp.stack(
        [lax.dynamic_slice_in_dim(p[0], (1 - me) * half, half, 0) for p in split_own]
    )
    split_got = swap(
        core_order(split_sent, 2)
    )
    first_zero = back_first(*back_zero, whole_rows(0), resid_zero)
    send_zero = swap(first_zero[0])
    back_one = back_whole(1, grads_rest)
    first_split = back_first(
        flat(split_own),
        [split_got[i] for i in range(3)],
        jnp.stack(
            (
                split * tiles + extra,
                tiles + extra - me * half_tiles,
                whole * tiles + extra,
                extra,
                split_lens[0] - extra * MID_ROWS,
            )
        ),
        resid_rest,
    )
    send_split = swap(first_split[0])
    first_one = back_first(*back_one, whole_rows(1), resid_rest)
    send_one = swap(first_one[0])

    down_sum, query_sum, value_sum = (
        first_zero[i] + first_split[i] + first_one[i] for i in range(1, 4)
    )
    up_sum = 8.0 * jnp.concatenate((query_sum[:rank], value_sum[rank:]))
    up_mine = up_sum[:, :columns]
    up_theirs = core_order(up_sum[:, columns:], 1)
    up_sum = jnp.concatenate(
        (jnp.where(me == 0, up_mine, up_theirs), jnp.where(me == 0, up_theirs, up_mine)), axis=1
    )
    live_row = jnp.full((8, width), jnp.sum(lengths).astype(f32))
    total = sum_all(jnp.concatenate((down_sum, up_sum, live_row)))
    active = total[-1, 0] / 2
    grad_down = total[: 2 * rank].reshape(2, rank, width).transpose(0, 2, 1) / active
    grad_up = total[2 * rank : 4 * rank].reshape(2, rank, width) / active

    def place(pieces):
        out = jnp.zeros((seqs * length, width), bf16)
        for piece, start in pieces:
            out = lax.dynamic_update_slice_in_dim(out, piece, start, 0)
        return out.reshape(tokens.shape)

    here = split * length + half * me
    there = split * length + half * (1 - me)
    block_out = place(
        (
            (block_zero, mine[0] * length),
            (block_rest[:length], mine[1] * length),
            (block_rest[length:], here),
            (block_zero_got, theirs[0] * length),
            (block_rest_got[:length], theirs[1] * length),
            (block_rest_got[length:], there),
        )
    )
    input_grad = place(
        (
            (first_zero[0], mine[0] * length),
            (first_split[0], here),
            (first_one[0], mine[1] * length),
            (send_zero, theirs[0] * length),
            (send_split, there),
            (send_one, theirs[1] * length),
        )
    )
    new_down = adam_decay_update(
        adapter_down_factor, grad_down, down_first_moment, down_second_moment
    )
    new_up = adam_decay_update(adapter_up_factor, grad_up, up_first_moment, up_second_moment)
    return (
        block_out,
        input_grad,
        new_down[0],
        new_up[0],
        new_down[1],
        new_up[1],
        new_down[2],
        new_up[2],
    )


def solution(mesh):
    in_specs = (
        P("dp", None, None),
        P("dp", None, None),
        P("dp"),
        P(),
        P(),
        P(None, None, "mp"),
        P("mp", None),
        P(),
        P(),
        P(),
        P(None, "mp"),
        P("mp"),
        P("mp", None),
        P(),
        P(),
        P(),
        P(),
        P(),
        P(),
        P(),
    )
    out_specs = (P("dp", None, None), P("dp", None, None), P(), P(), P(), P(), P(), P())
    return jax.shard_map(
        per_device_pair if mesh.shape["mp"] == 2 else per_device,
        mesh=mesh,
        in_specs=in_specs,
        out_specs=out_specs,
        check_vma=False,
    )
```

```python
import functools

import jax
import jax.numpy as jnp
from jax import lax
from jax.experimental import pallas as pl
from jax.experimental.pallas import tpu as pltpu
from jax.sharding import PartitionSpec as P

HEAD = 64


def layer_norm(values, norm_gain, norm_shift):
    centre = values - jnp.mean(values, axis=-1, keepdims=True)
    spread = jnp.mean(centre * centre, axis=-1, keepdims=True)
    return centre * lax.rsqrt(spread + 1e-05) * norm_gain + norm_shift


def gelu_tanh(values):
    return (
        0.5
        * values
        * (1.0 + jnp.tanh(0.7978845608028654 * (values + 0.044715 * values * values * values)))
    )


def head_major(matrix, seq_rows, head_count):
    return (
        matrix.reshape(seq_rows, -1, head_count, HEAD)
        .transpose(0, 2, 1, 3)
        .reshape(seq_rows * head_count, -1, HEAD)
    )


def token_major(stacked, seq_rows, head_count):
    return (
        stacked.reshape(seq_rows, head_count, -1, HEAD)
        .transpose(0, 2, 1, 3)
        .reshape(-1, head_count * HEAD)
    )


def masked_scores(query_rows, key_rows, seq_len):
    scores = jnp.einsum(
        "qd,kd->qk", query_rows, key_rows, preferred_element_type=jnp.float32
    ) * HEAD ** (-0.5)
    position = jnp.arange(scores.shape[0])
    allowed = (position[None, :] <= position[:, None]) & (position[None, :] < seq_len)
    return jnp.where(allowed, scores, -1e30)


def attend_forward(pieces):
    query_rows, key_rows, value_token_rows, seq_len = pieces
    scores = masked_scores(query_rows, key_rows, seq_len)
    row_max = jnp.max(scores, axis=-1, keepdims=True)
    weights = jnp.exp(scores - row_max)
    row_sum = jnp.sum(weights, axis=-1, keepdims=True)
    probabilities = (weights / row_sum).astype(jnp.bfloat16)
    head_out = jnp.dot(probabilities, value_token_rows, preferred_element_type=jnp.float32)
    return (head_out, row_max[:, 0] + jnp.log(row_sum[:, 0]))


def attend_backward(pieces):
    query_rows, key_rows, value_token_rows, seq_len, grad_head, log_sums = pieces
    scores = masked_scores(query_rows, key_rows, seq_len)
    probabilities = jnp.exp(scores - log_sums[:, None])
    value_gradient_rows = jnp.einsum(
        "qk,qd->kd",
        probabilities.astype(jnp.bfloat16),
        grad_head,
        preferred_element_type=jnp.float32,
    )
    grad_probs = jnp.einsum(
        "qd,kd->qk", grad_head, value_token_rows, preferred_element_type=jnp.float32
    )
    grad_scores = probabilities * (
        grad_probs - jnp.sum(grad_probs * probabilities, axis=-1, keepdims=True)
    )
    grad_scores = grad_scores.astype(jnp.bfloat16)
    query_gradient_rows = jnp.dot(
        grad_scores, key_rows, preferred_element_type=jnp.float32
    ) * HEAD ** (-0.5)
    grad_keys = jnp.einsum(
        "qk,qd->kd", grad_scores, query_rows, preferred_element_type=jnp.float32
    ) * HEAD ** (-0.5)
    return (query_gradient_rows, grad_keys, value_gradient_rows)


def adam_decay_update(adapter, gradient, first_mom, second_mom):
    first_new = 0.9 * first_mom + 0.1 * gradient
    second_new = 0.999 * second_mom + 0.001 * gradient * gradient
    update = first_new / (1.0 - 0.9**10) / (jnp.sqrt(second_new / (1.0 - 0.999**10)) + 1e-08)
    return (adapter - 0.25 * (update + 0.01 * adapter), first_new, second_new)


def per_device(
    tokens,
    cotangent,
    lengths,
    first_norm_gain,
    first_norm_bias,
    query_key_value_weight,
    attention_output_weight,
    attention_output_bias,
    second_norm_gain,
    second_norm_bias,
    feedforward_up_weight,
    feedforward_up_bias,
    feedforward_down_weight,
    feedforward_down_bias,
    adapter_down_factor,
    adapter_up_factor,
    down_first_moment,
    up_first_moment,
    down_second_moment,
    up_second_moment,
):
    seq_rows, seq_len_all, model_width = tokens.shape
    tok_count = seq_rows * seq_len_all
    groups = lax.axis_size("mp")
    worker_shard = lax.axis_index("mp")
    shard_width = query_key_value_weight.shape[2]
    head_count = shard_width // HEAD
    adapter_rank_size = adapter_down_factor.shape[2]
    tokens_f32 = tokens.reshape(tok_count, model_width).astype(jnp.float32)
    normalized_rows = layer_norm(tokens_f32, first_norm_gain, first_norm_bias).astype(jnp.bfloat16)
    down_reduced = adapter_down_factor.astype(jnp.bfloat16)
    up_reduced = adapter_up_factor.astype(jnp.bfloat16)
    up_columns = lax.dynamic_slice_in_dim(up_reduced, worker_shard * shard_width, shard_width, 2)
    down_pair = jnp.concatenate((down_reduced[0], down_reduced[1]), axis=1)
    adapter_pair = jnp.dot(normalized_rows, down_pair, preferred_element_type=jnp.float32).astype(
        jnp.bfloat16
    )
    adapter_query_delta = adapter_pair[:, :adapter_rank_size]
    adapter_value_delta = adapter_pair[:, adapter_rank_size:]
    query_rows = (
        jnp.dot(normalized_rows, query_key_value_weight[0], preferred_element_type=jnp.float32)
        + 8.0 * jnp.dot(adapter_query_delta, up_columns[0], preferred_element_type=jnp.float32)
    ).astype(jnp.bfloat16)
    key_rows = jnp.dot(
        normalized_rows, query_key_value_weight[1], preferred_element_type=jnp.float32
    ).astype(jnp.bfloat16)
    value_token_rows = (
        jnp.dot(normalized_rows, query_key_value_weight[2], preferred_element_type=jnp.float32)
        + 8.0 * jnp.dot(adapter_value_delta, up_columns[1], preferred_element_type=jnp.float32)
    ).astype(jnp.bfloat16)
    limits = jnp.repeat(lengths, head_count)
    query_heads = head_major(query_rows, seq_rows, head_count)
    key_heads = head_major(key_rows, seq_rows, head_count)
    value_heads = head_major(value_token_rows, seq_rows, head_count)
    head_out, log_sums = lax.map(attend_forward, (query_heads, key_heads, value_heads, limits))
    attended = token_major(head_out, seq_rows, head_count).astype(jnp.bfloat16)
    attn_share = (
        lax.psum_scatter(
            jnp.dot(attended, attention_output_weight, preferred_element_type=jnp.float32),
            "mp",
            scatter_dimension=0,
            tiled=True,
        )
        + attention_output_bias
    )

    def norm_two(values):
        return layer_norm(values, second_norm_gain, second_norm_bias)

    def norm_one(values):
        return layer_norm(values, first_norm_gain, first_norm_bias)

    attn_full = lax.all_gather(attn_share, "mp", axis=0, tiled=True)
    residual = tokens_f32 + attn_full
    normed_two = norm_two(residual).astype(jnp.bfloat16)
    hidden_pre = (
        jnp.dot(normed_two, feedforward_up_weight, preferred_element_type=jnp.float32)
        + feedforward_up_bias
    )
    hidden = gelu_tanh(hidden_pre).astype(jnp.bfloat16)
    mlp_share = (
        lax.psum_scatter(
            jnp.dot(hidden, feedforward_down_weight, preferred_element_type=jnp.float32).astype(
                jnp.bfloat16
            ),
            "mp",
            scatter_dimension=0,
            tiled=True,
        ).astype(jnp.float32)
        + feedforward_down_bias
    )
    mlp_full = lax.all_gather(mlp_share.astype(jnp.bfloat16), "mp", axis=0, tiled=True).astype(
        mlp_share.dtype
    )
    block_out = (residual + mlp_full).astype(jnp.bfloat16)
    live_mask = (jnp.arange(seq_len_all)[None, :] < lengths[:, None]).reshape(tok_count, 1)
    grad_out = jnp.where(
        live_mask, cotangent.reshape(tok_count, model_width), jnp.zeros((), jnp.bfloat16)
    )
    grad_hidden = jnp.einsum(
        "td,fd->tf", grad_out, feedforward_down_weight, preferred_element_type=jnp.float32
    )
    _, gelu_back = jax.vjp(gelu_tanh, hidden_pre)
    grad_pre = gelu_back(grad_hidden)[0].astype(jnp.bfloat16)
    grad_norm2_share = lax.psum_scatter(
        jnp.einsum(
            "tf,df->td", grad_pre, feedforward_up_weight, preferred_element_type=jnp.float32
        ),
        "mp",
        scatter_dimension=0,
        tiled=True,
    )
    grad_norm2 = lax.all_gather(grad_norm2_share, "mp", axis=0, tiled=True)
    _, norm2_back = jax.vjp(norm_two, residual)
    grad_resid = grad_out.astype(jnp.float32) + norm2_back(grad_norm2)[0]
    grad_resid_low = grad_resid.astype(jnp.bfloat16)
    grad_attended = jnp.einsum(
        "td,ed->te", grad_resid_low, attention_output_weight, preferred_element_type=jnp.float32
    ).astype(jnp.bfloat16)
    grad_head = head_major(grad_attended, seq_rows, head_count)
    head_dq, head_dk, head_dv = lax.map(
        attend_backward, (query_heads, key_heads, value_heads, limits, grad_head, log_sums)
    )
    query_gradient_rows = token_major(head_dq, seq_rows, head_count).astype(jnp.bfloat16)
    grad_keys = token_major(head_dk, seq_rows, head_count).astype(jnp.bfloat16)
    value_gradient_rows = token_major(head_dv, seq_rows, head_count).astype(jnp.bfloat16)
    adapter_query_gradient = 8.0 * jnp.einsum(
        "te,re->tr", query_gradient_rows, up_columns[0], preferred_element_type=jnp.float32
    )
    adapter_value_gradient = 8.0 * jnp.einsum(
        "te,re->tr", value_gradient_rows, up_columns[1], preferred_element_type=jnp.float32
    )
    adapter_gradient = jnp.concatenate((adapter_query_gradient, adapter_value_gradient), axis=1)
    down_pair_float32 = down_pair.astype(jnp.float32)
    partial_sum = jnp.einsum(
        "te,de->td",
        query_gradient_rows,
        query_key_value_weight[0],
        preferred_element_type=jnp.float32,
    )
    partial_sum = partial_sum + jnp.einsum(
        "te,de->td", grad_keys, query_key_value_weight[1], preferred_element_type=jnp.float32
    )
    partial_sum = partial_sum + jnp.einsum(
        "te,de->td",
        value_gradient_rows,
        query_key_value_weight[2],
        preferred_element_type=jnp.float32,
    )
    grad_norm1_share = lax.psum_scatter(
        partial_sum
        + jnp.einsum(
            "gy,wy->gw", adapter_gradient, down_pair_float32, precision=lax.Precision.HIGHEST
        ),
        "mp",
        scatter_dimension=0,
        tiled=True,
    )
    grad_down_both = jnp.einsum(
        "fi,fg->ig",
        normalized_rows.astype(jnp.float32),
        adapter_gradient,
        precision=lax.Precision.HIGHEST,
    )
    grad_down = jnp.stack(
        (grad_down_both[:, :adapter_rank_size], grad_down_both[:, adapter_rank_size:])
    )
    grad_up_query = 8.0 * jnp.einsum(
        "zm,zj->mj", adapter_query_delta, query_gradient_rows, preferred_element_type=jnp.float32
    )
    grad_up_value = 8.0 * jnp.einsum(
        "zm,zj->mj", adapter_value_delta, value_gradient_rows, preferred_element_type=jnp.float32
    )
    up_column_gradient = jnp.stack((grad_up_query, grad_up_value))
    grad_up = lax.dynamic_update_slice_in_dim(
        jnp.zeros(adapter_up_factor.shape, jnp.float32),
        up_column_gradient,
        worker_shard * shard_width,
        2,
    )
    live_local = jnp.sum(lengths).astype(jnp.float32)
    down_reduced_sum, up_reduced_sum, live_sum = lax.psum(
        (grad_down, grad_up, live_local), ("dp", "mp")
    )
    active_token_total = live_sum / groups
    grad_norm1 = lax.all_gather(grad_norm1_share, "mp", axis=0, tiled=True)
    _, norm1_back = jax.vjp(norm_one, tokens_f32)
    input_grad = (grad_resid + norm1_back(grad_norm1)[0]).astype(jnp.bfloat16)
    down_factor_next, down_first_moment_next, down_second_moment_next = adam_decay_update(
        adapter_down_factor,
        down_reduced_sum / active_token_total,
        down_first_moment,
        down_second_moment,
    )
    up_factor_next, up_first_moment_next, up_second_moment_next = adam_decay_update(
        adapter_up_factor, up_reduced_sum / active_token_total, up_first_moment, up_second_moment
    )
    return (
        block_out.reshape(seq_rows, seq_len_all, model_width),
        input_grad.reshape(seq_rows, seq_len_all, model_width),
        down_factor_next,
        up_factor_next,
        down_first_moment_next,
        up_first_moment_next,
        down_second_moment_next,
        up_second_moment_next,
    )


TILE = 256
NT = (((1,), (1,)), ((), ()))


def head_lanes(half):
    lane = lax.broadcasted_iota(jnp.int32, (1, 2 * HEAD), 1)
    return (lane >= half * HEAD) & (lane < (half + 1) * HEAD)


def one_head(block, half):
    return jnp.where(head_lanes(half), block, jnp.zeros((), block.dtype))


def edge_allowed(key_start, query_start, seq_len):
    key_at = key_start + lax.broadcasted_iota(jnp.int32, (TILE, TILE), 0)
    query_at = query_start + lax.broadcasted_iota(jnp.int32, (TILE, TILE), 1)
    return (key_at <= query_at) & (key_at < seq_len)


def attention_forward_kernel(lens_ref, q_ref, k_ref, v_ref, out_ref, lse_ref, vt_ref):
    seq_len = lens_ref[pl.program_id(0)]
    live_tiles = (seq_len + TILE - 1) // TILE
    vt_ref[...] = v_ref[0].T
    tiles = q_ref.shape[1] // TILE

    def row_tile(tile, extent):
        rows = pl.ds(tile * TILE, TILE)
        inner = (extent - 1) * TILE
        query = q_ref[0, rows, :] * HEAD ** (-0.5)
        allowed = edge_allowed(inner, tile * TILE, seq_len)
        outs = []
        for half in range(2):
            mine = one_head(query, half)
            edge = lax.dot_general(
                k_ref[0, pl.ds(inner, TILE), :], mine, NT, preferred_element_type=jnp.float32
            )
            edge = jnp.where(allowed, edge, -1e30)
            top = jnp.max(edge, axis=0, keepdims=True)
            if inner:
                past = lax.dot_general(
                    k_ref[0, pl.ds(0, inner), :], mine, NT, preferred_element_type=jnp.float32
                )
                top = jnp.maximum(top, jnp.max(past, axis=0, keepdims=True))
            head_rows = pl.ds(half * HEAD, HEAD)
            edge = jnp.exp(edge - top)
            total = jnp.sum(edge, axis=0, keepdims=True)
            out = jnp.dot(
                vt_ref[head_rows, pl.ds(inner, TILE)],
                edge.astype(jnp.bfloat16),
                preferred_element_type=jnp.float32,
            )
            if inner:
                past = jnp.exp(past - top)
                total = total + jnp.sum(past, axis=0, keepdims=True)
                out = out + jnp.dot(
                    vt_ref[head_rows, pl.ds(0, inner)],
                    past.astype(jnp.bfloat16),
                    preferred_element_type=jnp.float32,
                )
            outs.append(out / total)
            lse_ref[0, 0, pl.ds(half, 1), rows] = top + jnp.log(total)
        out_ref[0, rows, :] = jnp.concatenate(outs, axis=0).T.astype(out_ref.dtype)

    for tile in range(tiles):
        for extent in range(1, tile + 2):
            pl.when(jnp.minimum(live_tiles, tile + 1) == extent)(
                lambda tile=tile, extent=extent: row_tile(tile, extent)
            )


def attention_forward(lens, query, key, value):
    seqs, length, width = query.shape
    pairs = width // (2 * HEAD)
    spec = pl.BlockSpec((1, length, 2 * HEAD), lambda s, h, lens: (s, 0, h))
    return pl.pallas_call(
        attention_forward_kernel,
        grid_spec=pltpu.PrefetchScalarGridSpec(
            num_scalar_prefetch=1,
            grid=(seqs, pairs),
            in_specs=[spec] * 3,
            out_specs=[spec, pl.BlockSpec((1, 1, 2, length), lambda s, h, lens: (s, h, 0, 0))],
            scratch_shapes=[pltpu.VMEM((2 * HEAD, length), jnp.bfloat16)],
        ),
        out_shape=[
            jax.ShapeDtypeStruct(query.shape, jnp.bfloat16),
            jax.ShapeDtypeStruct((seqs, pairs, 2, length), jnp.float32),
        ],
        cost_estimate=pl.CostEstimate(
            flops=seqs * width * length * length * 3,
            bytes_accessed=seqs * width * length * 8,
            transcendentals=seqs * pairs * length * length,
        ),
        name="attention_forward",
    )(lens, query, key, value)


def attention_backward_kernel(
    lens_ref, q_ref, k_ref, v_ref, g_ref, lse_ref, dq_ref, dk_ref, dv_ref, kt_ref, dk_acc, dv_acc
):
    seq_len = lens_ref[pl.program_id(0)]
    kt_ref[...] = k_ref[0].T
    dk_acc[...] = jnp.zeros_like(dk_acc)
    dv_acc[...] = jnp.zeros_like(dv_acc)
    tiles = q_ref.shape[1] // TILE

    def row_tile(tile):
        rows = pl.ds(tile * TILE, TILE)
        inner = tile * TILE
        query = q_ref[0, rows, :] * HEAD ** (-0.5)
        grad = g_ref[rows, :]
        allowed = edge_allowed(inner, inner, seq_len)
        spans = [(inner, TILE)] + ([(0, inner)] if inner else [])
        outs = []
        for half in range(2):
            mine = one_head(query, half)
            mine_grad = one_head(grad, half)
            lse = lse_ref[0, 0, pl.ds(half, 1), rows]
            probs, grad_probs, row_dot = [], [], 0.0
            for at, (start, size) in enumerate(spans):
                keys = pl.ds(start, size)
                scores = lax.dot_general(
                    k_ref[0, keys, :], mine, NT, preferred_element_type=jnp.float32
                )
                if at == 0:
                    scores = jnp.where(allowed, scores, -1e30)
                prob = jnp.exp(scores - lse)
                dv_acc[keys, :] += jnp.dot(
                    prob.astype(jnp.bfloat16), mine_grad, preferred_element_type=jnp.float32
                )
                grad_prob = lax.dot_general(
                    v_ref[0, keys, :], mine_grad, NT, preferred_element_type=jnp.float32
                )
                row_dot = row_dot + jnp.sum(prob * grad_prob, axis=0, keepdims=True)
                probs.append(prob)
                grad_probs.append(grad_prob)
            out = 0.0
            for (start, size), prob, grad_prob in zip(spans, probs, grad_probs):
                keys = pl.ds(start, size)
                grad_scores = (prob * (grad_prob - row_dot)).astype(jnp.bfloat16)
                dk_acc[keys, :] += jnp.dot(grad_scores, mine, preferred_element_type=jnp.float32)
                out = out + jnp.dot(
                    kt_ref[pl.ds(half * HEAD, HEAD), keys],
                    grad_scores,
                    preferred_element_type=jnp.float32,
                )
            outs.append(out)
        dq = jnp.concatenate(outs, axis=0).T * HEAD ** (-0.5)
        dq_ref[0, rows, :] = dq.astype(dq_ref.dtype)

    for tile in range(tiles):
        pl.when(tile * TILE < seq_len)(lambda tile=tile: row_tile(tile))

        @pl.when(tile * TILE >= seq_len)
        def _(tile=tile):
            dq_ref[0, pl.ds(tile * TILE, TILE), :] = jnp.zeros((TILE, 2 * HEAD), dq_ref.dtype)

    dk_ref[0] = dk_acc[...].astype(dk_ref.dtype)
    dv_ref[0] = dv_acc[...].astype(dv_ref.dtype)


def attention_backward(lens, query, key, value, grad, lse, start):
    length, width = query.shape[1:]
    seqs = lens.shape[0]
    pairs = width // (2 * HEAD)

    def block(first):
        return pl.BlockSpec((1, length, 2 * HEAD), lambda s, h, lens: (s + first, 0, h))

    return pl.pallas_call(
        attention_backward_kernel,
        grid_spec=pltpu.PrefetchScalarGridSpec(
            num_scalar_prefetch=1,
            grid=(seqs, pairs),
            in_specs=[block(start)] * 3
            + [
                pl.BlockSpec((length, 2 * HEAD), lambda s, h, lens: (s, h)),
                pl.BlockSpec((1, 1, 2, length), lambda s, h, lens: (s + start, h, 0, 0)),
            ],
            out_specs=[block(0)] * 3,
            scratch_shapes=[
                pltpu.VMEM((2 * HEAD, length), jnp.bfloat16),
                pltpu.VMEM((length, 2 * HEAD), jnp.float32),
                pltpu.VMEM((length, 2 * HEAD), jnp.float32),
            ],
        ),
        out_shape=[jax.ShapeDtypeStruct((seqs, length, width), jnp.bfloat16)] * 3,
        cost_estimate=pl.CostEstimate(
            flops=seqs * width * length * length * 7,
            bytes_accessed=seqs * width * length * 14,
            transcendentals=seqs * pairs * length * length,
        ),
        name="attention_backward",
    )(lens, query, key, value, grad, lse)


MID_ROWS = 256
CHUNK = 1024


def centred(values):
    centre = values - jnp.mean(values, axis=-1, keepdims=True)
    inverse = lax.rsqrt(jnp.mean(centre * centre, axis=-1, keepdims=True) + 1e-05)
    return centre * inverse, inverse


def norm_backward(grad, gain, normal, inverse):
    grad = grad * gain
    mean = jnp.mean(grad, axis=-1, keepdims=True)
    along = jnp.mean(grad * normal, axis=-1, keepdims=True)
    return (grad - mean - normal * along) * inverse


def dot(a, b):
    return jnp.dot(a, b, preferred_element_type=jnp.float32)


def dot_t(a, b):
    return lax.dot_general(a, b, NT, preferred_element_type=jnp.float32)


def copies_of(pairs, sems):
    return [pltpu.make_async_copy(a, b, sems.at[i]) for i, (a, b) in enumerate(pairs)]


def middle_kernel(
    table_ref,
    tokens_ref,
    cotangent_ref,
    attended_own,
    attended_far,
    out_bias_ref,
    gain_ref,
    shift_ref,
    up_bias_ref,
    down_bias_ref,
    out_own,
    out_near,
    out_far,
    up_own,
    up_near,
    up_far,
    down_own,
    down_near,
    down_far,
    block_ref,
    resid_grad_ref,
    own_grad_ref,
    far_grad_ref,
    out_w,
    up_w,
    down_w,
    residual_ref,
    normed_ref,
    normal_ref,
    acc_ref,
    grad_acc_ref,
    sems,
):
    step = pl.program_id(0)

    pairs = []
    start = 0
    for piece in (out_own, out_near, out_far):
        rows = piece.shape[0]
        pairs.append((piece, out_w.at[pl.ds(start, rows), :]))
        start += rows
    chunk = 0
    for up, down in ((up_own, down_own), (up_near, down_near), (up_far, down_far)):
        for at in range(up.shape[1] // CHUNK):
            units = pl.ds(at * CHUNK, CHUNK)
            pairs.append((up.at[:, units], up_w.at[chunk]))
            pairs.append((down.at[units, :], down_w.at[chunk]))
            chunk += 1
    loads = copies_of(pairs, sems)

    @pl.when(step == 0)
    def _():
        for load in loads:
            load.start()
        for load in loads[:3]:
            load.wait()

    live = table_ref[2, step]
    residual = tokens_ref[...].astype(jnp.float32) + (
        dot(jnp.concatenate((attended_own[...], attended_far[...]), axis=1), out_w[...])
        + out_bias_ref[...]
    )
    residual_ref[...] = residual
    normal, inverse = centred(residual)
    normal_ref[...] = normal
    normed_ref[...] = (normal * gain_ref[...] + shift_ref[...]).astype(jnp.bfloat16)
    acc_ref[...] = jnp.zeros_like(acc_ref)

    @pl.when(step == 0)
    def _():
        for load in loads[3:]:
            load.wait()

    scale = 0.7978845608028654
    cube = 0.044715 * scale

    def forward_only(chunk, carry):
        pre = dot(normed_ref[...], up_w[chunk]) + up_bias_ref[chunk]
        tanh = jnp.tanh(pre * (scale + cube * (pre * pre)))
        hidden = (pre * (0.5 + 0.5 * tanh)).astype(jnp.bfloat16)
        acc_ref[...] += dot(hidden, down_w[chunk])
        return carry

    def finish():
        block_ref[...] = (residual_ref[...] + acc_ref[...] + down_bias_ref[...]).astype(
            block_ref.dtype
        )

    @pl.when(live > 0)
    def _():
        row = lax.broadcasted_iota(jnp.int32, (MID_ROWS, 1), 0)
        grad_out = jnp.where(row < live, cotangent_ref[...], jnp.zeros((), jnp.bfloat16))
        grad_acc_ref[...] = jnp.zeros_like(grad_acc_ref)

        def both_ways(chunk, carry):
            pre = dot(normed_ref[...], up_w[chunk]) + up_bias_ref[chunk]
            grad_hidden = dot_t(grad_out, down_w[chunk])
            square = pre * pre
            tanh = jnp.tanh(pre * (scale + cube * square))
            gate = 0.5 + 0.5 * tanh
            hidden = (pre * gate).astype(jnp.bfloat16)
            slope = gate + (pre * (0.5 - 0.5 * (tanh * tanh))) * (scale + 3.0 * cube * square)
            grad_pre = (grad_hidden * slope).astype(jnp.bfloat16)
            acc_ref[...] += dot(hidden, down_w[chunk])
            grad_acc_ref[...] += dot_t(grad_pre, up_w[chunk])
            return carry

        lax.fori_loop(0, up_w.shape[0], both_ways, 0, unroll=UNROLL)
        finish()
        grad_resid = grad_out.astype(jnp.float32) + norm_backward(
            grad_acc_ref[...], gain_ref[...], normal_ref[...], inverse
        )
        low = grad_resid.astype(jnp.bfloat16)
        resid_grad_ref[...] = low
        columns = own_grad_ref.shape[1]
        own_grad_ref[...] = dot_t(low, out_w[:columns]).astype(jnp.bfloat16)
        far_grad_ref[...] = dot_t(low, out_w[columns:]).astype(jnp.bfloat16)

    @pl.when(live <= 0)
    def _():
        lax.fori_loop(0, up_w.shape[0], forward_only, 0, unroll=UNROLL)
        finish()
        resid_grad_ref[...] = jnp.zeros_like(resid_grad_ref)
        own_grad_ref[...] = jnp.zeros_like(own_grad_ref)
        far_grad_ref[...] = jnp.zeros_like(far_grad_ref)


UNROLL = 2


def middle(
    table, tokens, cotangent, own, far, out_bias, gain, shift, up_bias, down_bias, weights
):
    rows, width = table.shape[1] * MID_ROWS, tokens.shape[1]
    columns = far.shape[1]
    units = up_bias.shape[0] * up_bias.shape[2]
    tile = pl.BlockSpec((MID_ROWS, width), lambda i, t: (i, 0))
    picked = pl.BlockSpec((MID_ROWS, width), lambda i, t: (t[0, i], 0))
    part = pl.BlockSpec((MID_ROWS, columns), lambda i, t: (i, 0))
    vector = pl.BlockSpec((1, width), lambda i, t: (0, 0))
    chunks = units // CHUNK
    low = jax.ShapeDtypeStruct((rows, width), jnp.bfloat16)
    thin = jax.ShapeDtypeStruct((rows, columns), jnp.bfloat16)
    wide = pltpu.VMEM((MID_ROWS, width), jnp.float32)
    return pl.pallas_call(
        middle_kernel,
        grid_spec=pltpu.PrefetchScalarGridSpec(
            num_scalar_prefetch=1,
            grid=(rows // MID_ROWS,),
            in_specs=[picked] * 2
            + [pl.BlockSpec((MID_ROWS, columns), lambda i, t, a=a: (t[a, i], 0)) for a in (1, 3)]
            + [vector] * 3
            + [pl.BlockSpec(up_bias.shape, lambda i, t: (0, 0, 0)), vector]
            + [pl.BlockSpec(memory_space=pl.ANY)] * 9,
            out_specs=[tile, tile, part, part],
            scratch_shapes=[
                pltpu.VMEM((width, width), jnp.bfloat16),
                pltpu.VMEM((chunks, width, CHUNK), jnp.bfloat16),
                pltpu.VMEM((chunks, CHUNK, width), jnp.bfloat16),
                wide,
                pltpu.VMEM((MID_ROWS, width), jnp.bfloat16),
                wide,
                wide,
                wide,
                pltpu.SemaphoreType.DMA((3 + 2 * chunks,)),
            ],
        ),
        out_shape=[low, low, thin, thin],
        compiler_params=pltpu.CompilerParams(vmem_limit_bytes=56 << 20),
        cost_estimate=pl.CostEstimate(
            flops=rows * width * (units * 8 + width * 4),
            bytes_accessed=rows * width * 12 + units * width * 4,
            transcendentals=rows * units,
        ),
        name="middle",
    )(
        table,
        tokens,
        cotangent,
        own,
        far,
        out_bias,
        gain,
        shift,
        up_bias,
        down_bias,
        *weights,
    )


PROJECT_ROWS = 256


def qkv_loads(own, near, far, weight_ref, sems):
    pairs = []
    start = 0
    for piece in (own, near, far):
        if piece is not None:
            columns = pl.ds(start, piece.shape[2])
            pairs.append((piece, weight_ref.at[:, :, columns]))
            start += piece.shape[2]
    return copies_of(pairs, sems)


def project_kernel(pieces, table_ref, *refs):
    tokens_ref, gain_ref, shift_ref, down_ref, up_ref = refs[:5]
    weights = list(refs[5 : 5 + pieces]) + [None] * (3 - pieces)
    query_ref, key_ref, value_ref, low_ref, weight_ref, sems = refs[5 + pieces :]
    loads = qkv_loads(*weights, weight_ref, sems)
    first = pl.program_id(0) == 0

    @pl.when(first)
    def _():
        for load in loads:
            load.start()

    normal, _ = centred(tokens_ref[...].astype(jnp.float32))
    normed = (normal * gain_ref[...] + shift_ref[...]).astype(jnp.bfloat16)
    low = dot_t(normed, down_ref[...]).astype(jnp.bfloat16)
    low_ref[...] = low.astype(jnp.float32).T

    @pl.when(first)
    def _():
        for load in loads:
            load.wait()

    query_ref[...] = (dot(normed, weight_ref[0]) + 8.0 * dot(low, up_ref[0])).astype(jnp.bfloat16)
    key_ref[...] = dot(normed, weight_ref[1]).astype(jnp.bfloat16)
    value_ref[...] = (dot(normed, weight_ref[2]) + 8.0 * dot(low, up_ref[1])).astype(jnp.bfloat16)


def project(table, tokens, gain, shift, down, up, *weights):
    rows, width = table.shape[0] * PROJECT_ROWS, tokens.shape[1]
    columns = up.shape[2]
    pairs = down.shape[0]
    out = pl.BlockSpec((PROJECT_ROWS, columns), lambda i, t: (i, 0))
    vector = pl.BlockSpec((1, width), lambda i, t: (0, 0))
    return pl.pallas_call(
        functools.partial(project_kernel, len(weights)),
        grid_spec=pltpu.PrefetchScalarGridSpec(
            num_scalar_prefetch=1,
            grid=(rows // PROJECT_ROWS,),
            in_specs=[
                pl.BlockSpec((PROJECT_ROWS, width), lambda i, t: (t[i], 0)),
                vector,
                vector,
                pl.BlockSpec(down.shape, lambda i, t: (0, 0)),
                pl.BlockSpec(up.shape, lambda i, t: (0, 0, 0)),
            ]
            + [pl.BlockSpec(memory_space=pl.ANY)] * len(weights),
            out_specs=[out] * 3 + [pl.BlockSpec((pairs, PROJECT_ROWS), lambda i, t: (0, i))],
            scratch_shapes=[
                pltpu.VMEM((3, width, columns), jnp.bfloat16),
                pltpu.SemaphoreType.DMA((len(weights),)),
            ],
        ),
        out_shape=[jax.ShapeDtypeStruct((rows, columns), jnp.bfloat16)] * 3
        + [jax.ShapeDtypeStruct((pairs, rows), jnp.float32)],
        cost_estimate=pl.CostEstimate(
            flops=rows * width * columns * 6,
            bytes_accessed=rows * (width + 3 * columns) * 2 + 6 * width * columns,
            transcendentals=rows,
        ),
        name="project",
    )(table, tokens, gain, shift, down, up, *weights)


def first_backward_kernel(
    table_ref,
    tokens_ref,
    resid_grad_ref,
    low_ref,
    query_own,
    key_own,
    value_own,
    query_far,
    key_far,
    value_far,
    gain_ref,
    shift_ref,
    down_ref,
    up_ref,
    own_ref,
    near_ref,
    far_ref,
    input_ref,
    down_grad_ref,
    query_up_ref,
    value_up_ref,
    weight_ref,
    sems,
):
    first = pl.program_id(0) == 0
    loads = qkv_loads(own_ref, near_ref, far_ref, weight_ref, sems)

    @pl.when(first)
    def _():
        for load in loads:
            load.start()
        down_grad_ref[...] = jnp.zeros_like(down_grad_ref)
        query_up_ref[...] = jnp.zeros_like(query_up_ref)
        value_up_ref[...] = jnp.zeros_like(value_up_ref)

    normal, inverse = centred(tokens_ref[...].astype(jnp.float32))
    normed = (normal * gain_ref[...] + shift_ref[...]).astype(jnp.bfloat16)
    query = jnp.concatenate((query_own[...], query_far[...]), axis=1)
    key = jnp.concatenate((key_own[...], key_far[...]), axis=1)
    value = jnp.concatenate((value_own[...], value_far[...]), axis=1)
    adapter = 8.0 * (dot_t(query, up_ref[0]) + dot_t(value, up_ref[1]))
    high = adapter.astype(jnp.bfloat16)
    rest = (adapter - high.astype(jnp.float32)).astype(jnp.bfloat16)
    down_grad_ref[...] += dot(high.astype(jnp.float32).T.astype(jnp.bfloat16), normed) + dot(
        rest.astype(jnp.float32).T.astype(jnp.bfloat16), normed
    )
    low = low_ref[...].astype(jnp.bfloat16)
    query_up_ref[...] += dot(low, query)
    value_up_ref[...] += dot(low, value)

    @pl.when(first)
    def _():
        for load in loads:
            load.wait()

    grad = (
        dot_t(query, weight_ref[0])
        + dot_t(key, weight_ref[1])
        + dot_t(value, weight_ref[2])
        + dot(high, down_ref[...])
        + dot(rest, down_ref[...])
    )
    input_ref[...] = (
        resid_grad_ref[...].astype(jnp.float32)
        + norm_backward(grad, gain_ref[...], normal, inverse)
    ).astype(input_ref.dtype)


def first_backward(
    table, tokens, resid_grad, low, own, far, gain, shift, down, up, weights
):
    tiles = table.shape[1]
    rows, width = tiles * PROJECT_ROWS, tokens.shape[1]
    pairs = down.shape[0]
    columns = own[0].shape[1]
    tile = pl.BlockSpec((PROJECT_ROWS, width), lambda i, t: (t[0, i], 0))
    vector = pl.BlockSpec((1, width), lambda i, t: (0, 0))
    small = pl.BlockSpec((pairs, width), lambda i, t: (0, 0))
    sums = jax.ShapeDtypeStruct((pairs, width), jnp.float32)
    return pl.pallas_call(
        first_backward_kernel,
        grid_spec=pltpu.PrefetchScalarGridSpec(
            num_scalar_prefetch=1,
            grid=(tiles,),
            in_specs=[
                tile,
                pl.BlockSpec((PROJECT_ROWS, width), lambda i, t: (t[1, i], 0)),
                pl.BlockSpec((pairs, PROJECT_ROWS), lambda i, t: (0, t[2, i])),
            ]
            + [pl.BlockSpec((PROJECT_ROWS, columns), lambda i, t: (t[3, i], 0))] * 3
            + [pl.BlockSpec((PROJECT_ROWS, columns), lambda i, t: (i, 0))] * 3
            + [vector, vector, small, pl.BlockSpec(up.shape, lambda i, t: (0, 0, 0))]
            + [pl.BlockSpec(memory_space=pl.ANY)] * 3,
            out_specs=[pl.BlockSpec((PROJECT_ROWS, width), lambda i, t: (i, 0))] + [small] * 3,
            scratch_shapes=[
                pltpu.VMEM((3, width, width), jnp.bfloat16),
                pltpu.SemaphoreType.DMA((3,)),
            ],
        ),
        out_shape=[jax.ShapeDtypeStruct((rows, width), jnp.bfloat16)] + [sums] * 3,
        cost_estimate=pl.CostEstimate(
            flops=rows * width * width * 7,
            bytes_accessed=rows * width * 12 + 6 * width * width,
            transcendentals=rows,
        ),
        name="first_backward",
    )(table, tokens, resid_grad, low, *own, *far, gain, shift, down, up, *weights)


def swap(value):
    return lax.ppermute(value, "mp", [(0, 1), (1, 0)])


def after(value, *earlier):
    return lax.optimization_barrier((value, *earlier))[0]


def core_swap(value):
    return lax.ppermute(value, "dp", [(i, i ^ 1) for i in range(lax.axis_size("dp"))])


def core_half(shard, axis):
    size = shard.shape[axis] // 2
    core = lax.rem(lax.axis_index("dp"), 2)
    return lax.dynamic_slice_in_dim(shard, core * size, size, axis)


def core_order(value, axis):
    size = value.shape[axis] // 2
    core = lax.rem(lax.axis_index("dp"), 2)
    low = lax.slice_in_dim(value, 0, size, axis=axis)
    high = lax.slice_in_dim(value, size, 2 * size, axis=axis)
    return jnp.where(
        core == 0, value, jnp.concatenate((high, low), axis=axis)
    )


def sum_all(value):
    count = lax.axis_size("dp")
    if count & (count - 1):
        return lax.psum(value, ("dp", "mp"))
    bit = 1
    while bit < count:
        value = value + lax.ppermute(value, "dp", [(i, i ^ bit) for i in range(count)])
        bit *= 2
    return value + swap(value)


def per_device_pair(
    tokens,
    cotangent,
    lengths,
    first_norm_gain,
    first_norm_bias,
    query_key_value_weight,
    attention_output_weight,
    attention_output_bias,
    second_norm_gain,
    second_norm_bias,
    feedforward_up_weight,
    feedforward_up_bias,
    feedforward_down_weight,
    feedforward_down_bias,
    adapter_down_factor,
    adapter_up_factor,
    down_first_moment,
    up_first_moment,
    down_second_moment,
    up_second_moment,
):
    return pair_step(tokens, cotangent, lengths, first_norm_gain, first_norm_bias, query_key_value_weight, attention_output_weight, attention_output_bias, second_norm_gain, second_norm_bias, feedforward_up_weight, feedforward_up_bias, feedforward_down_weight, feedforward_down_bias, adapter_down_factor, adapter_up_factor, down_first_moment, up_first_moment, down_second_moment, up_second_moment)


def pair_step(
    tokens,
    cotangent,
    lengths,
    first_norm_gain,
    first_norm_bias,
    query_key_value_weight,
    attention_output_weight,
    attention_output_bias,
    second_norm_gain,
    second_norm_bias,
    feedforward_up_weight,
    feedforward_up_bias,
    feedforward_down_weight,
    feedforward_down_bias,
    adapter_down_factor,
    adapter_up_factor,
    down_first_moment,
    up_first_moment,
    down_second_moment,
    up_second_moment,
):
    f32, bf16 = jnp.float32, jnp.bfloat16
    seqs, length, width = tokens.shape
    rank = adapter_down_factor.shape[2]
    me = lax.axis_index("mp")
    columns = query_key_value_weight.shape[2]
    whole, half = 2, length // 2
    tiles, half_tiles = length // MID_ROWS, half // MID_ROWS

    def row(vector):
        return vector.reshape(1, -1)

    qkv_near = swap(core_half(query_key_value_weight, 2))
    up_bias = jnp.concatenate(
        (feedforward_up_bias, core_order(swap(feedforward_up_bias), 0))
    ).reshape(-1, 1, CHUNK)

    down_low = adapter_down_factor.astype(bf16).transpose(0, 2, 1).reshape(2 * rank, width)
    up_low = adapter_up_factor.astype(bf16)
    blank = jnp.zeros_like(up_low[0])
    up_low = jnp.stack(
        (jnp.concatenate((up_low[0], blank)), jnp.concatenate((blank, up_low[1])))
    )
    up_own = lax.dynamic_slice_in_dim(up_low, me * columns, columns, 2)
    up_other = core_order(
        lax.dynamic_slice_in_dim(up_low, (1 - me) * columns, columns, 2), 2
    )
    up_both = jnp.concatenate((up_own, up_other), axis=2)

    places = jnp.arange(seqs, dtype=jnp.int32)
    longer = (lengths[None, :] > lengths[:, None]) | (
        (lengths[None, :] == lengths[:, None]) & (places[None, :] < places[:, None])
    )
    standing = jnp.sum(longer.astype(jnp.int32), axis=1)
    order = jnp.sum(jnp.where(standing[None, :] == places[:, None], places[None, :], 0), axis=1)
    split = order[0]

    mine = jnp.stack((jnp.where(me == 0, order[1], order[2]), jnp.where(me == 0, order[4], order[3])))
    theirs = jnp.stack(
        (jnp.where(me == 0, order[2], order[1]), jnp.where(me == 0, order[3], order[4]))
    )

    def lens_of(index):
        return jnp.sum(jnp.where(places[None, :] == index[:, None], lengths[None, :], 0), axis=1)

    own_lens = lens_of(mine)
    split_lens = lens_of(split[None])
    three_lens = jnp.concatenate((own_lens, split_lens))
    flat_tokens = tokens.reshape(-1, width)
    flat_cotangent = cotangent.reshape(-1, width)
    step = jnp.arange(whole * tiles, dtype=jnp.int32)
    extra = jnp.arange(half_tiles, dtype=jnp.int32) + me * half_tiles
    whole_table = mine[step // tiles] * tiles + step % tiles
    token_table = jnp.concatenate((whole_table, split * tiles + extra))
    own_table = jnp.concatenate((step, whole * tiles + extra))
    live_table = jnp.concatenate(
        (
            own_lens[step // tiles] - (step % tiles) * MID_ROWS,
            split_lens[0] - extra * MID_ROWS,
        )
    )
    three_table = jnp.concatenate(
        (whole_table, split * tiles + jnp.arange(tiles, dtype=jnp.int32))
    )
    gain_one, shift_one = row(first_norm_gain), row(first_norm_bias)

    def sequences(pieces):
        return [piece.reshape(-1, length, columns) for piece in pieces]

    *own_heads, low = project(
        three_table,
        flat_tokens,
        gain_one,
        shift_one,
        down_low,
        up_own,
        query_key_value_weight,
    )
    own_heads = sequences(own_heads)
    qkv_near = after(qkv_near, own_heads[0])
    qkv_far = core_swap(qkv_near)
    out_near = swap(after(core_half(attention_output_weight, 0), qkv_near))
    up_near = swap(after(core_half(feedforward_up_weight, 1), qkv_near))
    attended_own, lse_own = attention_forward(three_lens, *own_heads)
    sent = lax.dynamic_slice_in_dim(attended_own[whole], (1 - me) * half, half, 0)
    attended_got = swap(core_order(sent, 1))
    qkv_far = after(qkv_far, attended_own)
    down_near = swap(after(core_half(feedforward_down_weight, 0), qkv_far))
    qkv = (query_key_value_weight, qkv_near, qkv_far)
    *far_heads, _ = project(
        whole_table,
        flat_tokens,
        gain_one,
        shift_one,
        down_low,
        up_other,
        qkv_near,
        qkv_far,
    )
    far_heads = sequences(far_heads)
    out_far = core_swap(after(out_near, far_heads[0]))
    up_far = core_swap(after(up_near, far_heads[0]))
    attended_far, lse_far = attention_forward(own_lens, *far_heads)
    down_far = core_swap(after(down_near, attended_far))
    far_all = jnp.concatenate((attended_far.reshape(-1, columns), attended_got), axis=0)
    weights = (
        attention_output_weight,
        out_near,
        out_far,
        feedforward_up_weight,
        up_near,
        up_far,
        feedforward_down_weight,
        down_near,
        down_far,
    )
    middle_table = jnp.stack(
        (token_table, own_table, live_table, jnp.arange(token_table.shape[0], dtype=jnp.int32))
    )

    def run_middle(first, last):
        return middle(
            middle_table[:, first:last],
            flat_tokens,
            flat_cotangent,
            attended_own.reshape(-1, columns),
            far_all,
            row(attention_output_bias),
            row(second_norm_gain),
            row(second_norm_bias),
            up_bias,
            row(feedforward_down_bias),
            weights,
        )

    block_zero, resid_zero, *grads_zero = run_middle(0, tiles)
    block_zero_got = swap(block_zero)
    block_rest, resid_rest, *grads_rest = run_middle(tiles, token_table.shape[0])
    grad_got = swap(core_order(grads_rest[1][length:], 1))
    block_rest_got = swap(block_rest)
    grad_kept = grads_rest[0][length:]
    grad_split = jnp.concatenate(
        (jnp.where(me == 0, grad_kept, grad_got), jnp.where(me == 0, grad_got, grad_kept))
    )

    def flat(pieces):
        return [piece.reshape(-1, columns) for piece in pieces]

    def back_whole(index, grads):
        lens = own_lens[index : index + 1]
        own = attention_backward(lens, *own_heads, grads[0], lse_own, index)
        far = attention_backward(lens, *far_heads, grads[1], lse_far, index)
        return flat(own), flat(far)

    span = jnp.arange(tiles, dtype=jnp.int32)

    def back_first(own, far, table, resid_grad):
        return first_backward(
            table,
            flat_tokens,
            resid_grad,
            low,
            own,
            far,
            gain_one,
            shift_one,
            down_low,
            up_both,
            qkv,
        )

    def whole_rows(index):
        at = index * tiles + span
        return jnp.stack((token_table[at], span, at, span, live_table[at]))

    back_zero = back_whole(0, grads_zero)
    split_own = attention_backward(split_lens, *own_heads, grad_split, lse_own, whole)
    split_sent = jnp.stack(
        [lax.dynamic_slice_in_dim(p[0], (1 - me) * half, half, 0) for p in split_own]
    )
    split_got = swap(core_order(split_sent, 2))
    first_zero = back_first(*back_zero, whole_rows(0), resid_zero)
    send_zero = swap(first_zero[0])
    back_one = back_whole(1, grads_rest)
    first_split = back_first(
        flat(split_own),
        [split_got[i] for i in range(3)],
        jnp.stack(
            (
                split * tiles + extra,
                tiles + extra - me * half_tiles,
                whole * tiles + extra,
                extra,
                split_lens[0] - extra * MID_ROWS,
            )
        ),
        resid_rest,
    )
    send_split = swap(first_split[0])
    first_one = back_first(*back_one, whole_rows(1), resid_rest)
    send_one = swap(first_one[0])

    down_sum, query_sum, value_sum = (
        first_zero[i] + first_split[i] + first_one[i] for i in range(1, 4)
    )
    up_sum = 8.0 * jnp.concatenate((query_sum[:rank], value_sum[rank:]))
    up_mine = up_sum[:, :columns]
    up_theirs = core_order(up_sum[:, columns:], 1)
    up_sum = jnp.concatenate(
        (jnp.where(me == 0, up_mine, up_theirs), jnp.where(me == 0, up_theirs, up_mine)), axis=1
    )
    live_row = jnp.full((8, width), jnp.sum(lengths).astype(f32))
    total = sum_all(jnp.concatenate((down_sum, up_sum, live_row)))
    active = total[-1, 0] / 2
    grad_down = total[: 2 * rank].reshape(2, rank, width).transpose(0, 2, 1) / active
    grad_up = total[2 * rank : 4 * rank].reshape(2, rank, width) / active

    def place(pieces):
        out = jnp.zeros((seqs * length, width), bf16)
        for piece, start in pieces:
            out = lax.dynamic_update_slice_in_dim(out, piece, start, 0)
        return out.reshape(tokens.shape)

    here = split * length + half * me
    there = split * length + half * (1 - me)
    block_out = place(
        (
            (block_zero, mine[0] * length),
            (block_rest[:length], mine[1] * length),
            (block_rest[length:], here),
            (block_zero_got, theirs[0] * length),
            (block_rest_got[:length], theirs[1] * length),
            (block_rest_got[length:], there),
        )
    )
    input_grad = place(
        (
            (first_zero[0], mine[0] * length),
            (first_split[0], here),
            (first_one[0], mine[1] * length),
            (send_zero, theirs[0] * length),
            (send_split, there),
            (send_one, theirs[1] * length),
        )
    )
    new_down = adam_decay_update(
        adapter_down_factor, grad_down, down_first_moment, down_second_moment
    )
    new_up = adam_decay_update(adapter_up_factor, grad_up, up_first_moment, up_second_moment)
    return (
        block_out,
        input_grad,
        new_down[0],
        new_up[0],
        new_down[1],
        new_up[1],
        new_down[2],
        new_up[2],
    )


def solution(mesh):
    in_specs = (
        P("dp", None, None),
        P("dp", None, None),
        P("dp"),
        P(),
        P(),
        P(None, None, "mp"),
        P("mp", None),
        P(),
        P(),
        P(),
        P(None, "mp"),
        P("mp"),
        P("mp", None),
        P(),
        P(),
        P(),
        P(),
        P(),
        P(),
        P(),
    )
    out_specs = (P("dp", None, None), P("dp", None, None), P(), P(), P(), P(), P(), P())
    return jax.shard_map(
        per_device_pair if mesh.shape["mp"] == 2 else per_device,
        mesh=mesh,
        in_specs=in_specs,
        out_specs=out_specs,
        check_vma=False,
    )
```

```python
import functools

import jax
import jax.numpy as jnp
from jax import lax
from jax.experimental import pallas as pl
from jax.experimental.pallas import tpu as pltpu
from jax.sharding import PartitionSpec as P

HEAD = 64


def layer_norm(values, norm_gain, norm_shift):
    centre = values - jnp.mean(values, axis=-1, keepdims=True)
    spread = jnp.mean(centre * centre, axis=-1, keepdims=True)
    return centre * lax.rsqrt(spread + 1e-05) * norm_gain + norm_shift


def gelu_tanh(values):
    return (
        0.5
        * values
        * (1.0 + jnp.tanh(0.7978845608028654 * (values + 0.044715 * values * values * values)))
    )


def head_major(matrix, seq_rows, head_count):
    return (
        matrix.reshape(seq_rows, -1, head_count, HEAD)
        .transpose(0, 2, 1, 3)
        .reshape(seq_rows * head_count, -1, HEAD)
    )


def token_major(stacked, seq_rows, head_count):
    return (
        stacked.reshape(seq_rows, head_count, -1, HEAD)
        .transpose(0, 2, 1, 3)
        .reshape(-1, head_count * HEAD)
    )


def masked_scores(query_rows, key_rows, seq_len):
    scores = jnp.einsum(
        "qd,kd->qk", query_rows, key_rows, preferred_element_type=jnp.float32
    ) * HEAD ** (-0.5)
    position = jnp.arange(scores.shape[0])
    allowed = (position[None, :] <= position[:, None]) & (position[None, :] < seq_len)
    return jnp.where(allowed, scores, -1e30)


def attend_forward(pieces):
    query_rows, key_rows, value_token_rows, seq_len = pieces
    scores = masked_scores(query_rows, key_rows, seq_len)
    row_max = jnp.max(scores, axis=-1, keepdims=True)
    weights = jnp.exp(scores - row_max)
    row_sum = jnp.sum(weights, axis=-1, keepdims=True)
    probabilities = (weights / row_sum).astype(jnp.bfloat16)
    head_out = jnp.dot(probabilities, value_token_rows, preferred_element_type=jnp.float32)
    return (head_out, row_max[:, 0] + jnp.log(row_sum[:, 0]))


def attend_backward(pieces):
    query_rows, key_rows, value_token_rows, seq_len, grad_head, log_sums = pieces
    scores = masked_scores(query_rows, key_rows, seq_len)
    probabilities = jnp.exp(scores - log_sums[:, None])
    value_gradient_rows = jnp.einsum(
        "qk,qd->kd",
        probabilities.astype(jnp.bfloat16),
        grad_head,
        preferred_element_type=jnp.float32,
    )
    grad_probs = jnp.einsum(
        "qd,kd->qk", grad_head, value_token_rows, preferred_element_type=jnp.float32
    )
    grad_scores = probabilities * (
        grad_probs - jnp.sum(grad_probs * probabilities, axis=-1, keepdims=True)
    )
    grad_scores = grad_scores.astype(jnp.bfloat16)
    query_gradient_rows = jnp.dot(
        grad_scores, key_rows, preferred_element_type=jnp.float32
    ) * HEAD ** (-0.5)
    grad_keys = jnp.einsum(
        "qk,qd->kd", grad_scores, query_rows, preferred_element_type=jnp.float32
    ) * HEAD ** (-0.5)
    return (query_gradient_rows, grad_keys, value_gradient_rows)


def adam_decay_update(adapter, gradient, first_mom, second_mom):
    first_new = 0.9 * first_mom + 0.1 * gradient
    second_new = 0.999 * second_mom + 0.001 * gradient * gradient
    update = first_new / (1.0 - 0.9**10) / (jnp.sqrt(second_new / (1.0 - 0.999**10)) + 1e-08)
    return (adapter - 0.25 * (update + 0.01 * adapter), first_new, second_new)


def per_device(
    tokens,
    cotangent,
    lengths,
    first_norm_gain,
    first_norm_bias,
    query_key_value_weight,
    attention_output_weight,
    attention_output_bias,
    second_norm_gain,
    second_norm_bias,
    feedforward_up_weight,
    feedforward_up_bias,
    feedforward_down_weight,
    feedforward_down_bias,
    adapter_down_factor,
    adapter_up_factor,
    down_first_moment,
    up_first_moment,
    down_second_moment,
    up_second_moment,
):
    seq_rows, seq_len_all, model_width = tokens.shape
    tok_count = seq_rows * seq_len_all
    groups = lax.axis_size("mp")
    worker_shard = lax.axis_index("mp")
    shard_width = query_key_value_weight.shape[2]
    head_count = shard_width // HEAD
    adapter_rank_size = adapter_down_factor.shape[2]
    tokens_f32 = tokens.reshape(tok_count, model_width).astype(jnp.float32)
    normalized_rows = layer_norm(tokens_f32, first_norm_gain, first_norm_bias).astype(jnp.bfloat16)
    down_reduced = adapter_down_factor.astype(jnp.bfloat16)
    up_reduced = adapter_up_factor.astype(jnp.bfloat16)
    up_columns = lax.dynamic_slice_in_dim(up_reduced, worker_shard * shard_width, shard_width, 2)
    down_pair = jnp.concatenate((down_reduced[0], down_reduced[1]), axis=1)
    adapter_pair = jnp.dot(normalized_rows, down_pair, preferred_element_type=jnp.float32).astype(
        jnp.bfloat16
    )
    adapter_query_delta = adapter_pair[:, :adapter_rank_size]
    adapter_value_delta = adapter_pair[:, adapter_rank_size:]
    query_rows = (
        jnp.dot(normalized_rows, query_key_value_weight[0], preferred_element_type=jnp.float32)
        + 8.0 * jnp.dot(adapter_query_delta, up_columns[0], preferred_element_type=jnp.float32)
    ).astype(jnp.bfloat16)
    key_rows = jnp.dot(
        normalized_rows, query_key_value_weight[1], preferred_element_type=jnp.float32
    ).astype(jnp.bfloat16)
    value_token_rows = (
        jnp.dot(normalized_rows, query_key_value_weight[2], preferred_element_type=jnp.float32)
        + 8.0 * jnp.dot(adapter_value_delta, up_columns[1], preferred_element_type=jnp.float32)
    ).astype(jnp.bfloat16)
    limits = jnp.repeat(lengths, head_count)
    query_heads = head_major(query_rows, seq_rows, head_count)
    key_heads = head_major(key_rows, seq_rows, head_count)
    value_heads = head_major(value_token_rows, seq_rows, head_count)
    head_out, log_sums = lax.map(attend_forward, (query_heads, key_heads, value_heads, limits))
    attended = token_major(head_out, seq_rows, head_count).astype(jnp.bfloat16)
    attn_share = (
        lax.psum_scatter(
            jnp.dot(attended, attention_output_weight, preferred_element_type=jnp.float32),
            "mp",
            scatter_dimension=0,
            tiled=True,
        )
        + attention_output_bias
    )

    def norm_two(values):
        return layer_norm(values, second_norm_gain, second_norm_bias)

    def norm_one(values):
        return layer_norm(values, first_norm_gain, first_norm_bias)

    attn_full = lax.all_gather(attn_share, "mp", axis=0, tiled=True)
    residual = tokens_f32 + attn_full
    normed_two = norm_two(residual).astype(jnp.bfloat16)
    hidden_pre = (
        jnp.dot(normed_two, feedforward_up_weight, preferred_element_type=jnp.float32)
        + feedforward_up_bias
    )
    hidden = gelu_tanh(hidden_pre).astype(jnp.bfloat16)
    mlp_share = (
        lax.psum_scatter(
            jnp.dot(hidden, feedforward_down_weight, preferred_element_type=jnp.float32).astype(
                jnp.bfloat16
            ),
            "mp",
            scatter_dimension=0,
            tiled=True,
        ).astype(jnp.float32)
        + feedforward_down_bias
    )
    mlp_full = lax.all_gather(mlp_share.astype(jnp.bfloat16), "mp", axis=0, tiled=True).astype(
        mlp_share.dtype
    )
    block_out = (residual + mlp_full).astype(jnp.bfloat16)
    live_mask = (jnp.arange(seq_len_all)[None, :] < lengths[:, None]).reshape(tok_count, 1)
    grad_out = jnp.where(
        live_mask, cotangent.reshape(tok_count, model_width), jnp.zeros((), jnp.bfloat16)
    )
    grad_hidden = jnp.einsum(
        "td,fd->tf", grad_out, feedforward_down_weight, preferred_element_type=jnp.float32
    )
    _, gelu_back = jax.vjp(gelu_tanh, hidden_pre)
    grad_pre = gelu_back(grad_hidden)[0].astype(jnp.bfloat16)
    grad_norm2_share = lax.psum_scatter(
        jnp.einsum(
            "tf,df->td", grad_pre, feedforward_up_weight, preferred_element_type=jnp.float32
        ),
        "mp",
        scatter_dimension=0,
        tiled=True,
    )
    grad_norm2 = lax.all_gather(grad_norm2_share, "mp", axis=0, tiled=True)
    _, norm2_back = jax.vjp(norm_two, residual)
    grad_resid = grad_out.astype(jnp.float32) + norm2_back(grad_norm2)[0]
    grad_resid_low = grad_resid.astype(jnp.bfloat16)
    grad_attended = jnp.einsum(
        "td,ed->te", grad_resid_low, attention_output_weight, preferred_element_type=jnp.float32
    ).astype(jnp.bfloat16)
    grad_head = head_major(grad_attended, seq_rows, head_count)
    head_dq, head_dk, head_dv = lax.map(
        attend_backward, (query_heads, key_heads, value_heads, limits, grad_head, log_sums)
    )
    query_gradient_rows = token_major(head_dq, seq_rows, head_count).astype(jnp.bfloat16)
    grad_keys = token_major(head_dk, seq_rows, head_count).astype(jnp.bfloat16)
    value_gradient_rows = token_major(head_dv, seq_rows, head_count).astype(jnp.bfloat16)
    adapter_query_gradient = 8.0 * jnp.einsum(
        "te,re->tr", query_gradient_rows, up_columns[0], preferred_element_type=jnp.float32
    )
    adapter_value_gradient = 8.0 * jnp.einsum(
        "te,re->tr", value_gradient_rows, up_columns[1], preferred_element_type=jnp.float32
    )
    adapter_gradient = jnp.concatenate((adapter_query_gradient, adapter_value_gradient), axis=1)
    down_pair_float32 = down_pair.astype(jnp.float32)
    partial_sum = jnp.einsum(
        "te,de->td",
        query_gradient_rows,
        query_key_value_weight[0],
        preferred_element_type=jnp.float32,
    )
    partial_sum = partial_sum + jnp.einsum(
        "te,de->td", grad_keys, query_key_value_weight[1], preferred_element_type=jnp.float32
    )
    partial_sum = partial_sum + jnp.einsum(
        "te,de->td",
        value_gradient_rows,
        query_key_value_weight[2],
        preferred_element_type=jnp.float32,
    )
    grad_norm1_share = lax.psum_scatter(
        partial_sum
        + jnp.einsum(
            "gy,wy->gw", adapter_gradient, down_pair_float32, precision=lax.Precision.HIGHEST
        ),
        "mp",
        scatter_dimension=0,
        tiled=True,
    )
    grad_down_both = jnp.einsum(
        "fi,fg->ig",
        normalized_rows.astype(jnp.float32),
        adapter_gradient,
        precision=lax.Precision.HIGHEST,
    )
    grad_down = jnp.stack(
        (grad_down_both[:, :adapter_rank_size], grad_down_both[:, adapter_rank_size:])
    )
    grad_up_query = 8.0 * jnp.einsum(
        "zm,zj->mj", adapter_query_delta, query_gradient_rows, preferred_element_type=jnp.float32
    )
    grad_up_value = 8.0 * jnp.einsum(
        "zm,zj->mj", adapter_value_delta, value_gradient_rows, preferred_element_type=jnp.float32
    )
    up_column_gradient = jnp.stack((grad_up_query, grad_up_value))
    grad_up = lax.dynamic_update_slice_in_dim(
        jnp.zeros(adapter_up_factor.shape, jnp.float32),
        up_column_gradient,
        worker_shard * shard_width,
        2,
    )
    live_local = jnp.sum(lengths).astype(jnp.float32)
    down_reduced_sum, up_reduced_sum, live_sum = lax.psum(
        (grad_down, grad_up, live_local), ("dp", "mp")
    )
    active_token_total = live_sum / groups
    grad_norm1 = lax.all_gather(grad_norm1_share, "mp", axis=0, tiled=True)
    _, norm1_back = jax.vjp(norm_one, tokens_f32)
    input_grad = (grad_resid + norm1_back(grad_norm1)[0]).astype(jnp.bfloat16)
    down_factor_next, down_first_moment_next, down_second_moment_next = adam_decay_update(
        adapter_down_factor,
        down_reduced_sum / active_token_total,
        down_first_moment,
        down_second_moment,
    )
    up_factor_next, up_first_moment_next, up_second_moment_next = adam_decay_update(
        adapter_up_factor, up_reduced_sum / active_token_total, up_first_moment, up_second_moment
    )
    return (
        block_out.reshape(seq_rows, seq_len_all, model_width),
        input_grad.reshape(seq_rows, seq_len_all, model_width),
        down_factor_next,
        up_factor_next,
        down_first_moment_next,
        up_first_moment_next,
        down_second_moment_next,
        up_second_moment_next,
    )


TILE = 256
NT = (((1,), (1,)), ((), ()))


def head_lanes(half):
    lane = lax.broadcasted_iota(jnp.int32, (1, 2 * HEAD), 1)
    return (lane >= half * HEAD) & (lane < (half + 1) * HEAD)


def one_head(block, half):
    return jnp.where(head_lanes(half), block, jnp.zeros((), block.dtype))


def edge_allowed(key_start, query_start, seq_len):
    key_at = key_start + lax.broadcasted_iota(jnp.int32, (TILE, TILE), 0)
    query_at = query_start + lax.broadcasted_iota(jnp.int32, (TILE, TILE), 1)
    return (key_at <= query_at) & (key_at < seq_len)


def attention_forward_kernel(lens_ref, q_ref, k_ref, v_ref, out_ref, lse_ref, vt_ref):
    seq_len = lens_ref[pl.program_id(0)]
    live_tiles = (seq_len + TILE - 1) // TILE
    vt_ref[...] = v_ref[0].T
    tiles = q_ref.shape[1] // TILE

    def row_tile(tile, extent):
        rows = pl.ds(tile * TILE, TILE)
        inner = (extent - 1) * TILE
        query = both_heads(q_ref[0, rows, :] * HEAD ** (-0.5))
        allowed = edge_allowed(inner, tile * TILE, seq_len)
        allowed = jnp.concatenate((allowed, allowed), axis=1)
        scores = []
        for span in range(extent):
            part = lax.dot_general(
                k_ref[0, pl.ds(span * TILE, TILE), :],
                query,
                NT,
                preferred_element_type=jnp.float32,
            )
            if span == extent - 1:
                part = jnp.where(allowed, part, -1e30)
            scores.append(part)
        top = functools.reduce(
            jnp.maximum, [jnp.max(part, axis=0, keepdims=True) for part in scores]
        )
        total, outs = 0.0, [0.0, 0.0]
        for span, part in enumerate(scores):
            part = jnp.exp(part - top)
            total = total + jnp.sum(part, axis=0, keepdims=True)
            part = part.astype(jnp.bfloat16)
            for half in range(2):
                outs[half] = outs[half] + jnp.dot(
                    vt_ref[pl.ds(half * HEAD, HEAD), pl.ds(span * TILE, TILE)],
                    part[:, half * TILE : (half + 1) * TILE],
                    preferred_element_type=jnp.float32,
                )
        lse = top + jnp.log(total)
        scale = 1.0 / total
        for half in range(2):
            columns = slice(half * TILE, (half + 1) * TILE)
            outs[half] = outs[half] * scale[:, columns]
            lse_ref[0, 0, pl.ds(half, 1), rows] = lse[:, columns]
        out_ref[0, rows, :] = jnp.concatenate(outs, axis=0).T.astype(out_ref.dtype)

    for tile in range(tiles):
        for extent in range(1, tile + 2):
            pl.when(jnp.minimum(live_tiles, tile + 1) == extent)(
                lambda tile=tile, extent=extent: row_tile(tile, extent)
            )


def attention_forward(lens, query, key, value):
    seqs, length, width = query.shape
    pairs = width // (2 * HEAD)
    spec = pl.BlockSpec((1, length, 2 * HEAD), lambda s, h, lens: (s, 0, h))
    return pl.pallas_call(
        attention_forward_kernel,
        grid_spec=pltpu.PrefetchScalarGridSpec(
            num_scalar_prefetch=1,
            grid=(seqs, pairs),
            in_specs=[spec] * 3,
            out_specs=[spec, pl.BlockSpec((1, 1, 2, length), lambda s, h, lens: (s, h, 0, 0))],
            scratch_shapes=[pltpu.VMEM((2 * HEAD, length), jnp.bfloat16)],
        ),
        out_shape=[
            jax.ShapeDtypeStruct(query.shape, jnp.bfloat16),
            jax.ShapeDtypeStruct((seqs, pairs, 2, length), jnp.float32),
        ],
        cost_estimate=pl.CostEstimate(
            flops=seqs * width * length * length * 3,
            bytes_accessed=seqs * width * length * 8,
            transcendentals=seqs * pairs * length * length,
        ),
        name="attention_forward",
    )(lens, query, key, value)


def both_heads(block):
    return jnp.concatenate((one_head(block, 0), one_head(block, 1)), axis=0)


def attention_backward_kernel(
    lens_ref,
    q_ref,
    k_ref,
    v_ref,
    g_ref,
    out_ref,
    lse_ref,
    dq_ref,
    dk_ref,
    dv_ref,
    kt_ref,
    dk_acc,
    dv_acc,
):
    seq_len = lens_ref[pl.program_id(0)]
    kt_ref[...] = k_ref[0].T
    dk_acc[...] = jnp.zeros_like(dk_acc)
    dv_acc[...] = jnp.zeros_like(dv_acc)
    tiles = q_ref.shape[1] // TILE

    def row_tile(tile):
        rows = pl.ds(tile * TILE, TILE)
        query = both_heads(q_ref[0, rows, :] * HEAD ** (-0.5))
        grad = g_ref[rows, :]
        product = (grad.astype(jnp.float32) * out_ref[0, rows, :].astype(jnp.float32)).T
        grad = both_heads(grad)

        def head_pair(pick):
            return jnp.concatenate([pick(half) for half in range(2)], axis=1)

        lse = head_pair(lambda half: lse_ref[0, 0, pl.ds(half, 1), rows])
        row_dot = head_pair(
            lambda half: jnp.sum(
                product[half * HEAD : (half + 1) * HEAD], axis=0, keepdims=True
            )
        )
        allowed = edge_allowed(0, 0, seq_len - tile * TILE)
        allowed = jnp.concatenate((allowed, allowed), axis=1)
        outs = [0.0, 0.0]
        for span in range(tile + 1):
            keys = pl.ds(span * TILE, TILE)
            scores = lax.dot_general(
                k_ref[0, keys, :], query, NT, preferred_element_type=jnp.float32
            )
            if span == tile:
                scores = jnp.where(allowed, scores, -1e30)
            prob = jnp.exp(scores - lse)
            grad_prob = lax.dot_general(
                v_ref[0, keys, :], grad, NT, preferred_element_type=jnp.float32
            )
            grad_scores = (prob * (grad_prob - row_dot)).astype(jnp.bfloat16)
            dv_acc[keys, :] += jnp.dot(
                prob.astype(jnp.bfloat16), grad, preferred_element_type=jnp.float32
            )
            dk_acc[keys, :] += jnp.dot(grad_scores, query, preferred_element_type=jnp.float32)
            for half in range(2):
                outs[half] = outs[half] + jnp.dot(
                    kt_ref[pl.ds(half * HEAD, HEAD), keys],
                    grad_scores[:, half * TILE : (half + 1) * TILE],
                    preferred_element_type=jnp.float32,
                )
        dq = jnp.concatenate(outs, axis=0).T * HEAD ** (-0.5)
        dq_ref[0, rows, :] = dq.astype(dq_ref.dtype)

    for tile in range(tiles):
        pl.when(tile * TILE < seq_len)(lambda tile=tile: row_tile(tile))

        @pl.when(tile * TILE >= seq_len)
        def _(tile=tile):
            dq_ref[0, pl.ds(tile * TILE, TILE), :] = jnp.zeros((TILE, 2 * HEAD), dq_ref.dtype)

    dk_ref[0] = dk_acc[...].astype(dk_ref.dtype)
    dv_ref[0] = dv_acc[...].astype(dv_ref.dtype)


def attention_backward(lens, query, key, value, grad, out, lse, start):
    length, width = query.shape[1:]
    seqs = lens.shape[0]
    pairs = width // (2 * HEAD)

    def block(first):
        return pl.BlockSpec((1, length, 2 * HEAD), lambda s, h, lens: (s + first, 0, h))

    return pl.pallas_call(
        attention_backward_kernel,
        grid_spec=pltpu.PrefetchScalarGridSpec(
            num_scalar_prefetch=1,
            grid=(seqs, pairs),
            in_specs=[block(start)] * 3
            + [
                pl.BlockSpec((length, 2 * HEAD), lambda s, h, lens: (s, h)),
                block(start),
                pl.BlockSpec((1, 1, 2, length), lambda s, h, lens: (s + start, h, 0, 0)),
            ],
            out_specs=[block(0)] * 3,
            scratch_shapes=[
                pltpu.VMEM((2 * HEAD, length), jnp.bfloat16),
                pltpu.VMEM((length, 2 * HEAD), jnp.float32),
                pltpu.VMEM((length, 2 * HEAD), jnp.float32),
            ],
        ),
        out_shape=[jax.ShapeDtypeStruct((seqs, length, width), jnp.bfloat16)] * 3,
        cost_estimate=pl.CostEstimate(
            flops=seqs * width * length * length * 7,
            bytes_accessed=seqs * width * length * 14,
            transcendentals=seqs * pairs * length * length,
        ),
        name="attention_backward",
    )(lens, query, key, value, grad, out, lse)


MID_ROWS = 256
CHUNK = 1024


def centred(values):
    centre = values - jnp.mean(values, axis=-1, keepdims=True)
    inverse = lax.rsqrt(jnp.mean(centre * centre, axis=-1, keepdims=True) + 1e-05)
    return centre * inverse, inverse


def norm_backward(grad, gain, normal, inverse):
    grad = grad * gain
    mean = jnp.mean(grad, axis=-1, keepdims=True)
    along = jnp.mean(grad * normal, axis=-1, keepdims=True)
    return (grad - mean - normal * along) * inverse


def dot(a, b):
    return jnp.dot(a, b, preferred_element_type=jnp.float32)


def dot_t(a, b):
    return lax.dot_general(a, b, NT, preferred_element_type=jnp.float32)


def copies_of(pairs, sems):
    return [pltpu.make_async_copy(a, b, sems.at[i]) for i, (a, b) in enumerate(pairs)]


def middle_kernel(
    table_ref,
    tokens_ref,
    cotangent_ref,
    attended_own,
    attended_far,
    out_bias_ref,
    gain_ref,
    shift_ref,
    up_bias_ref,
    down_bias_ref,
    out_own,
    out_near,
    out_far,
    up_own,
    up_near,
    up_far,
    down_own,
    down_near,
    down_far,
    block_ref,
    resid_grad_ref,
    own_grad_ref,
    far_grad_ref,
    out_w,
    up_w,
    down_w,
    residual_ref,
    normed_ref,
    normal_ref,
    acc_ref,
    grad_acc_ref,
    sems,
):
    step = pl.program_id(0)

    pairs = []
    start = 0
    for piece in (out_own, out_near, out_far):
        rows = piece.shape[0]
        pairs.append((piece, out_w.at[pl.ds(start, rows), :]))
        start += rows
    chunk = 0
    for up, down in ((up_own, down_own), (up_near, down_near), (up_far, down_far)):
        for at in range(up.shape[1] // CHUNK):
            units = pl.ds(at * CHUNK, CHUNK)
            pairs.append((up.at[:, units], up_w.at[chunk]))
            pairs.append((down.at[units, :], down_w.at[chunk]))
            chunk += 1
    loads = copies_of(pairs, sems)

    @pl.when(step == 0)
    def _():
        for load in loads:
            load.start()
        for load in loads[:3]:
            load.wait()

    live = table_ref[2, step]
    residual = tokens_ref[...].astype(jnp.float32) + (
        dot(jnp.concatenate((attended_own[...], attended_far[...]), axis=1), out_w[...])
        + out_bias_ref[...]
    )
    residual_ref[...] = residual
    normal, inverse = centred(residual)
    normal_ref[...] = normal
    normed_ref[...] = (normal * gain_ref[...] + shift_ref[...]).astype(jnp.bfloat16)
    acc_ref[...] = jnp.zeros_like(acc_ref)

    @pl.when(step == 0)
    def _():
        for load in loads[3:]:
            load.wait()

    scale = 0.7978845608028654
    cube = 0.044715 * scale

    def forward_only(chunk, carry):
        pre = dot(normed_ref[...], up_w[chunk]) + up_bias_ref[chunk]
        tanh = jnp.tanh(pre * (scale + cube * (pre * pre)))
        hidden = (pre * (0.5 + 0.5 * tanh)).astype(jnp.bfloat16)
        acc_ref[...] += dot(hidden, down_w[chunk])
        return carry

    def finish():
        block_ref[...] = (residual_ref[...] + acc_ref[...] + down_bias_ref[...]).astype(
            block_ref.dtype
        )

    @pl.when(live > 0)
    def _():
        row = lax.broadcasted_iota(jnp.int32, (MID_ROWS, 1), 0)
        grad_out = jnp.where(row < live, cotangent_ref[...], jnp.zeros((), jnp.bfloat16))
        grad_acc_ref[...] = jnp.zeros_like(grad_acc_ref)

        def both_ways(chunk, carry):
            pre = dot(normed_ref[...], up_w[chunk]) + up_bias_ref[chunk]
            grad_hidden = dot_t(grad_out, down_w[chunk])
            square = pre * pre
            tanh = jnp.tanh(pre * (scale + cube * square))
            gate = 0.5 + 0.5 * tanh
            hidden = (pre * gate).astype(jnp.bfloat16)
            slope = gate + (pre * (0.5 - 0.5 * (tanh * tanh))) * (scale + 3.0 * cube * square)
            grad_pre = (grad_hidden * slope).astype(jnp.bfloat16)
            acc_ref[...] += dot(hidden, down_w[chunk])
            grad_acc_ref[...] += dot_t(grad_pre, up_w[chunk])
            return carry

        lax.fori_loop(0, up_w.shape[0], both_ways, 0, unroll=UNROLL)
        finish()
        grad_resid = grad_out.astype(jnp.float32) + norm_backward(
            grad_acc_ref[...], gain_ref[...], normal_ref[...], inverse
        )
        low = grad_resid.astype(jnp.bfloat16)
        resid_grad_ref[...] = low
        columns = own_grad_ref.shape[1]
        own_grad_ref[...] = dot_t(low, out_w[:columns]).astype(jnp.bfloat16)
        far_grad_ref[...] = dot_t(low, out_w[columns:]).astype(jnp.bfloat16)

    @pl.when(live <= 0)
    def _():
        lax.fori_loop(0, up_w.shape[0], forward_only, 0, unroll=UNROLL)
        finish()
        resid_grad_ref[...] = jnp.zeros_like(resid_grad_ref)
        own_grad_ref[...] = jnp.zeros_like(own_grad_ref)
        far_grad_ref[...] = jnp.zeros_like(far_grad_ref)


UNROLL = 2


def middle(
    table, tokens, cotangent, own, far, out_bias, gain, shift, up_bias, down_bias, weights
):
    rows, width = table.shape[1] * MID_ROWS, tokens.shape[1]
    columns = far.shape[1]
    units = up_bias.shape[0] * up_bias.shape[2]
    tile = pl.BlockSpec((MID_ROWS, width), lambda i, t: (i, 0))
    picked = pl.BlockSpec((MID_ROWS, width), lambda i, t: (t[0, i], 0))
    part = pl.BlockSpec((MID_ROWS, columns), lambda i, t: (i, 0))
    vector = pl.BlockSpec((1, width), lambda i, t: (0, 0))
    chunks = units // CHUNK
    low = jax.ShapeDtypeStruct((rows, width), jnp.bfloat16)
    thin = jax.ShapeDtypeStruct((rows, columns), jnp.bfloat16)
    wide = pltpu.VMEM((MID_ROWS, width), jnp.float32)
    return pl.pallas_call(
        middle_kernel,
        grid_spec=pltpu.PrefetchScalarGridSpec(
            num_scalar_prefetch=1,
            grid=(rows // MID_ROWS,),
            in_specs=[picked] * 2
            + [pl.BlockSpec((MID_ROWS, columns), lambda i, t, a=a: (t[a, i], 0)) for a in (1, 3)]
            + [vector] * 3
            + [pl.BlockSpec(up_bias.shape, lambda i, t: (0, 0, 0)), vector]
            + [pl.BlockSpec(memory_space=pl.ANY)] * 9,
            out_specs=[tile, tile, part, part],
            scratch_shapes=[
                pltpu.VMEM((width, width), jnp.bfloat16),
                pltpu.VMEM((chunks, width, CHUNK), jnp.bfloat16),
                pltpu.VMEM((chunks, CHUNK, width), jnp.bfloat16),
                wide,
                pltpu.VMEM((MID_ROWS, width), jnp.bfloat16),
                wide,
                wide,
                wide,
                pltpu.SemaphoreType.DMA((3 + 2 * chunks,)),
            ],
        ),
        out_shape=[low, low, thin, thin],
        compiler_params=pltpu.CompilerParams(vmem_limit_bytes=56 << 20),
        cost_estimate=pl.CostEstimate(
            flops=rows * width * (units * 8 + width * 4),
            bytes_accessed=rows * width * 12 + units * width * 4,
            transcendentals=rows * units,
        ),
        name="middle",
    )(
        table,
        tokens,
        cotangent,
        own,
        far,
        out_bias,
        gain,
        shift,
        up_bias,
        down_bias,
        *weights,
    )


PROJECT_ROWS = 256


def qkv_loads(own, near, far, weight_ref, sems):
    pairs = []
    start = 0
    for piece in (own, near, far):
        if piece is not None:
            columns = pl.ds(start, piece.shape[2])
            pairs.append((piece, weight_ref.at[:, :, columns]))
            start += piece.shape[2]
    return copies_of(pairs, sems)


def project_kernel(pieces, table_ref, *refs):
    tokens_ref, gain_ref, shift_ref, down_ref, up_ref = refs[:5]
    weights = list(refs[5 : 5 + pieces]) + [None] * (3 - pieces)
    query_ref, key_ref, value_ref, low_ref, weight_ref, sems = refs[5 + pieces :]
    loads = qkv_loads(*weights, weight_ref, sems)
    first = pl.program_id(0) == 0

    @pl.when(first)
    def _():
        for load in loads:
            load.start()

    normal, _ = centred(tokens_ref[...].astype(jnp.float32))
    normed = (normal * gain_ref[...] + shift_ref[...]).astype(jnp.bfloat16)
    low = dot_t(normed, down_ref[...]).astype(jnp.bfloat16)
    low_ref[...] = low.astype(jnp.float32).T

    @pl.when(first)
    def _():
        for load in loads:
            load.wait()

    query_ref[...] = (dot(normed, weight_ref[0]) + 8.0 * dot(low, up_ref[0])).astype(jnp.bfloat16)
    key_ref[...] = dot(normed, weight_ref[1]).astype(jnp.bfloat16)
    value_ref[...] = (dot(normed, weight_ref[2]) + 8.0 * dot(low, up_ref[1])).astype(jnp.bfloat16)


def project(table, tokens, gain, shift, down, up, *weights):
    rows, width = table.shape[0] * PROJECT_ROWS, tokens.shape[1]
    columns = up.shape[2]
    pairs = down.shape[0]
    out = pl.BlockSpec((PROJECT_ROWS, columns), lambda i, t: (i, 0))
    vector = pl.BlockSpec((1, width), lambda i, t: (0, 0))
    return pl.pallas_call(
        functools.partial(project_kernel, len(weights)),
        grid_spec=pltpu.PrefetchScalarGridSpec(
            num_scalar_prefetch=1,
            grid=(rows // PROJECT_ROWS,),
            in_specs=[
                pl.BlockSpec((PROJECT_ROWS, width), lambda i, t: (t[i], 0)),
                vector,
                vector,
                pl.BlockSpec(down.shape, lambda i, t: (0, 0)),
                pl.BlockSpec(up.shape, lambda i, t: (0, 0, 0)),
            ]
            + [pl.BlockSpec(memory_space=pl.ANY)] * len(weights),
            out_specs=[out] * 3 + [pl.BlockSpec((pairs, PROJECT_ROWS), lambda i, t: (0, i))],
            scratch_shapes=[
                pltpu.VMEM((3, width, columns), jnp.bfloat16),
                pltpu.SemaphoreType.DMA((len(weights),)),
            ],
        ),
        out_shape=[jax.ShapeDtypeStruct((rows, columns), jnp.bfloat16)] * 3
        + [jax.ShapeDtypeStruct((pairs, rows), jnp.float32)],
        cost_estimate=pl.CostEstimate(
            flops=rows * width * columns * 6,
            bytes_accessed=rows * (width + 3 * columns) * 2 + 6 * width * columns,
            transcendentals=rows,
        ),
        name="project",
    )(table, tokens, gain, shift, down, up, *weights)


def first_backward_kernel(
    table_ref,
    tokens_ref,
    resid_grad_ref,
    low_ref,
    query_own,
    key_own,
    value_own,
    query_far,
    key_far,
    value_far,
    gain_ref,
    shift_ref,
    down_ref,
    up_ref,
    own_ref,
    near_ref,
    far_ref,
    input_ref,
    down_grad_ref,
    query_up_ref,
    value_up_ref,
    weight_ref,
    sems,
):
    first = pl.program_id(0) == 0
    loads = qkv_loads(own_ref, near_ref, far_ref, weight_ref, sems)

    @pl.when(first)
    def _():
        for load in loads:
            load.start()
        down_grad_ref[...] = jnp.zeros_like(down_grad_ref)
        query_up_ref[...] = jnp.zeros_like(query_up_ref)
        value_up_ref[...] = jnp.zeros_like(value_up_ref)

    normal, inverse = centred(tokens_ref[...].astype(jnp.float32))
    normed = (normal * gain_ref[...] + shift_ref[...]).astype(jnp.bfloat16)
    query = jnp.concatenate((query_own[...], query_far[...]), axis=1)
    key = jnp.concatenate((key_own[...], key_far[...]), axis=1)
    value = jnp.concatenate((value_own[...], value_far[...]), axis=1)
    adapter = 8.0 * (dot_t(query, up_ref[0]) + dot_t(value, up_ref[1]))
    high = adapter.astype(jnp.bfloat16)
    rest = (adapter - high.astype(jnp.float32)).astype(jnp.bfloat16)
    down_grad_ref[...] += dot(high.astype(jnp.float32).T.astype(jnp.bfloat16), normed) + dot(
        rest.astype(jnp.float32).T.astype(jnp.bfloat16), normed
    )
    low = low_ref[...].astype(jnp.bfloat16)
    query_up_ref[...] += dot(low, query)
    value_up_ref[...] += dot(low, value)

    @pl.when(first)
    def _():
        for load in loads:
            load.wait()

    grad = (
        dot_t(query, weight_ref[0])
        + dot_t(key, weight_ref[1])
        + dot_t(value, weight_ref[2])
        + dot(high, down_ref[...])
        + dot(rest, down_ref[...])
    )
    input_ref[...] = (
        resid_grad_ref[...].astype(jnp.float32)
        + norm_backward(grad, gain_ref[...], normal, inverse)
    ).astype(input_ref.dtype)


def first_backward(
    table, tokens, resid_grad, low, own, far, gain, shift, down, up, weights
):
    tiles = table.shape[1]
    rows, width = tiles * PROJECT_ROWS, tokens.shape[1]
    pairs = down.shape[0]
    columns = own[0].shape[1]
    tile = pl.BlockSpec((PROJECT_ROWS, width), lambda i, t: (t[0, i], 0))
    vector = pl.BlockSpec((1, width), lambda i, t: (0, 0))
    small = pl.BlockSpec((pairs, width), lambda i, t: (0, 0))
    sums = jax.ShapeDtypeStruct((pairs, width), jnp.float32)
    return pl.pallas_call(
        first_backward_kernel,
        grid_spec=pltpu.PrefetchScalarGridSpec(
            num_scalar_prefetch=1,
            grid=(tiles,),
            in_specs=[
                tile,
                pl.BlockSpec((PROJECT_ROWS, width), lambda i, t: (t[1, i], 0)),
                pl.BlockSpec((pairs, PROJECT_ROWS), lambda i, t: (0, t[2, i])),
            ]
            + [pl.BlockSpec((PROJECT_ROWS, columns), lambda i, t: (t[3, i], 0))] * 3
            + [pl.BlockSpec((PROJECT_ROWS, columns), lambda i, t: (i, 0))] * 3
            + [vector, vector, small, pl.BlockSpec(up.shape, lambda i, t: (0, 0, 0))]
            + [pl.BlockSpec(memory_space=pl.ANY)] * 3,
            out_specs=[pl.BlockSpec((PROJECT_ROWS, width), lambda i, t: (i, 0))] + [small] * 3,
            scratch_shapes=[
                pltpu.VMEM((3, width, width), jnp.bfloat16),
                pltpu.SemaphoreType.DMA((3,)),
            ],
        ),
        out_shape=[jax.ShapeDtypeStruct((rows, width), jnp.bfloat16)] + [sums] * 3,
        cost_estimate=pl.CostEstimate(
            flops=rows * width * width * 7,
            bytes_accessed=rows * width * 12 + 6 * width * width,
            transcendentals=rows,
        ),
        name="first_backward",
    )(table, tokens, resid_grad, low, *own, *far, gain, shift, down, up, *weights)


def swap(value):
    return lax.ppermute(value, "mp", [(0, 1), (1, 0)])


def after(value, *earlier):
    return lax.optimization_barrier((value, *earlier))[0]


def core_swap(value):
    return lax.ppermute(value, "dp", [(i, i ^ 1) for i in range(lax.axis_size("dp"))])


def core_half(shard, axis):
    size = shard.shape[axis] // 2
    core = lax.rem(lax.axis_index("dp"), 2)
    return lax.dynamic_slice_in_dim(shard, core * size, size, axis)


def core_order(value, axis):
    size = value.shape[axis] // 2
    core = lax.rem(lax.axis_index("dp"), 2)
    low = lax.slice_in_dim(value, 0, size, axis=axis)
    high = lax.slice_in_dim(value, size, 2 * size, axis=axis)
    return jnp.where(
        core == 0, value, jnp.concatenate((high, low), axis=axis)
    )


def sum_all(value):
    count = lax.axis_size("dp")
    if count & (count - 1):
        return lax.psum(value, ("dp", "mp"))
    bit = 1
    while bit < count:
        value = value + lax.ppermute(value, "dp", [(i, i ^ bit) for i in range(count)])
        bit *= 2
    return value + swap(value)


def per_device_pair(
    tokens,
    cotangent,
    lengths,
    first_norm_gain,
    first_norm_bias,
    query_key_value_weight,
    attention_output_weight,
    attention_output_bias,
    second_norm_gain,
    second_norm_bias,
    feedforward_up_weight,
    feedforward_up_bias,
    feedforward_down_weight,
    feedforward_down_bias,
    adapter_down_factor,
    adapter_up_factor,
    down_first_moment,
    up_first_moment,
    down_second_moment,
    up_second_moment,
):
    return pair_step(tokens, cotangent, lengths, first_norm_gain, first_norm_bias, query_key_value_weight, attention_output_weight, attention_output_bias, second_norm_gain, second_norm_bias, feedforward_up_weight, feedforward_up_bias, feedforward_down_weight, feedforward_down_bias, adapter_down_factor, adapter_up_factor, down_first_moment, up_first_moment, down_second_moment, up_second_moment)


def pair_step(
    tokens,
    cotangent,
    lengths,
    first_norm_gain,
    first_norm_bias,
    query_key_value_weight,
    attention_output_weight,
    attention_output_bias,
    second_norm_gain,
    second_norm_bias,
    feedforward_up_weight,
    feedforward_up_bias,
    feedforward_down_weight,
    feedforward_down_bias,
    adapter_down_factor,
    adapter_up_factor,
    down_first_moment,
    up_first_moment,
    down_second_moment,
    up_second_moment,
):
    f32, bf16 = jnp.float32, jnp.bfloat16
    seqs, length, width = tokens.shape
    rank = adapter_down_factor.shape[2]
    me = lax.axis_index("mp")
    columns = query_key_value_weight.shape[2]
    whole, half = 2, length // 2
    tiles, half_tiles = length // MID_ROWS, half // MID_ROWS

    def row(vector):
        return vector.reshape(1, -1)

    qkv_near = swap(core_half(query_key_value_weight, 2))
    up_bias = jnp.concatenate(
        (feedforward_up_bias, core_order(swap(feedforward_up_bias), 0))
    ).reshape(-1, 1, CHUNK)

    down_low = adapter_down_factor.astype(bf16).transpose(0, 2, 1).reshape(2 * rank, width)
    up_low = adapter_up_factor.astype(bf16)
    blank = jnp.zeros_like(up_low[0])
    up_low = jnp.stack(
        (jnp.concatenate((up_low[0], blank)), jnp.concatenate((blank, up_low[1])))
    )
    up_own = lax.dynamic_slice_in_dim(up_low, me * columns, columns, 2)
    up_other = core_order(
        lax.dynamic_slice_in_dim(up_low, (1 - me) * columns, columns, 2), 2
    )
    up_both = jnp.concatenate((up_own, up_other), axis=2)

    places = jnp.arange(seqs, dtype=jnp.int32)
    longer = (lengths[None, :] > lengths[:, None]) | (
        (lengths[None, :] == lengths[:, None]) & (places[None, :] < places[:, None])
    )
    standing = jnp.sum(longer.astype(jnp.int32), axis=1)
    order = jnp.sum(jnp.where(standing[None, :] == places[:, None], places[None, :], 0), axis=1)
    split = order[0]

    mine = jnp.stack((jnp.where(me == 0, order[1], order[2]), jnp.where(me == 0, order[4], order[3])))
    theirs = jnp.stack(
        (jnp.where(me == 0, order[2], order[1]), jnp.where(me == 0, order[3], order[4]))
    )

    def lens_of(index):
        return jnp.sum(jnp.where(places[None, :] == index[:, None], lengths[None, :], 0), axis=1)

    own_lens = lens_of(mine)
    split_lens = lens_of(split[None])
    three_lens = jnp.concatenate((own_lens, split_lens))
    flat_tokens = tokens.reshape(-1, width)
    flat_cotangent = cotangent.reshape(-1, width)
    step = jnp.arange(whole * tiles, dtype=jnp.int32)
    extra = jnp.arange(half_tiles, dtype=jnp.int32) + me * half_tiles
    whole_table = mine[step // tiles] * tiles + step % tiles
    token_table = jnp.concatenate((whole_table, split * tiles + extra))
    own_table = jnp.concatenate((step, whole * tiles + extra))
    live_table = jnp.concatenate(
        (
            own_lens[step // tiles] - (step % tiles) * MID_ROWS,
            split_lens[0] - extra * MID_ROWS,
        )
    )
    three_table = jnp.concatenate(
        (whole_table, split * tiles + jnp.arange(tiles, dtype=jnp.int32))
    )
    gain_one, shift_one = row(first_norm_gain), row(first_norm_bias)

    def sequences(pieces):
        return [piece.reshape(-1, length, columns) for piece in pieces]

    *own_heads, low = project(
        three_table,
        flat_tokens,
        gain_one,
        shift_one,
        down_low,
        up_own,
        query_key_value_weight,
    )
    own_heads = sequences(own_heads)
    qkv_near = after(qkv_near, own_heads[0])
    qkv_far = core_swap(qkv_near)
    out_near = swap(after(core_half(attention_output_weight, 0), qkv_near))
    up_near = swap(after(core_half(feedforward_up_weight, 1), qkv_near))
    attended_own, lse_own = attention_forward(three_lens, *own_heads)
    sent = lax.dynamic_slice_in_dim(attended_own[whole], (1 - me) * half, half, 0)
    attended_got = swap(core_order(sent, 1))
    qkv_far = after(qkv_far, attended_own)
    down_near = swap(after(core_half(feedforward_down_weight, 0), qkv_far))
    qkv = (query_key_value_weight, qkv_near, qkv_far)
    *far_heads, _ = project(
        whole_table,
        flat_tokens,
        gain_one,
        shift_one,
        down_low,
        up_other,
        qkv_near,
        qkv_far,
    )
    far_heads = sequences(far_heads)
    out_far = core_swap(after(out_near, far_heads[0]))
    up_far = core_swap(after(up_near, far_heads[0]))
    attended_far, lse_far = attention_forward(own_lens, *far_heads)
    down_far = core_swap(after(down_near, attended_far))
    far_all = jnp.concatenate((attended_far.reshape(-1, columns), attended_got), axis=0)
    weights = (
        attention_output_weight,
        out_near,
        out_far,
        feedforward_up_weight,
        up_near,
        up_far,
        feedforward_down_weight,
        down_near,
        down_far,
    )
    middle_table = jnp.stack(
        (token_table, own_table, live_table, jnp.arange(token_table.shape[0], dtype=jnp.int32))
    )

    def run_middle(first, last):
        return middle(
            middle_table[:, first:last],
            flat_tokens,
            flat_cotangent,
            attended_own.reshape(-1, columns),
            far_all,
            row(attention_output_bias),
            row(second_norm_gain),
            row(second_norm_bias),
            up_bias,
            row(feedforward_down_bias),
            weights,
        )

    block_zero, resid_zero, *grads_zero = run_middle(0, tiles)
    block_zero_got = swap(block_zero)
    block_rest, resid_rest, *grads_rest = run_middle(tiles, token_table.shape[0])
    grad_got = swap(core_order(grads_rest[1][length:], 1))
    block_rest_got = swap(block_rest)
    grad_kept = grads_rest[0][length:]
    grad_split = jnp.concatenate(
        (jnp.where(me == 0, grad_kept, grad_got), jnp.where(me == 0, grad_got, grad_kept))
    )

    def flat(pieces):
        return [piece.reshape(-1, columns) for piece in pieces]

    def back_whole(index, grads):
        lens = own_lens[index : index + 1]
        own = attention_backward(lens, *own_heads, grads[0], attended_own, lse_own, index)
        far = attention_backward(lens, *far_heads, grads[1], attended_far, lse_far, index)
        return flat(own), flat(far)

    span = jnp.arange(tiles, dtype=jnp.int32)

    def back_first(own, far, table, resid_grad):
        return first_backward(
            table,
            flat_tokens,
            resid_grad,
            low,
            own,
            far,
            gain_one,
            shift_one,
            down_low,
            up_both,
            qkv,
        )

    def whole_rows(index):
        at = index * tiles + span
        return jnp.stack((token_table[at], span, at, span, live_table[at]))

    back_zero = back_whole(0, grads_zero)
    split_own = attention_backward(split_lens, *own_heads, grad_split, attended_own, lse_own, whole)
    split_sent = jnp.stack(
        [lax.dynamic_slice_in_dim(p[0], (1 - me) * half, half, 0) for p in split_own]
    )
    split_got = swap(core_order(split_sent, 2))
    first_zero = back_first(*back_zero, whole_rows(0), resid_zero)
    send_zero = swap(first_zero[0])
    back_one = back_whole(1, grads_rest)
    first_split = back_first(
        flat(split_own),
        [split_got[i] for i in range(3)],
        jnp.stack(
            (
                split * tiles + extra,
                tiles + extra - me * half_tiles,
                whole * tiles + extra,
                extra,
                split_lens[0] - extra * MID_ROWS,
            )
        ),
        resid_rest,
    )
    send_split = swap(first_split[0])
    first_one = back_first(*back_one, whole_rows(1), resid_rest)
    send_one = swap(first_one[0])

    down_sum, query_sum, value_sum = (
        first_zero[i] + first_split[i] + first_one[i] for i in range(1, 4)
    )
    up_sum = 8.0 * jnp.concatenate((query_sum[:rank], value_sum[rank:]))
    up_mine = up_sum[:, :columns]
    up_theirs = core_order(up_sum[:, columns:], 1)
    up_sum = jnp.concatenate(
        (jnp.where(me == 0, up_mine, up_theirs), jnp.where(me == 0, up_theirs, up_mine)), axis=1
    )
    live_row = jnp.full((8, width), jnp.sum(lengths).astype(f32))
    total = sum_all(jnp.concatenate((down_sum, up_sum, live_row)))
    active = total[-1, 0] / 2
    grad_down = total[: 2 * rank].reshape(2, rank, width).transpose(0, 2, 1) / active
    grad_up = total[2 * rank : 4 * rank].reshape(2, rank, width) / active

    def place(pieces):
        out = jnp.zeros((seqs * length, width), bf16)
        for piece, start in pieces:
            out = lax.dynamic_update_slice_in_dim(out, piece, start, 0)
        return out.reshape(tokens.shape)

    here = split * length + half * me
    there = split * length + half * (1 - me)
    block_out = place(
        (
            (block_zero, mine[0] * length),
            (block_rest[:length], mine[1] * length),
            (block_rest[length:], here),
            (block_zero_got, theirs[0] * length),
            (block_rest_got[:length], theirs[1] * length),
            (block_rest_got[length:], there),
        )
    )
    input_grad = place(
        (
            (first_zero[0], mine[0] * length),
            (first_split[0], here),
            (first_one[0], mine[1] * length),
            (send_zero, theirs[0] * length),
            (send_split, there),
            (send_one, theirs[1] * length),
        )
    )
    new_down = adam_decay_update(
        adapter_down_factor, grad_down, down_first_moment, down_second_moment
    )
    new_up = adam_decay_update(adapter_up_factor, grad_up, up_first_moment, up_second_moment)
    return (
        block_out,
        input_grad,
        new_down[0],
        new_up[0],
        new_down[1],
        new_up[1],
        new_down[2],
        new_up[2],
    )


def solution(mesh):
    in_specs = (
        P("dp", None, None),
        P("dp", None, None),
        P("dp"),
        P(),
        P(),
        P(None, None, "mp"),
        P("mp", None),
        P(),
        P(),
        P(),
        P(None, "mp"),
        P("mp"),
        P("mp", None),
        P(),
        P(),
        P(),
        P(),
        P(),
        P(),
        P(),
    )
    out_specs = (P("dp", None, None), P("dp", None, None), P(), P(), P(), P(), P(), P())
    return jax.shard_map(
        per_device_pair if mesh.shape["mp"] == 2 else per_device,
        mesh=mesh,
        in_specs=in_specs,
        out_specs=out_specs,
        check_vma=False,
    )
```

```python
import functools

import jax
import jax.numpy as jnp
from jax import lax
from jax.experimental import pallas as pl
from jax.experimental.pallas import tpu as pltpu
from jax.sharding import PartitionSpec as P

HEAD = 64


def layer_norm(values, norm_gain, norm_shift):
    centre = values - jnp.mean(values, axis=-1, keepdims=True)
    spread = jnp.mean(centre * centre, axis=-1, keepdims=True)
    return centre * lax.rsqrt(spread + 1e-05) * norm_gain + norm_shift


def gelu_tanh(values):
    return (
        0.5
        * values
        * (1.0 + jnp.tanh(0.7978845608028654 * (values + 0.044715 * values * values * values)))
    )


def head_major(matrix, seq_rows, head_count):
    return (
        matrix.reshape(seq_rows, -1, head_count, HEAD)
        .transpose(0, 2, 1, 3)
        .reshape(seq_rows * head_count, -1, HEAD)
    )


def token_major(stacked, seq_rows, head_count):
    return (
        stacked.reshape(seq_rows, head_count, -1, HEAD)
        .transpose(0, 2, 1, 3)
        .reshape(-1, head_count * HEAD)
    )


def masked_scores(query_rows, key_rows, seq_len):
    scores = jnp.einsum(
        "qd,kd->qk", query_rows, key_rows, preferred_element_type=jnp.float32
    ) * HEAD ** (-0.5)
    position = jnp.arange(scores.shape[0])
    allowed = (position[None, :] <= position[:, None]) & (position[None, :] < seq_len)
    return jnp.where(allowed, scores, -1e30)


def attend_forward(pieces):
    query_rows, key_rows, value_token_rows, seq_len = pieces
    scores = masked_scores(query_rows, key_rows, seq_len)
    row_max = jnp.max(scores, axis=-1, keepdims=True)
    weights = jnp.exp(scores - row_max)
    row_sum = jnp.sum(weights, axis=-1, keepdims=True)
    probabilities = (weights / row_sum).astype(jnp.bfloat16)
    head_out = jnp.dot(probabilities, value_token_rows, preferred_element_type=jnp.float32)
    return (head_out, row_max[:, 0] + jnp.log(row_sum[:, 0]))


def attend_backward(pieces):
    query_rows, key_rows, value_token_rows, seq_len, grad_head, log_sums = pieces
    scores = masked_scores(query_rows, key_rows, seq_len)
    probabilities = jnp.exp(scores - log_sums[:, None])
    value_gradient_rows = jnp.einsum(
        "qk,qd->kd",
        probabilities.astype(jnp.bfloat16),
        grad_head,
        preferred_element_type=jnp.float32,
    )
    grad_probs = jnp.einsum(
        "qd,kd->qk", grad_head, value_token_rows, preferred_element_type=jnp.float32
    )
    grad_scores = probabilities * (
        grad_probs - jnp.sum(grad_probs * probabilities, axis=-1, keepdims=True)
    )
    grad_scores = grad_scores.astype(jnp.bfloat16)
    query_gradient_rows = jnp.dot(
        grad_scores, key_rows, preferred_element_type=jnp.float32
    ) * HEAD ** (-0.5)
    grad_keys = jnp.einsum(
        "qk,qd->kd", grad_scores, query_rows, preferred_element_type=jnp.float32
    ) * HEAD ** (-0.5)
    return (query_gradient_rows, grad_keys, value_gradient_rows)


def adam_decay_update(adapter, gradient, first_mom, second_mom):
    first_new = 0.9 * first_mom + 0.1 * gradient
    second_new = 0.999 * second_mom + 0.001 * gradient * gradient
    update = first_new / (1.0 - 0.9**10) / (jnp.sqrt(second_new / (1.0 - 0.999**10)) + 1e-08)
    return (adapter - 0.25 * (update + 0.01 * adapter), first_new, second_new)


def per_device(
    tokens,
    cotangent,
    lengths,
    first_norm_gain,
    first_norm_bias,
    query_key_value_weight,
    attention_output_weight,
    attention_output_bias,
    second_norm_gain,
    second_norm_bias,
    feedforward_up_weight,
    feedforward_up_bias,
    feedforward_down_weight,
    feedforward_down_bias,
    adapter_down_factor,
    adapter_up_factor,
    down_first_moment,
    up_first_moment,
    down_second_moment,
    up_second_moment,
):
    seq_rows, seq_len_all, model_width = tokens.shape
    tok_count = seq_rows * seq_len_all
    groups = lax.axis_size("mp")
    worker_shard = lax.axis_index("mp")
    shard_width = query_key_value_weight.shape[2]
    head_count = shard_width // HEAD
    adapter_rank_size = adapter_down_factor.shape[2]
    tokens_f32 = tokens.reshape(tok_count, model_width).astype(jnp.float32)
    normalized_rows = layer_norm(tokens_f32, first_norm_gain, first_norm_bias).astype(jnp.bfloat16)
    down_reduced = adapter_down_factor.astype(jnp.bfloat16)
    up_reduced = adapter_up_factor.astype(jnp.bfloat16)
    up_columns = lax.dynamic_slice_in_dim(up_reduced, worker_shard * shard_width, shard_width, 2)
    down_pair = jnp.concatenate((down_reduced[0], down_reduced[1]), axis=1)
    adapter_pair = jnp.dot(normalized_rows, down_pair, preferred_element_type=jnp.float32).astype(
        jnp.bfloat16
    )
    adapter_query_delta = adapter_pair[:, :adapter_rank_size]
    adapter_value_delta = adapter_pair[:, adapter_rank_size:]
    query_rows = (
        jnp.dot(normalized_rows, query_key_value_weight[0], preferred_element_type=jnp.float32)
        + 8.0 * jnp.dot(adapter_query_delta, up_columns[0], preferred_element_type=jnp.float32)
    ).astype(jnp.bfloat16)
    key_rows = jnp.dot(
        normalized_rows, query_key_value_weight[1], preferred_element_type=jnp.float32
    ).astype(jnp.bfloat16)
    value_token_rows = (
        jnp.dot(normalized_rows, query_key_value_weight[2], preferred_element_type=jnp.float32)
        + 8.0 * jnp.dot(adapter_value_delta, up_columns[1], preferred_element_type=jnp.float32)
    ).astype(jnp.bfloat16)
    limits = jnp.repeat(lengths, head_count)
    query_heads = head_major(query_rows, seq_rows, head_count)
    key_heads = head_major(key_rows, seq_rows, head_count)
    value_heads = head_major(value_token_rows, seq_rows, head_count)
    head_out, log_sums = lax.map(attend_forward, (query_heads, key_heads, value_heads, limits))
    attended = token_major(head_out, seq_rows, head_count).astype(jnp.bfloat16)
    attn_share = (
        lax.psum_scatter(
            jnp.dot(attended, attention_output_weight, preferred_element_type=jnp.float32),
            "mp",
            scatter_dimension=0,
            tiled=True,
        )
        + attention_output_bias
    )

    def norm_two(values):
        return layer_norm(values, second_norm_gain, second_norm_bias)

    def norm_one(values):
        return layer_norm(values, first_norm_gain, first_norm_bias)

    attn_full = lax.all_gather(attn_share, "mp", axis=0, tiled=True)
    residual = tokens_f32 + attn_full
    normed_two = norm_two(residual).astype(jnp.bfloat16)
    hidden_pre = (
        jnp.dot(normed_two, feedforward_up_weight, preferred_element_type=jnp.float32)
        + feedforward_up_bias
    )
    hidden = gelu_tanh(hidden_pre).astype(jnp.bfloat16)
    mlp_share = (
        lax.psum_scatter(
            jnp.dot(hidden, feedforward_down_weight, preferred_element_type=jnp.float32).astype(
                jnp.bfloat16
            ),
            "mp",
            scatter_dimension=0,
            tiled=True,
        ).astype(jnp.float32)
        + feedforward_down_bias
    )
    mlp_full = lax.all_gather(mlp_share.astype(jnp.bfloat16), "mp", axis=0, tiled=True).astype(
        mlp_share.dtype
    )
    block_out = (residual + mlp_full).astype(jnp.bfloat16)
    live_mask = (jnp.arange(seq_len_all)[None, :] < lengths[:, None]).reshape(tok_count, 1)
    grad_out = jnp.where(
        live_mask, cotangent.reshape(tok_count, model_width), jnp.zeros((), jnp.bfloat16)
    )
    grad_hidden = jnp.einsum(
        "td,fd->tf", grad_out, feedforward_down_weight, preferred_element_type=jnp.float32
    )
    _, gelu_back = jax.vjp(gelu_tanh, hidden_pre)
    grad_pre = gelu_back(grad_hidden)[0].astype(jnp.bfloat16)
    grad_norm2_share = lax.psum_scatter(
        jnp.einsum(
            "tf,df->td", grad_pre, feedforward_up_weight, preferred_element_type=jnp.float32
        ),
        "mp",
        scatter_dimension=0,
        tiled=True,
    )
    grad_norm2 = lax.all_gather(grad_norm2_share, "mp", axis=0, tiled=True)
    _, norm2_back = jax.vjp(norm_two, residual)
    grad_resid = grad_out.astype(jnp.float32) + norm2_back(grad_norm2)[0]
    grad_resid_low = grad_resid.astype(jnp.bfloat16)
    grad_attended = jnp.einsum(
        "td,ed->te", grad_resid_low, attention_output_weight, preferred_element_type=jnp.float32
    ).astype(jnp.bfloat16)
    grad_head = head_major(grad_attended, seq_rows, head_count)
    head_dq, head_dk, head_dv = lax.map(
        attend_backward, (query_heads, key_heads, value_heads, limits, grad_head, log_sums)
    )
    query_gradient_rows = token_major(head_dq, seq_rows, head_count).astype(jnp.bfloat16)
    grad_keys = token_major(head_dk, seq_rows, head_count).astype(jnp.bfloat16)
    value_gradient_rows = token_major(head_dv, seq_rows, head_count).astype(jnp.bfloat16)
    adapter_query_gradient = 8.0 * jnp.einsum(
        "te,re->tr", query_gradient_rows, up_columns[0], preferred_element_type=jnp.float32
    )
    adapter_value_gradient = 8.0 * jnp.einsum(
        "te,re->tr", value_gradient_rows, up_columns[1], preferred_element_type=jnp.float32
    )
    adapter_gradient = jnp.concatenate((adapter_query_gradient, adapter_value_gradient), axis=1)
    down_pair_float32 = down_pair.astype(jnp.float32)
    partial_sum = jnp.einsum(
        "te,de->td",
        query_gradient_rows,
        query_key_value_weight[0],
        preferred_element_type=jnp.float32,
    )
    partial_sum = partial_sum + jnp.einsum(
        "te,de->td", grad_keys, query_key_value_weight[1], preferred_element_type=jnp.float32
    )
    partial_sum = partial_sum + jnp.einsum(
        "te,de->td",
        value_gradient_rows,
        query_key_value_weight[2],
        preferred_element_type=jnp.float32,
    )
    grad_norm1_share = lax.psum_scatter(
        partial_sum
        + jnp.einsum(
            "gy,wy->gw", adapter_gradient, down_pair_float32, precision=lax.Precision.HIGHEST
        ),
        "mp",
        scatter_dimension=0,
        tiled=True,
    )
    grad_down_both = jnp.einsum(
        "fi,fg->ig",
        normalized_rows.astype(jnp.float32),
        adapter_gradient,
        precision=lax.Precision.HIGHEST,
    )
    grad_down = jnp.stack(
        (grad_down_both[:, :adapter_rank_size], grad_down_both[:, adapter_rank_size:])
    )
    grad_up_query = 8.0 * jnp.einsum(
        "zm,zj->mj", adapter_query_delta, query_gradient_rows, preferred_element_type=jnp.float32
    )
    grad_up_value = 8.0 * jnp.einsum(
        "zm,zj->mj", adapter_value_delta, value_gradient_rows, preferred_element_type=jnp.float32
    )
    up_column_gradient = jnp.stack((grad_up_query, grad_up_value))
    grad_up = lax.dynamic_update_slice_in_dim(
        jnp.zeros(adapter_up_factor.shape, jnp.float32),
        up_column_gradient,
        worker_shard * shard_width,
        2,
    )
    live_local = jnp.sum(lengths).astype(jnp.float32)
    down_reduced_sum, up_reduced_sum, live_sum = lax.psum(
        (grad_down, grad_up, live_local), ("dp", "mp")
    )
    active_token_total = live_sum / groups
    grad_norm1 = lax.all_gather(grad_norm1_share, "mp", axis=0, tiled=True)
    _, norm1_back = jax.vjp(norm_one, tokens_f32)
    input_grad = (grad_resid + norm1_back(grad_norm1)[0]).astype(jnp.bfloat16)
    down_factor_next, down_first_moment_next, down_second_moment_next = adam_decay_update(
        adapter_down_factor,
        down_reduced_sum / active_token_total,
        down_first_moment,
        down_second_moment,
    )
    up_factor_next, up_first_moment_next, up_second_moment_next = adam_decay_update(
        adapter_up_factor, up_reduced_sum / active_token_total, up_first_moment, up_second_moment
    )
    return (
        block_out.reshape(seq_rows, seq_len_all, model_width),
        input_grad.reshape(seq_rows, seq_len_all, model_width),
        down_factor_next,
        up_factor_next,
        down_first_moment_next,
        up_first_moment_next,
        down_second_moment_next,
        up_second_moment_next,
    )


TILE = 256
NT = (((1,), (1,)), ((), ()))


def head_lanes(half):
    lane = lax.broadcasted_iota(jnp.int32, (1, 2 * HEAD), 1)
    return (lane >= half * HEAD) & (lane < (half + 1) * HEAD)


def one_head(block, half):
    return jnp.where(head_lanes(half), block, jnp.zeros((), block.dtype))


def edge_allowed(key_start, query_start, seq_len):
    key_at = key_start + lax.broadcasted_iota(jnp.int32, (TILE, TILE), 0)
    query_at = query_start + lax.broadcasted_iota(jnp.int32, (TILE, TILE), 1)
    return (key_at <= query_at) & (key_at < seq_len)


def attention_forward_kernel(lens_ref, q_ref, k_ref, v_ref, out_ref, lse_ref, vt_ref):
    seq_len = lens_ref[pl.program_id(0)]
    live_tiles = (seq_len + TILE - 1) // TILE
    vt_ref[...] = v_ref[0].T
    tiles = q_ref.shape[1] // TILE

    def row_tile(tile, extent):
        rows = pl.ds(tile * TILE, TILE)
        inner = (extent - 1) * TILE
        query = both_heads(q_ref[0, rows, :] * HEAD ** (-0.5))
        allowed = edge_allowed(inner, tile * TILE, seq_len)
        allowed = jnp.concatenate((allowed, allowed), axis=1)
        scores = []
        for span in range(extent):
            part = lax.dot_general(
                k_ref[0, pl.ds(span * TILE, TILE), :],
                query,
                NT,
                preferred_element_type=jnp.float32,
            )
            if span == extent - 1:
                part = jnp.where(allowed, part, -1e30)
            scores.append(part)
        top = functools.reduce(
            jnp.maximum, [jnp.max(part, axis=0, keepdims=True) for part in scores]
        )
        total, outs = 0.0, [0.0, 0.0]
        for span, part in enumerate(scores):
            part = jnp.exp(part - top)
            total = total + jnp.sum(part, axis=0, keepdims=True)
            part = part.astype(jnp.bfloat16)
            for half in range(2):
                outs[half] = outs[half] + jnp.dot(
                    vt_ref[pl.ds(half * HEAD, HEAD), pl.ds(span * TILE, TILE)],
                    part[:, half * TILE : (half + 1) * TILE],
                    preferred_element_type=jnp.float32,
                )
        lse = top + jnp.log(total)
        scale = 1.0 / total
        for half in range(2):
            columns = slice(half * TILE, (half + 1) * TILE)
            outs[half] = outs[half] * scale[:, columns]
            lse_ref[0, 0, pl.ds(half, 1), rows] = lse[:, columns]
        out_ref[0, rows, :] = jnp.concatenate(outs, axis=0).T.astype(out_ref.dtype)

    for tile in range(tiles):
        for extent in range(1, tile + 2):
            pl.when(jnp.minimum(live_tiles, tile + 1) == extent)(
                lambda tile=tile, extent=extent: row_tile(tile, extent)
            )


def attention_forward(lens, query, key, value):
    seqs, length, width = query.shape
    pairs = width // (2 * HEAD)
    spec = pl.BlockSpec((1, length, 2 * HEAD), lambda s, h, lens: (s, 0, h))
    return pl.pallas_call(
        attention_forward_kernel,
        grid_spec=pltpu.PrefetchScalarGridSpec(
            num_scalar_prefetch=1,
            grid=(seqs, pairs),
            in_specs=[spec] * 3,
            out_specs=[spec, pl.BlockSpec((1, 1, 2, length), lambda s, h, lens: (s, h, 0, 0))],
            scratch_shapes=[pltpu.VMEM((2 * HEAD, length), jnp.bfloat16)],
        ),
        out_shape=[
            jax.ShapeDtypeStruct(query.shape, jnp.bfloat16),
            jax.ShapeDtypeStruct((seqs, pairs, 2, length), jnp.float32),
        ],
        cost_estimate=pl.CostEstimate(
            flops=seqs * width * length * length * 3,
            bytes_accessed=seqs * width * length * 8,
            transcendentals=seqs * pairs * length * length,
        ),
        name="attention_forward",
    )(lens, query, key, value)


def both_heads(block):
    return jnp.concatenate((one_head(block, 0), one_head(block, 1)), axis=0)


def attention_backward_kernel(
    lens_ref,
    q_ref,
    k_ref,
    v_ref,
    g_ref,
    out_ref,
    lse_ref,
    dq_ref,
    dk_ref,
    dv_ref,
    kt_ref,
    dk_acc,
    dv_acc,
):
    seq_len = lens_ref[pl.program_id(0)]
    kt_ref[...] = k_ref[0].T
    dk_acc[...] = jnp.zeros_like(dk_acc)
    dv_acc[...] = jnp.zeros_like(dv_acc)
    tiles = q_ref.shape[1] // TILE

    def row_tile(tile):
        rows = pl.ds(tile * TILE, TILE)
        query = both_heads(q_ref[0, rows, :] * HEAD ** (-0.5))
        grad = g_ref[rows, :]
        product = (grad.astype(jnp.float32) * out_ref[0, rows, :].astype(jnp.float32)).T
        grad = both_heads(grad)

        def head_pair(pick):
            return jnp.concatenate([pick(half) for half in range(2)], axis=1)

        lse = head_pair(lambda half: lse_ref[0, 0, pl.ds(half, 1), rows])
        row_dot = head_pair(
            lambda half: jnp.sum(
                product[half * HEAD : (half + 1) * HEAD], axis=0, keepdims=True
            )
        )
        allowed = edge_allowed(0, 0, seq_len - tile * TILE)
        allowed = jnp.concatenate((allowed, allowed), axis=1)
        outs = [0.0, 0.0]
        for span in range(tile + 1):
            keys = pl.ds(span * TILE, TILE)
            scores = lax.dot_general(
                k_ref[0, keys, :], query, NT, preferred_element_type=jnp.float32
            )
            if span == tile:
                scores = jnp.where(allowed, scores, -1e30)
            prob = jnp.exp(scores - lse)
            grad_prob = lax.dot_general(
                v_ref[0, keys, :], grad, NT, preferred_element_type=jnp.float32
            )
            grad_scores = (prob * (grad_prob - row_dot)).astype(jnp.bfloat16)
            dv_acc[keys, :] += jnp.dot(
                prob.astype(jnp.bfloat16), grad, preferred_element_type=jnp.float32
            )
            dk_acc[keys, :] += jnp.dot(grad_scores, query, preferred_element_type=jnp.float32)
            for half in range(2):
                outs[half] = outs[half] + jnp.dot(
                    kt_ref[pl.ds(half * HEAD, HEAD), keys],
                    grad_scores[:, half * TILE : (half + 1) * TILE],
                    preferred_element_type=jnp.float32,
                )
        dq = jnp.concatenate(outs, axis=0).T * HEAD ** (-0.5)
        dq_ref[0, rows, :] = dq.astype(dq_ref.dtype)

    for tile in range(tiles):
        pl.when(tile * TILE < seq_len)(lambda tile=tile: row_tile(tile))

        @pl.when(tile * TILE >= seq_len)
        def _(tile=tile):
            dq_ref[0, pl.ds(tile * TILE, TILE), :] = jnp.zeros((TILE, 2 * HEAD), dq_ref.dtype)

    dk_ref[0] = dk_acc[...].astype(dk_ref.dtype)
    dv_ref[0] = dv_acc[...].astype(dv_ref.dtype)


def attention_backward(lens, query, key, value, grad, out, lse, start):
    length, width = query.shape[1:]
    seqs = lens.shape[0]
    pairs = width // (2 * HEAD)

    def block(first):
        return pl.BlockSpec((1, length, 2 * HEAD), lambda s, h, lens: (s + first, 0, h))

    return pl.pallas_call(
        attention_backward_kernel,
        grid_spec=pltpu.PrefetchScalarGridSpec(
            num_scalar_prefetch=1,
            grid=(seqs, pairs),
            in_specs=[block(start)] * 3
            + [
                pl.BlockSpec((length, 2 * HEAD), lambda s, h, lens: (s, h)),
                block(start),
                pl.BlockSpec((1, 1, 2, length), lambda s, h, lens: (s + start, h, 0, 0)),
            ],
            out_specs=[block(0)] * 3,
            scratch_shapes=[
                pltpu.VMEM((2 * HEAD, length), jnp.bfloat16),
                pltpu.VMEM((length, 2 * HEAD), jnp.float32),
                pltpu.VMEM((length, 2 * HEAD), jnp.float32),
            ],
        ),
        out_shape=[jax.ShapeDtypeStruct((seqs, length, width), jnp.bfloat16)] * 3,
        cost_estimate=pl.CostEstimate(
            flops=seqs * width * length * length * 7,
            bytes_accessed=seqs * width * length * 14,
            transcendentals=seqs * pairs * length * length,
        ),
        name="attention_backward",
    )(lens, query, key, value, grad, out, lse)


MID_ROWS = 256
CHUNK = 1024


def centred(values):
    centre = values - jnp.mean(values, axis=-1, keepdims=True)
    inverse = lax.rsqrt(jnp.mean(centre * centre, axis=-1, keepdims=True) + 1e-05)
    return centre * inverse, inverse


def norm_backward(grad, gain, normal, inverse):
    grad = grad * gain
    mean = jnp.mean(grad, axis=-1, keepdims=True)
    along = jnp.mean(grad * normal, axis=-1, keepdims=True)
    return (grad - mean - normal * along) * inverse


def dot(a, b):
    return jnp.dot(a, b, preferred_element_type=jnp.float32)


def dot_t(a, b):
    return lax.dot_general(a, b, NT, preferred_element_type=jnp.float32)


def copies_of(pairs, sems):
    return [pltpu.make_async_copy(a, b, sems.at[i]) for i, (a, b) in enumerate(pairs)]


def middle_kernel(
    table_ref,
    tokens_ref,
    cotangent_ref,
    attended_own,
    attended_far,
    out_bias_ref,
    gain_ref,
    shift_ref,
    up_bias_ref,
    down_bias_ref,
    out_own,
    out_near,
    out_far,
    up_own,
    up_near,
    up_far,
    down_own,
    down_near,
    down_far,
    block_ref,
    full_ref,
    resid_grad_ref,
    own_grad_ref,
    far_grad_ref,
    out_w,
    up_w,
    down_w,
    residual_ref,
    normed_ref,
    normal_ref,
    acc_ref,
    grad_acc_ref,
    sems,
):
    step = pl.program_id(0)

    pairs = []
    start = 0
    for piece in (out_own, out_near, out_far):
        rows = piece.shape[0]
        pairs.append((piece, out_w.at[pl.ds(start, rows), :]))
        start += rows
    chunk = 0
    for up, down in ((up_own, down_own), (up_near, down_near), (up_far, down_far)):
        for at in range(up.shape[1] // CHUNK):
            units = pl.ds(at * CHUNK, CHUNK)
            pairs.append((up.at[:, units], up_w.at[chunk]))
            pairs.append((down.at[units, :], down_w.at[chunk]))
            chunk += 1
    loads = copies_of(pairs, sems)

    @pl.when(step == 0)
    def _():
        for load in loads:
            load.start()
        for load in loads[:3]:
            load.wait()

    live = table_ref[2, step]
    residual = tokens_ref[...].astype(jnp.float32) + (
        dot(jnp.concatenate((attended_own[...], attended_far[...]), axis=1), out_w[...])
        + out_bias_ref[...]
    )
    residual_ref[...] = residual
    normal, inverse = centred(residual)
    normal_ref[...] = normal
    normed_ref[...] = (normal * gain_ref[...] + shift_ref[...]).astype(jnp.bfloat16)
    acc_ref[...] = jnp.zeros_like(acc_ref)

    @pl.when(step == 0)
    def _():
        for load in loads[3:]:
            load.wait()

    scale = 0.7978845608028654
    cube = 0.044715 * scale

    def forward_only(chunk, carry):
        pre = dot(normed_ref[...], up_w[chunk]) + up_bias_ref[chunk]
        tanh = jnp.tanh(pre * (scale + cube * (pre * pre)))
        hidden = (pre * (0.5 + 0.5 * tanh)).astype(jnp.bfloat16)
        acc_ref[...] += dot(hidden, down_w[chunk])
        return carry

    def finish():
        block = (residual_ref[...] + acc_ref[...] + down_bias_ref[...]).astype(block_ref.dtype)
        block_ref[...] = block
        full_ref[...] = block

    @pl.when(live > 0)
    def _():
        row = lax.broadcasted_iota(jnp.int32, (MID_ROWS, 1), 0)
        grad_out = jnp.where(row < live, cotangent_ref[...], jnp.zeros((), jnp.bfloat16))
        grad_acc_ref[...] = jnp.zeros_like(grad_acc_ref)

        def both_ways(chunk, carry):
            pre = dot(normed_ref[...], up_w[chunk]) + up_bias_ref[chunk]
            grad_hidden = dot_t(grad_out, down_w[chunk])
            square = pre * pre
            tanh = jnp.tanh(pre * (scale + cube * square))
            gate = 0.5 + 0.5 * tanh
            hidden = (pre * gate).astype(jnp.bfloat16)
            slope = gate + (pre * (0.5 - 0.5 * (tanh * tanh))) * (scale + 3.0 * cube * square)
            grad_pre = (grad_hidden * slope).astype(jnp.bfloat16)
            acc_ref[...] += dot(hidden, down_w[chunk])
            grad_acc_ref[...] += dot_t(grad_pre, up_w[chunk])
            return carry

        lax.fori_loop(0, up_w.shape[0], both_ways, 0, unroll=UNROLL)
        finish()
        grad_resid = grad_out.astype(jnp.float32) + norm_backward(
            grad_acc_ref[...], gain_ref[...], normal_ref[...], inverse
        )
        low = grad_resid.astype(jnp.bfloat16)
        resid_grad_ref[...] = low
        columns = own_grad_ref.shape[1]
        own_grad_ref[...] = dot_t(low, out_w[:columns]).astype(jnp.bfloat16)
        far_grad_ref[...] = dot_t(low, out_w[columns:]).astype(jnp.bfloat16)

    @pl.when(live <= 0)
    def _():
        lax.fori_loop(0, up_w.shape[0], forward_only, 0, unroll=UNROLL)
        finish()
        resid_grad_ref[...] = jnp.zeros_like(resid_grad_ref)
        own_grad_ref[...] = jnp.zeros_like(own_grad_ref)
        far_grad_ref[...] = jnp.zeros_like(far_grad_ref)


UNROLL = 2


def without(kernel, place, *refs):
    return kernel(*refs[:place], *refs[place + 1 :])


def middle(
    table, tokens, cotangent, own, far, out_bias, gain, shift, up_bias, down_bias, weights, into
):
    rows, width = table.shape[1] * MID_ROWS, tokens.shape[1]
    columns = far.shape[1]
    units = up_bias.shape[0] * up_bias.shape[2]
    tile = pl.BlockSpec((MID_ROWS, width), lambda i, t: (i, 0))
    picked = pl.BlockSpec((MID_ROWS, width), lambda i, t: (t[0, i], 0))
    part = pl.BlockSpec((MID_ROWS, columns), lambda i, t: (i, 0))
    vector = pl.BlockSpec((1, width), lambda i, t: (0, 0))
    chunks = units // CHUNK
    low = jax.ShapeDtypeStruct((rows, width), jnp.bfloat16)
    thin = jax.ShapeDtypeStruct((rows, columns), jnp.bfloat16)
    wide = pltpu.VMEM((MID_ROWS, width), jnp.float32)
    operands = (
        table,
        tokens,
        cotangent,
        own,
        far,
        out_bias,
        gain,
        shift,
        up_bias,
        down_bias,
        *weights,
    )
    place = len(operands)
    kernel, extra, aliases = middle_kernel, (), {}
    if into is not None:
        kernel = functools.partial(without, middle_kernel, place)
        extra, aliases = (into,), {place: 1}
    return pl.pallas_call(
        kernel,
        grid_spec=pltpu.PrefetchScalarGridSpec(
            num_scalar_prefetch=1,
            grid=(rows // MID_ROWS,),
            in_specs=[picked] * 2
            + [pl.BlockSpec((MID_ROWS, columns), lambda i, t, a=a: (t[a, i], 0)) for a in (1, 3)]
            + [vector] * 3
            + [pl.BlockSpec(up_bias.shape, lambda i, t: (0, 0, 0)), vector]
            + [pl.BlockSpec(memory_space=pl.ANY)] * (9 + len(extra)),
            out_specs=[tile, picked, tile, part, part],
            scratch_shapes=[
                pltpu.VMEM((width, width), jnp.bfloat16),
                pltpu.VMEM((chunks, width, CHUNK), jnp.bfloat16),
                pltpu.VMEM((chunks, CHUNK, width), jnp.bfloat16),
                wide,
                pltpu.VMEM((MID_ROWS, width), jnp.bfloat16),
                wide,
                wide,
                wide,
                pltpu.SemaphoreType.DMA((3 + 2 * chunks,)),
            ],
        ),
        out_shape=[low, jax.ShapeDtypeStruct(tokens.shape, jnp.bfloat16), low, thin, thin],
        input_output_aliases=aliases,
        compiler_params=pltpu.CompilerParams(vmem_limit_bytes=56 << 20),
        cost_estimate=pl.CostEstimate(
            flops=rows * width * (units * 8 + width * 4),
            bytes_accessed=rows * width * 12 + units * width * 4,
            transcendentals=rows * units,
        ),
        name="middle",
    )(*operands, *extra)


PROJECT_ROWS = 256


def qkv_loads(own, near, far, weight_ref, sems):
    pairs = []
    start = 0
    for piece in (own, near, far):
        if piece is not None:
            columns = pl.ds(start, piece.shape[2])
            pairs.append((piece, weight_ref.at[:, :, columns]))
            start += piece.shape[2]
    return copies_of(pairs, sems)


def project_kernel(pieces, table_ref, *refs):
    tokens_ref, gain_ref, shift_ref, down_ref, up_ref = refs[:5]
    weights = list(refs[5 : 5 + pieces]) + [None] * (3 - pieces)
    query_ref, key_ref, value_ref, low_ref, weight_ref, sems = refs[5 + pieces :]
    loads = qkv_loads(*weights, weight_ref, sems)
    first = pl.program_id(0) == 0

    @pl.when(first)
    def _():
        for load in loads:
            load.start()

    normal, _ = centred(tokens_ref[...].astype(jnp.float32))
    normed = (normal * gain_ref[...] + shift_ref[...]).astype(jnp.bfloat16)
    low = dot_t(normed, down_ref[...]).astype(jnp.bfloat16)
    low_ref[...] = low.astype(jnp.float32).T

    @pl.when(first)
    def _():
        for load in loads:
            load.wait()

    query_ref[...] = (dot(normed, weight_ref[0]) + 8.0 * dot(low, up_ref[0])).astype(jnp.bfloat16)
    key_ref[...] = dot(normed, weight_ref[1]).astype(jnp.bfloat16)
    value_ref[...] = (dot(normed, weight_ref[2]) + 8.0 * dot(low, up_ref[1])).astype(jnp.bfloat16)


def project(table, tokens, gain, shift, down, up, *weights):
    rows, width = table.shape[0] * PROJECT_ROWS, tokens.shape[1]
    columns = up.shape[2]
    pairs = down.shape[0]
    out = pl.BlockSpec((PROJECT_ROWS, columns), lambda i, t: (i, 0))
    vector = pl.BlockSpec((1, width), lambda i, t: (0, 0))
    return pl.pallas_call(
        functools.partial(project_kernel, len(weights)),
        grid_spec=pltpu.PrefetchScalarGridSpec(
            num_scalar_prefetch=1,
            grid=(rows // PROJECT_ROWS,),
            in_specs=[
                pl.BlockSpec((PROJECT_ROWS, width), lambda i, t: (t[i], 0)),
                vector,
                vector,
                pl.BlockSpec(down.shape, lambda i, t: (0, 0)),
                pl.BlockSpec(up.shape, lambda i, t: (0, 0, 0)),
            ]
            + [pl.BlockSpec(memory_space=pl.ANY)] * len(weights),
            out_specs=[out] * 3 + [pl.BlockSpec((pairs, PROJECT_ROWS), lambda i, t: (0, i))],
            scratch_shapes=[
                pltpu.VMEM((3, width, columns), jnp.bfloat16),
                pltpu.SemaphoreType.DMA((len(weights),)),
            ],
        ),
        out_shape=[jax.ShapeDtypeStruct((rows, columns), jnp.bfloat16)] * 3
        + [jax.ShapeDtypeStruct((pairs, rows), jnp.float32)],
        cost_estimate=pl.CostEstimate(
            flops=rows * width * columns * 6,
            bytes_accessed=rows * (width + 3 * columns) * 2 + 6 * width * columns,
            transcendentals=rows,
        ),
        name="project",
    )(table, tokens, gain, shift, down, up, *weights)


def first_backward_kernel(
    table_ref,
    tokens_ref,
    resid_grad_ref,
    low_ref,
    query_own,
    key_own,
    value_own,
    query_far,
    key_far,
    value_far,
    gain_ref,
    shift_ref,
    down_ref,
    up_ref,
    own_ref,
    near_ref,
    far_ref,
    input_ref,
    full_ref,
    down_grad_ref,
    query_up_ref,
    value_up_ref,
    weight_ref,
    sems,
):
    first = pl.program_id(0) == 0
    loads = qkv_loads(own_ref, near_ref, far_ref, weight_ref, sems)

    @pl.when(first)
    def _():
        for load in loads:
            load.start()
        down_grad_ref[...] = jnp.zeros_like(down_grad_ref)
        query_up_ref[...] = jnp.zeros_like(query_up_ref)
        value_up_ref[...] = jnp.zeros_like(value_up_ref)

    @pl.when(first)
    def _():
        for load in loads:
            load.wait()

    live = table_ref[4, pl.program_id(0)]

    @pl.when(live > 0)
    def _():
        normal, inverse = centred(tokens_ref[...].astype(jnp.float32))
        normed = (normal * gain_ref[...] + shift_ref[...]).astype(jnp.bfloat16)
        query = jnp.concatenate((query_own[...], query_far[...]), axis=1)
        key = jnp.concatenate((key_own[...], key_far[...]), axis=1)
        value = jnp.concatenate((value_own[...], value_far[...]), axis=1)
        adapter = 8.0 * (dot_t(query, up_ref[0]) + dot_t(value, up_ref[1]))
        high = adapter.astype(jnp.bfloat16)
        rest = (adapter - high.astype(jnp.float32)).astype(jnp.bfloat16)
        down_grad_ref[...] += dot(high.astype(jnp.float32).T.astype(jnp.bfloat16), normed) + dot(
            rest.astype(jnp.float32).T.astype(jnp.bfloat16), normed
        )
        low = low_ref[...].astype(jnp.bfloat16)
        query_up_ref[...] += dot(low, query)
        value_up_ref[...] += dot(low, value)

        grad = (
            dot_t(query, weight_ref[0])
            + dot_t(key, weight_ref[1])
            + dot_t(value, weight_ref[2])
            + dot(high, down_ref[...])
            + dot(rest, down_ref[...])
        )
        result = (
            resid_grad_ref[...].astype(jnp.float32)
            + norm_backward(grad, gain_ref[...], normal, inverse)
        ).astype(input_ref.dtype)
        input_ref[...] = result
        full_ref[...] = result

    @pl.when(live <= 0)
    def _():
        input_ref[...] = jnp.zeros_like(input_ref)
        full_ref[...] = jnp.zeros_like(full_ref)


def first_backward(
    table, tokens, resid_grad, low, own, far, gain, shift, down, up, weights, into
):
    tiles = table.shape[1]
    rows, width = tiles * PROJECT_ROWS, tokens.shape[1]
    pairs = down.shape[0]
    columns = own[0].shape[1]
    tile = pl.BlockSpec((PROJECT_ROWS, width), lambda i, t: (t[0, i], 0))
    vector = pl.BlockSpec((1, width), lambda i, t: (0, 0))
    small = pl.BlockSpec((pairs, width), lambda i, t: (0, 0))
    sums = jax.ShapeDtypeStruct((pairs, width), jnp.float32)
    operands = (table, tokens, resid_grad, low, *own, *far, gain, shift, down, up, *weights)
    place = len(operands)
    kernel, extra, aliases = first_backward_kernel, (), {}
    if into is not None:
        kernel = functools.partial(without, first_backward_kernel, place)
        extra, aliases = (into,), {place: 1}
    return pl.pallas_call(
        kernel,
        grid_spec=pltpu.PrefetchScalarGridSpec(
            num_scalar_prefetch=1,
            grid=(tiles,),
            in_specs=[
                tile,
                pl.BlockSpec((PROJECT_ROWS, width), lambda i, t: (t[1, i], 0)),
                pl.BlockSpec((pairs, PROJECT_ROWS), lambda i, t: (0, t[2, i])),
            ]
            + [pl.BlockSpec((PROJECT_ROWS, columns), lambda i, t: (t[3, i], 0))] * 3
            + [pl.BlockSpec((PROJECT_ROWS, columns), lambda i, t: (i, 0))] * 3
            + [vector, vector, small, pl.BlockSpec(up.shape, lambda i, t: (0, 0, 0))]
            + [pl.BlockSpec(memory_space=pl.ANY)] * (3 + len(extra)),
            out_specs=[pl.BlockSpec((PROJECT_ROWS, width), lambda i, t: (i, 0)), tile] + [small] * 3,
            scratch_shapes=[
                pltpu.VMEM((3, width, width), jnp.bfloat16),
                pltpu.SemaphoreType.DMA((3,)),
            ],
        ),
        out_shape=[
            jax.ShapeDtypeStruct((rows, width), jnp.bfloat16),
            jax.ShapeDtypeStruct(tokens.shape, jnp.bfloat16),
        ]
        + [sums] * 3,
        input_output_aliases=aliases,
        cost_estimate=pl.CostEstimate(
            flops=rows * width * width * 7,
            bytes_accessed=rows * width * 12 + 6 * width * width,
            transcendentals=rows,
        ),
        name="first_backward",
    )(*operands, *extra)


def swap(value):
    return lax.ppermute(value, "mp", [(0, 1), (1, 0)])


def after(value, *earlier):
    return lax.optimization_barrier((value, *earlier))[0]


def core_swap(value):
    return lax.ppermute(value, "dp", [(i, i ^ 1) for i in range(lax.axis_size("dp"))])


def core_half(shard, axis):
    size = shard.shape[axis] // 2
    core = lax.rem(lax.axis_index("dp"), 2)
    return lax.dynamic_slice_in_dim(shard, core * size, size, axis)


def core_order(value, axis):
    size = value.shape[axis] // 2
    core = lax.rem(lax.axis_index("dp"), 2)
    low = lax.slice_in_dim(value, 0, size, axis=axis)
    high = lax.slice_in_dim(value, size, 2 * size, axis=axis)
    return jnp.where(
        core == 0, value, jnp.concatenate((high, low), axis=axis)
    )


def sum_all(value):
    count = lax.axis_size("dp")
    if count & (count - 1):
        return lax.psum(value, ("dp", "mp"))
    bit = 1
    while bit < count:
        value = value + lax.ppermute(value, "dp", [(i, i ^ bit) for i in range(count)])
        bit *= 2
    return value + swap(value)


def per_device_pair(
    tokens,
    cotangent,
    lengths,
    first_norm_gain,
    first_norm_bias,
    query_key_value_weight,
    attention_output_weight,
    attention_output_bias,
    second_norm_gain,
    second_norm_bias,
    feedforward_up_weight,
    feedforward_up_bias,
    feedforward_down_weight,
    feedforward_down_bias,
    adapter_down_factor,
    adapter_up_factor,
    down_first_moment,
    up_first_moment,
    down_second_moment,
    up_second_moment,
):
    return pair_step(tokens, cotangent, lengths, first_norm_gain, first_norm_bias, query_key_value_weight, attention_output_weight, attention_output_bias, second_norm_gain, second_norm_bias, feedforward_up_weight, feedforward_up_bias, feedforward_down_weight, feedforward_down_bias, adapter_down_factor, adapter_up_factor, down_first_moment, up_first_moment, down_second_moment, up_second_moment)


def pair_step(
    tokens,
    cotangent,
    lengths,
    first_norm_gain,
    first_norm_bias,
    query_key_value_weight,
    attention_output_weight,
    attention_output_bias,
    second_norm_gain,
    second_norm_bias,
    feedforward_up_weight,
    feedforward_up_bias,
    feedforward_down_weight,
    feedforward_down_bias,
    adapter_down_factor,
    adapter_up_factor,
    down_first_moment,
    up_first_moment,
    down_second_moment,
    up_second_moment,
):
    f32, bf16 = jnp.float32, jnp.bfloat16
    seqs, length, width = tokens.shape
    rank = adapter_down_factor.shape[2]
    me = lax.axis_index("mp")
    columns = query_key_value_weight.shape[2]
    whole, half = 2, length // 2
    tiles, half_tiles = length // MID_ROWS, half // MID_ROWS

    def row(vector):
        return vector.reshape(1, -1)

    qkv_near = swap(core_half(query_key_value_weight, 2))
    up_bias = jnp.concatenate(
        (feedforward_up_bias, core_order(swap(feedforward_up_bias), 0))
    ).reshape(-1, 1, CHUNK)

    down_low = adapter_down_factor.astype(bf16).transpose(0, 2, 1).reshape(2 * rank, width)
    up_low = adapter_up_factor.astype(bf16)
    blank = jnp.zeros_like(up_low[0])
    up_low = jnp.stack(
        (jnp.concatenate((up_low[0], blank)), jnp.concatenate((blank, up_low[1])))
    )
    up_own = lax.dynamic_slice_in_dim(up_low, me * columns, columns, 2)
    up_other = core_order(
        lax.dynamic_slice_in_dim(up_low, (1 - me) * columns, columns, 2), 2
    )
    up_both = jnp.concatenate((up_own, up_other), axis=2)

    places = jnp.arange(seqs, dtype=jnp.int32)
    longer = (lengths[None, :] > lengths[:, None]) | (
        (lengths[None, :] == lengths[:, None]) & (places[None, :] < places[:, None])
    )
    standing = jnp.sum(longer.astype(jnp.int32), axis=1)
    order = jnp.sum(jnp.where(standing[None, :] == places[:, None], places[None, :], 0), axis=1)
    split = order[0]

    mine = jnp.stack((jnp.where(me == 0, order[1], order[2]), jnp.where(me == 0, order[4], order[3])))
    theirs = jnp.stack(
        (jnp.where(me == 0, order[2], order[1]), jnp.where(me == 0, order[3], order[4]))
    )

    def lens_of(index):
        return jnp.sum(jnp.where(places[None, :] == index[:, None], lengths[None, :], 0), axis=1)

    own_lens = lens_of(mine)
    split_lens = lens_of(split[None])
    three_lens = jnp.concatenate((own_lens, split_lens))
    flat_tokens = tokens.reshape(-1, width)
    flat_cotangent = cotangent.reshape(-1, width)
    step = jnp.arange(whole * tiles, dtype=jnp.int32)
    extra = jnp.arange(half_tiles, dtype=jnp.int32) + me * half_tiles
    whole_table = mine[step // tiles] * tiles + step % tiles
    token_table = jnp.concatenate((whole_table, split * tiles + extra))
    own_table = jnp.concatenate((step, whole * tiles + extra))
    live_table = jnp.concatenate(
        (
            own_lens[step // tiles] - (step % tiles) * MID_ROWS,
            split_lens[0] - extra * MID_ROWS,
        )
    )
    three_table = jnp.concatenate(
        (whole_table, split * tiles + jnp.arange(tiles, dtype=jnp.int32))
    )
    gain_one, shift_one = row(first_norm_gain), row(first_norm_bias)

    def sequences(pieces):
        return [piece.reshape(-1, length, columns) for piece in pieces]

    *own_heads, low = project(
        three_table,
        flat_tokens,
        gain_one,
        shift_one,
        down_low,
        up_own,
        query_key_value_weight,
    )
    own_heads = sequences(own_heads)
    qkv_near = after(qkv_near, own_heads[0])
    qkv_far = core_swap(qkv_near)
    out_near = swap(after(core_half(attention_output_weight, 0), qkv_near))
    up_near = swap(after(core_half(feedforward_up_weight, 1), qkv_near))
    attended_own, lse_own = attention_forward(three_lens, *own_heads)
    sent = lax.dynamic_slice_in_dim(attended_own[whole], (1 - me) * half, half, 0)
    attended_got = swap(core_order(sent, 1))
    qkv_far = after(qkv_far, attended_own)
    down_near = swap(after(core_half(feedforward_down_weight, 0), qkv_far))
    qkv = (query_key_value_weight, qkv_near, qkv_far)
    *far_heads, _ = project(
        whole_table,
        flat_tokens,
        gain_one,
        shift_one,
        down_low,
        up_other,
        qkv_near,
        qkv_far,
    )
    far_heads = sequences(far_heads)
    out_far = core_swap(after(out_near, far_heads[0]))
    up_far = core_swap(after(up_near, far_heads[0]))
    attended_far, lse_far = attention_forward(own_lens, *far_heads)
    down_far = core_swap(after(down_near, attended_far))
    far_all = jnp.concatenate((attended_far.reshape(-1, columns), attended_got), axis=0)
    weights = (
        attention_output_weight,
        out_near,
        out_far,
        feedforward_up_weight,
        up_near,
        up_far,
        feedforward_down_weight,
        down_near,
        down_far,
    )
    middle_table = jnp.stack(
        (token_table, own_table, live_table, jnp.arange(token_table.shape[0], dtype=jnp.int32))
    )

    def run_middle(first, last, into):
        return middle(
            middle_table[:, first:last],
            flat_tokens,
            flat_cotangent,
            attended_own.reshape(-1, columns),
            far_all,
            row(attention_output_bias),
            row(second_norm_gain),
            row(second_norm_bias),
            up_bias,
            row(feedforward_down_bias),
            weights,
            into,
        )

    block_zero, block_out, resid_zero, *grads_zero = run_middle(0, tiles, None)
    block_zero_got = swap(block_zero)
    block_rest, block_out, resid_rest, *grads_rest = run_middle(
        tiles, token_table.shape[0], block_out
    )
    grad_got = swap(core_order(grads_rest[1][length:], 1))
    block_rest_got = swap(block_rest)
    grad_kept = grads_rest[0][length:]
    grad_split = jnp.concatenate(
        (jnp.where(me == 0, grad_kept, grad_got), jnp.where(me == 0, grad_got, grad_kept))
    )

    def flat(pieces):
        return [piece.reshape(-1, columns) for piece in pieces]

    def back_whole(index, grads):
        lens = own_lens[index : index + 1]
        own = attention_backward(lens, *own_heads, grads[0], attended_own, lse_own, index)
        far = attention_backward(lens, *far_heads, grads[1], attended_far, lse_far, index)
        return flat(own), flat(far)

    span = jnp.arange(tiles, dtype=jnp.int32)

    def back_first(own, far, table, resid_grad, into):
        return first_backward(
            table,
            flat_tokens,
            resid_grad,
            low,
            own,
            far,
            gain_one,
            shift_one,
            down_low,
            up_both,
            qkv,
            into,
        )

    def whole_rows(index):
        at = index * tiles + span
        return jnp.stack((token_table[at], span, at, span, live_table[at]))

    back_zero = back_whole(0, grads_zero)
    split_own = attention_backward(split_lens, *own_heads, grad_split, attended_own, lse_own, whole)
    split_sent = jnp.stack(
        [lax.dynamic_slice_in_dim(p[0], (1 - me) * half, half, 0) for p in split_own]
    )
    split_got = swap(core_order(split_sent, 2))
    first_zero = back_first(*back_zero, whole_rows(0), resid_zero, None)
    send_zero = swap(first_zero[0])
    back_one = back_whole(1, grads_rest)
    first_split = back_first(
        flat(split_own),
        [split_got[i] for i in range(3)],
        jnp.stack(
            (
                split * tiles + extra,
                tiles + extra - me * half_tiles,
                whole * tiles + extra,
                extra,
                split_lens[0] - extra * MID_ROWS,
            )
        ),
        resid_rest,
        first_zero[1],
    )
    send_split = swap(first_split[0])
    first_one = back_first(*back_one, whole_rows(1), resid_rest, first_split[1])
    send_one = swap(first_one[0])

    down_sum, query_sum, value_sum = (
        first_zero[i] + first_split[i] + first_one[i] for i in range(2, 5)
    )
    up_sum = 8.0 * jnp.concatenate((query_sum[:rank], value_sum[rank:]))
    up_mine = up_sum[:, :columns]
    up_theirs = core_order(up_sum[:, columns:], 1)
    up_sum = jnp.concatenate(
        (jnp.where(me == 0, up_mine, up_theirs), jnp.where(me == 0, up_theirs, up_mine)), axis=1
    )
    live_row = jnp.full((8, width), jnp.sum(lengths).astype(f32))
    total = sum_all(jnp.concatenate((down_sum, up_sum, live_row)))
    active = total[-1, 0] / 2
    grad_down = total[: 2 * rank].reshape(2, rank, width).transpose(0, 2, 1) / active
    grad_up = total[2 * rank : 4 * rank].reshape(2, rank, width) / active

    there = split * length + half * (1 - me)

    def fill(out, pieces):
        for piece, start in pieces:
            out = lax.dynamic_update_slice_in_dim(out, piece, start, 0)
        return out.reshape(tokens.shape)

    block_out = fill(
        block_out,
        (
            (block_zero_got, theirs[0] * length),
            (block_rest_got[:length], theirs[1] * length),
            (block_rest_got[length:], there),
        ),
    )
    input_grad = fill(
        first_one[1],
        (
            (send_zero, theirs[0] * length),
            (send_split, there),
            (send_one, theirs[1] * length),
        ),
    )
    new_down = adam_decay_update(
        adapter_down_factor, grad_down, down_first_moment, down_second_moment
    )
    new_up = adam_decay_update(adapter_up_factor, grad_up, up_first_moment, up_second_moment)
    return (
        block_out,
        input_grad,
        new_down[0],
        new_up[0],
        new_down[1],
        new_up[1],
        new_down[2],
        new_up[2],
    )


def solution(mesh):
    in_specs = (
        P("dp", None, None),
        P("dp", None, None),
        P("dp"),
        P(),
        P(),
        P(None, None, "mp"),
        P("mp", None),
        P(),
        P(),
        P(),
        P(None, "mp"),
        P("mp"),
        P("mp", None),
        P(),
        P(),
        P(),
        P(),
        P(),
        P(),
        P(),
    )
    out_specs = (P("dp", None, None), P("dp", None, None), P(), P(), P(), P(), P(), P())
    return jax.shard_map(
        per_device_pair if mesh.shape["mp"] == 2 else per_device,
        mesh=mesh,
        in_specs=in_specs,
        out_specs=out_specs,
        check_vma=False,
    )
```
